32 devices in a mesh: fsdp: 16 (over z, x, core), grp: 2 (over y).
Axes of the slice: x: 2, y: 2, z: 4, core: 2. Of those that a mesh axis runs over, the one named last changes fastest.
Arguments:
- block_in: bfloat16 [32, 680, 1024], P(('fsdp', 'grp')), may hold values from -6 to 6
- cotangent: bfloat16 [32, 680, 1024], P(('fsdp', 'grp')), may hold values from -6 to 6
- stop_scale: int32 [32], P(('fsdp', 'grp')), may hold values from 6 to 10
- class_label: int32 [32], P(('fsdp', 'grp')), may hold values from 0 to 999
- w_qkv: float32 [1024, 3072], P(('fsdp', 'grp')), may hold values from -0.1875 to 0.1875
- w_proj: float32 [1024, 1024], P(('fsdp', 'grp')), may hold values from -0.75 to 0.75
- w_fc1: float32 [1024, 4096], P(('fsdp', 'grp')), may hold values from -0.1875 to 0.1875
- w_fc2: float32 [4096, 1024], P(('fsdp', 'grp')), may hold values from -0.09375 to 0.09375
- w_ada: float32 [1024, 6144], P(('fsdp', 'grp')), may hold values from -0.1875 to 0.1875
- w_table: float32 [1000, 1024], P(None, ('fsdp', 'grp')), may hold values from -6 to 6
- m_qkv: float32 [1024, 3072], P(('fsdp', 'grp')), may hold values from -320 to 320
- m_proj: float32 [1024, 1024], P(('fsdp', 'grp')), may hold values from -96 to 96
- m_fc1: float32 [1024, 4096], P(('fsdp', 'grp')), may hold values from -256 to 256
- m_fc2: float32 [4096, 1024], P(('fsdp', 'grp')), may hold values from -256 to 256
- m_ada: float32 [1024, 6144], P(('fsdp', 'grp')), may hold values from -384 to 384
- m_table: float32 [1000, 1024], P(None, ('fsdp', 'grp')), may hold values from -80 to 80
- v_qkv: float32 [1024, 3072], P(('fsdp', 'grp')), may hold values from 2720 to 10880
- v_proj: float32 [1024, 1024], P(('fsdp', 'grp')), may hold values from 244.8 to 979.2
- v_fc1: float32 [1024, 4096], P(('fsdp', 'grp')), may hold values from 1740.8 to 6963.2
- v_fc2: float32 [4096, 1024], P(('fsdp', 'grp')), may hold values from 1740.8 to 6963.2
- v_ada: float32 [1024, 6144], P(('fsdp', 'grp')), may hold values from 3916.8 to 15667.2
- v_table: float32 [1000, 1024], P(None, ('fsdp', 'grp')), may hold values from 170 to 680
Outputs:
- block_out: bfloat16 [32, 680, 1024], P(('fsdp', 'grp'))
- grad_in: float32 [32, 680, 1024], P(('fsdp', 'grp'))
- new_qkv: float32 [1024, 3072], P(('fsdp', 'grp'))
- new_proj: float32 [1024, 1024], P(('fsdp', 'grp'))
- new_fc1: float32 [1024, 4096], P(('fsdp', 'grp'))
- new_fc2: float32 [4096, 1024], P(('fsdp', 'grp'))
- new_ada: float32 [1024, 6144], P(('fsdp', 'grp'))
- new_table: float32 [1000, 1024], P(None, ('fsdp', 'grp'))
- half_qkv: bfloat16 [1024, 3072], P(('fsdp', 'grp'))
- half_proj: bfloat16 [1024, 1024], P(('fsdp', 'grp'))
- half_fc1: bfloat16 [1024, 4096], P(('fsdp', 'grp'))
- half_fc2: bfloat16 [4096, 1024], P(('fsdp', 'grp'))
- half_ada: bfloat16 [1024, 6144], P(('fsdp', 'grp'))
- half_table: bfloat16 [1000, 1024], P(None, ('fsdp', 'grp'))
- first_qkv: float32 [1024, 3072], P(('fsdp', 'grp'))
- first_proj: float32 [1024, 1024], P(('fsdp', 'grp'))
- first_fc1: float32 [1024, 4096], P(('fsdp', 'grp'))
- first_fc2: float32 [4096, 1024], P(('fsdp', 'grp'))
- first_ada: float32 [1024, 6144], P(('fsdp', 'grp'))
- first_table: float32 [1000, 1024], P(None, ('fsdp', 'grp'))
- second_qkv: float32 [1024, 3072], P(('fsdp', 'grp'))
- second_proj: float32 [1024, 1024], P(('fsdp', 'grp'))
- second_fc1: float32 [1024, 4096], P(('fsdp', 'grp'))
- second_fc2: float32 [4096, 1024], P(('fsdp', 'grp'))
- second_ada: float32 [1024, 6144], P(('fsdp', 'grp'))
- second_table: float32 [1000, 1024], P(None, ('fsdp', 'grp'))
The draws below stay inside these ranges and needn't reach their ends.
Inputs may be any that keep to these rules, and one draw needn't show every extreme that they name: An item holds the tokens of its first stop_scale scales, from the start of its 680 slots; later slots are padding.
All inputs are finite; a program needn't handle non-finite values.
Results may differ from the reference program's by a relative error of at most 0.017.
The reference program's roundings to bfloat16 on the way count: a program that leaves them out, or rounds other values in their place, can miss the bound.
Values may be sent and summed in bfloat16 or wider, within the bound.
No kernel may reach another device: no remote copies, remote signals or barrier semaphores. Data moves between devices by JAX's collectives and lax.ppermute only.
A program may use at most 256 MiB of HBM per device.

```python
import math
import jax
import jax.numpy as jnp
import numpy as np
from jax import lax

D = 1024
HEADS = 16
HEAD = 64
FF = 4096
CLASSES = 1000
SCALES = 10
SLOT = 680
STEP = 3
ITEMS = 32


def with_ends(result, key, least, largest):
    longest = result.shape.index(max(result.shape))
    spots = []
    for shift in (0, 1):
        where = [jax.random.randint(jax.random.fold_in(key, axis), (), 0, length) for axis, length in enumerate(result.shape)]
        where[longest] = (where[longest] + shift) % result.shape[longest]
        spots.append(tuple(where))
    return result.at[spots[0]].set(least).at[spots[1]].set(largest)


def shard_levels(stream_key, extent, pieces, smallest, top_value):
    level, own = 1.0, jax.random.fold_in(stream_key, 6)
    for dim, shards_of in pieces:
        steps = jnp.exp(jax.random.uniform(jax.random.fold_in(own, dim), (shards_of,), jnp.float32, smallest / len(pieces), top_value / len(pieces)))
        level = level * jnp.repeat(steps, extent[dim] // shards_of).reshape([-1 if axis == dim else 1 for axis in range(len(extent))])
    return level


def gaussian(rng, dims, scale, reach, cuts=(), kind=jnp.bfloat16):
    factor_of = shard_levels(rng, dims, cuts, -0.22, 0.18) if cuts else 1.0
    drawn = jax.random.normal(rng, dims, jnp.float32) * scale * factor_of
    return jnp.minimum(jnp.maximum(drawn, -reach), reach).astype(kind)


def setup_inputs(seed: int = 0) -> dict:
    keys = jax.random.split(jax.random.key(seed), 23)
    block_in = gaussian(keys[0], (ITEMS, SLOT, D), 1.0, 6.0, ((0, 32),))
    cotangent = gaussian(keys[1], (ITEMS, SLOT, D), 1.0, 6.0, ((0, 32),))
    stop_scale = with_ends(jax.random.randint(keys[2], (ITEMS,), max(SCALES - 4, 2), SCALES + 1), jax.random.fold_in(keys[2], 1), max(SCALES - 4, 2), SCALES).astype(jnp.int32)
    class_label = with_ends(jax.random.randint(keys[3], (ITEMS,), 0, CLASSES), jax.random.fold_in(keys[3], 1), 0, CLASSES - 1).astype(jnp.int32)
    w_qkv = gaussian(keys[4], (D, 3 * D), D ** -0.5, 0.1875, ((0, 32),), jnp.float32)
    w_proj = gaussian(keys[5], (D, D), (D // 16) ** -0.5, 0.75, ((0, 32),), jnp.float32)
    w_fc1 = gaussian(keys[6], (D, FF), D ** -0.5, 0.1875, ((0, 32),), jnp.float32)
    w_fc2 = gaussian(keys[7], (FF, D), FF ** -0.5, 0.09375, ((0, 32),), jnp.float32)
    w_ada = gaussian(keys[8], (D, 6 * D), D ** -0.5, 0.1875, ((0, 32),), jnp.float32)
    w_table = gaussian(keys[9], (CLASSES, D), 1.0, 6.0, ((1, 32),), jnp.float32)
    m_qkv = gaussian(keys[10], (D, 3 * D), (0.5 * (ITEMS * SLOT // 2) ** 0.5), 320.0, ((0, 32),), jnp.float32)
    m_proj = gaussian(keys[11], (D, D), (0.15 * (ITEMS * SLOT // 2) ** 0.5), 96.0, ((0, 32),), jnp.float32)
    m_fc1 = gaussian(keys[12], (D, FF), (0.4 * (ITEMS * SLOT // 2) ** 0.5), 256.0, ((0, 32),), jnp.float32)
    m_fc2 = gaussian(keys[13], (FF, D), (0.4 * (ITEMS * SLOT // 2) ** 0.5), 256.0, ((0, 32),), jnp.float32)
    m_ada = gaussian(keys[14], (D, 6 * D), (0.6 * (ITEMS * SLOT // 2) ** 0.5), 384.0, ((0, 32),), jnp.float32)
    m_table = gaussian(keys[15], (CLASSES, D), (0.5 * SLOT ** 0.5), 80.0, ((1, 32),), jnp.float32)
    v_qkv = jnp.clip(jnp.exp(math.log(10880.0) - 1.3862944 * jax.random.uniform(keys[16], (D, 3 * D), jnp.float32) ** shard_levels(keys[16], (D, 3 * D), ((0, 32),), -0.2, 0.2)), 2720.0, 10880.0)
    v_proj = jnp.clip(jnp.exp(math.log(979.2) - 1.3862944 * jax.random.uniform(keys[17], (D, D), jnp.float32) ** shard_levels(keys[17], (D, D), ((0, 32),), -0.2, 0.2)), 244.8, 979.2)
    v_fc1 = jnp.clip(jnp.exp(math.log(6963.2) - 1.3862944 * jax.random.uniform(keys[18], (D, FF), jnp.float32) ** shard_levels(keys[18], (D, FF), ((0, 32),), -0.2, 0.2)), 1740.8, 6963.2)
    v_fc2 = jnp.clip(jnp.exp(math.log(6963.2) - 1.3862944 * jax.random.uniform(keys[19], (FF, D), jnp.float32) ** shard_levels(keys[19], (FF, D), ((0, 32),), -0.2, 0.2)), 1740.8, 6963.2)
    v_ada = jnp.clip(jnp.exp(math.log(15667.2) - 1.3862944 * jax.random.uniform(keys[20], (D, 6 * D), jnp.float32) ** shard_levels(keys[20], (D, 6 * D), ((0, 32),), -0.2, 0.2)), 3916.8, 15667.2)
    v_table = jnp.clip(jnp.exp(math.log(680.0) - 1.3862944 * jax.random.uniform(keys[21], (CLASSES, D), jnp.float32) ** shard_levels(keys[21], (CLASSES, D), ((1, 32),), -0.2, 0.2)), 170.0, 680.0)
    return {"block_in": block_in, "cotangent": cotangent, "stop_scale": stop_scale, "class_label": class_label, "w_qkv": w_qkv, "w_proj": w_proj, "w_fc1": w_fc1, "w_fc2": w_fc2, "w_ada": w_ada, "w_table": w_table, "m_qkv": m_qkv, "m_proj": m_proj, "m_fc1": m_fc1, "m_fc2": m_fc2, "m_ada": m_ada, "m_table": m_table, "v_qkv": v_qkv, "v_proj": v_proj, "v_fc1": v_fc1, "v_fc2": v_fc2, "v_ada": v_ada, "v_table": v_table}


@jax.custom_vjp
def low(v):
    return lax.optimization_barrier(v.astype(jnp.bfloat16)).astype(jnp.float32)

@jax.custom_vjp
def low_back(v):
    return v

def low_keep(v):
    return (low(v), None)

def low_pass(kept, grad):
    return (grad,)

def back_keep(v):
    return (v, None)

def back_low(kept, grad):
    return (low(grad),)
low.defvjp(low_keep, low_pass)
low_back.defvjp(back_keep, back_low)
patch_sides = (1, 2, 3, 4, 5, 6, 8, 10, 13, 16)
norm_eps = 1e-06
adam_eps = 1e-08
decay = 0.05
highest = lax.Precision.HIGHEST

def scale_layout(slots):
    squares = np.array(patch_sides[:SCALES], dtype=np.int64) ** 2
    bounds = np.cumsum(squares)
    scale_ids = np.searchsorted(bounds, np.arange(slots), side='right')
    return (bounds.astype(np.int32), scale_ids.astype(np.int32))

def norm_rows(values):
    centre = values - lax.optimization_barrier(jnp.mean(values, axis=-1, keepdims=True))
    spread = lax.optimization_barrier(jnp.mean(centre * centre, axis=-1, keepdims=True))
    return centre * lax.rsqrt(spread + norm_eps)

def modulate(values, scale_row, shift_row):
    return norm_rows(values) * (1.0 + scale_row) + shift_row

def gelu_tanh(values):
    return jax.nn.gelu(values, approximate=True)

def learn_rates():
    return (D ** (-0.5), (D // 16) ** (-0.5), D ** (-0.5), FF ** (-0.5), D ** (-0.5), 1.0)

def adamw(weight, gradient, first, second, bias_one, bias_two, rate):
    first_new = 0.5 * first + 0.5 * gradient
    second_new = 0.5 * second + 0.5 * gradient * gradient
    update = first_new / bias_one / (jnp.sqrt(second_new / bias_two) + adam_eps) + decay * weight
    weight_new = weight - rate * update
    return (weight_new, weight_new.astype(jnp.bfloat16), first_new, second_new)

def block_item(weights, tokens, ada_row, length, scale_table):
    mat_qkv, mat_proj, mat_fc1, mat_fc2 = weights
    gamma_one, scale_one, shift_one, gamma_two, scale_two, shift_two = jnp.split(ada_row, 6)
    position = jnp.arange(SLOT)
    valid = (position < length).astype(jnp.float32)
    allowed = (scale_table[None, :] <= scale_table[:, None]) & (position[None, :] < length)
    hidden = low(modulate(tokens, scale_one, shift_one))
    packed = low(low_back(jnp.dot(hidden, mat_qkv, precision=highest))).reshape(SLOT, 3, HEADS, HEAD)
    queries = packed[:, 0]
    key_rows = packed[:, 1]
    values = packed[:, 2]
    scores = low_back(jnp.einsum('qhd,khd->hqk', queries, key_rows, precision=highest) * 0.125)
    scores = jnp.where(allowed[None], scores, -1e+30)
    probs = low(jax.nn.softmax(scores, axis=-1))
    context = jnp.einsum('hqk,khd->qhd', probs, values, precision=highest).reshape(SLOT, D)
    context = low(low_back(context))
    attended = low_back(jnp.dot(context, mat_proj, precision=highest))
    middle = tokens + gamma_one * attended
    second = low(modulate(middle, scale_two, shift_two))
    inner = low_back(jnp.dot(second, mat_fc1, precision=highest))
    activated = low(gelu_tanh(inner))
    branch = low_back(jnp.dot(activated, mat_fc2, precision=highest))
    return (middle + gamma_two * branch) * valid[:, None]

def forward(params, tokens, stop_scale, class_label):
    w_qkv, w_proj, w_fc1, w_fc2, w_ada, w_table = params
    weights = (low(w_qkv), low(w_proj), low(w_fc1), low(w_fc2))
    cond = jnp.take(low(w_table), class_label, axis=0)
    lifted = low(jax.nn.silu(cond))
    ada = low_back(jnp.dot(lifted, low(w_ada), precision=highest))
    bounds, scale_ids = scale_layout(SLOT)
    picked = jnp.arange(SCALES)[None, :] == stop_scale[:, None] - 1
    lengths = lax.optimization_barrier(jnp.sum(jnp.where(picked, jnp.asarray(bounds)[None, :], 0), axis=1))
    scale_table = jnp.asarray(scale_ids)

    def one_item(inputs):
        return block_item(weights, inputs[0], inputs[1], inputs[2], scale_table)
    return lax.map(jax.checkpoint(one_item), (tokens, ada, lengths))

def reference(block_in, cotangent, stop_scale, class_label, w_qkv, w_proj, w_fc1, w_fc2, w_ada, w_table, m_qkv, m_proj, m_fc1, m_fc2, m_ada, m_table, v_qkv, v_proj, v_fc1, v_fc2, v_ada, v_table):
    tokens = block_in.astype(jnp.float32)
    params = (w_qkv, w_proj, w_fc1, w_fc2, w_ada, w_table)

    def wrapped(p_qkv, p_proj, p_fc1, p_fc2, p_ada, p_table, p_tokens):
        return forward((p_qkv, p_proj, p_fc1, p_fc2, p_ada, p_table), p_tokens, stop_scale, class_label)
    outcome, pullback = jax.vjp(wrapped, w_qkv, w_proj, w_fc1, w_fc2, w_ada, w_table, tokens)
    grads = pullback(cotangent.astype(jnp.float32))
    counter = jnp.float32(STEP)
    bias_one = 1.0 - jnp.power(jnp.float32(0.5), counter)
    bias_two = 1.0 - jnp.power(jnp.float32(0.5), counter)
    rates = learn_rates()
    firsts = (m_qkv, m_proj, m_fc1, m_fc2, m_ada, m_table)
    seconds = (v_qkv, v_proj, v_fc1, v_fc2, v_ada, v_table)
    res = [adamw(params[j], grads[j], firsts[j], seconds[j], bias_one, bias_two, rates[j]) for j in range(6)]
    return (outcome.astype(jnp.bfloat16), grads[6], res[0][0], res[1][0], res[2][0], res[3][0], res[4][0], res[5][0], res[0][1], res[1][1], res[2][1], res[3][1], res[4][1], res[5][1], res[0][2], res[1][2], res[2][2], res[3][2], res[4][2], res[5][2], res[0][3], res[1][3], res[2][3], res[3][3], res[4][3], res[5][3])
```

```python
import functools

import jax
import jax.numpy as jnp
import numpy as np
from jax import lax
from jax.experimental import pallas as pl
from jax.experimental.pallas import tpu as pltpu
from jax.sharding import PartitionSpec as P

D = 1024
HEADS = 16
HEAD = 64
FF = 4096
SCALES = 10
STEP = 3
AXES = ("fsdp", "grp")

patch_sides = (1, 2, 3, 4, 5, 6, 8, 10, 13, 16)
norm_eps = 1e-06
adam_eps = 1e-08
decay = 0.05
highest = lax.Precision.HIGHEST
bf16 = jnp.bfloat16
f32 = jnp.float32


def scale_layout(slots):
    squares = np.array(patch_sides[:SCALES], dtype=np.int64) ** 2
    bounds = np.cumsum(squares)
    scale_ids = np.searchsorted(bounds, np.arange(slots), side="right")
    return (bounds.astype(np.int32), scale_ids.astype(np.int32))


def norm_rows(values):
    centre = values - jnp.mean(values, axis=-1, keepdims=True)
    spread = jnp.mean(centre * centre, axis=-1, keepdims=True)
    return centre * lax.rsqrt(spread + norm_eps)


def modulate(values, scale_row, shift_row):
    return norm_rows(values) * (1.0 + scale_row) + shift_row


def gelu_tanh(values):
    return jax.nn.gelu(values, approximate=True)


def learn_rates():
    return (D ** (-0.5), (D // 16) ** (-0.5), D ** (-0.5), FF ** (-0.5), D ** (-0.5), 1.0)


def adamw(weight, gradient, first, second, bias_one, bias_two, rate):
    first_new = 0.5 * first + 0.5 * gradient
    second_new = 0.5 * second + 0.5 * gradient * gradient
    update = first_new / bias_one / (jnp.sqrt(second_new / bias_two) + adam_eps) + decay * weight
    weight_new = weight - rate * update
    return (weight_new, weight_new.astype(bf16), first_new, second_new)


def contract_rows(former, latter):
    return lax.dot_general(former, latter, (((0,), (0,)), ((), ())), preferred_element_type=f32)


def contract_cols(former, latter):
    return lax.dot_general(former, latter, (((1,), (1,)), ((), ())), preferred_element_type=f32)


def dot_nt(former, latter):
    return lax.dot_general(former, latter, (((1,), (1,)), ((), ())), preferred_element_type=f32)


def dot_nn(former, latter):
    return lax.dot_general(former, latter, (((1,), (0,)), ((), ())), preferred_element_type=f32)


def dot_tn(former, latter):
    return lax.dot_general(former, latter, (((0,), (0,)), ((), ())), preferred_element_type=f32)


FORWARD_TILES = ((0, 240, 256), (240, 416, 432), (416, 680, 680))
BACKWARD_TILES = ((0, 128, 160), (128, 384, 432), (384, 680, 680))


def attend_kernel(q_ref, k_ref, v_ref, bias_ref, context_ref, lse_ref):
    for begin, end, keys in FORWARD_TILES:
        q = q_ref[begin:end, :] * bf16(0.125)
        lane = lax.broadcasted_iota(jnp.int32, q.shape, 1)
        contexts, totals = [], []
        for head in range(2):
            own = jnp.where((lane < HEAD) == (head == 0), q, bf16(0))
            scores = dot_nt(own, k_ref[:keys, :]) + bias_ref[begin:end, :keys]
            largest = jnp.max(scores, axis=1, keepdims=True)
            expo = jnp.exp(scores - largest)
            total = jnp.sum(expo, axis=1, keepdims=True)
            probs = (expo * (1.0 / total)).astype(bf16)
            totals.append(largest + jnp.log(total))
            contexts.append(dot_nn(probs, v_ref[:keys, :]))
        left = lax.broadcasted_iota(jnp.int32, contexts[0].shape, 1) < HEAD
        context_ref[begin:end, :] = jnp.where(left, contexts[0], contexts[1]).astype(bf16)
        lse = jnp.where(left, totals[0], totals[1]).T
        lse_ref[0, 0:1, begin:end] = lse[0:1]
        lse_ref[0, 1:2, begin:end] = lse[HEAD : HEAD + 1]


def attend_forward(packed, bias):
    slots, width = packed.shape[0], packed.shape[1] // 3
    pairs = width // 128
    assert slots == FORWARD_TILES[-1][1]

    def block(offset):
        return pl.BlockSpec((slots, 128), lambda i: (0, offset + i))

    return pl.pallas_call(
        attend_kernel,
        grid=(pairs,),
        in_specs=[
            block(0),
            block(pairs),
            block(2 * pairs),
            pl.BlockSpec((slots, slots), lambda i: (0, 0)),
        ],
        out_specs=[block(0), pl.BlockSpec((1, 2, slots), lambda i: (i, 0, 0))],
        out_shape=[
            jax.ShapeDtypeStruct((slots, width), bf16),
            jax.ShapeDtypeStruct((pairs, 2, slots), f32),
        ],
        cost_estimate=pl.CostEstimate(
            flops=10 * slots * slots * width,
            bytes_accessed=12 * slots * width,
            transcendentals=slots * slots * HEADS,
        ),
        compiler_params=pltpu.CompilerParams(vmem_limit_bytes=48 << 20),
        name="attend",
    )(packed, packed, packed, bias)


def attend_back_kernel(
    q_ref, k_ref, v_ref, grad_ref, lse_ref, bias_ref, out_ref, keys_ref, values_ref
):
    for count, (begin, end, keys) in enumerate(reversed(BACKWARD_TILES)):
        q = q_ref[begin:end, :] * bf16(0.125)
        grad = grad_ref[begin:end, :]
        k = k_ref[:keys, :]
        v = v_ref[:keys, :]
        left = lax.broadcasted_iota(jnp.int32, q.shape, 1) < HEAD
        d_q, d_k, d_v = [], [], []
        for head in range(2):
            own = left == (head == 0)
            scores = dot_nt(k, jnp.where(own, q, bf16(0))) + bias_ref[:keys, begin:end]
            probs = jnp.exp(scores - lse_ref[0, head : head + 1, begin:end])
            d_probs = dot_nt(v, jnp.where(own, grad, bf16(0)))
            inner = jnp.sum(probs * d_probs, axis=0, keepdims=True)
            d_scores = (probs * (d_probs - inner)).astype(bf16)
            d_v.append(dot_nn(probs.astype(bf16), grad))
            d_k.append(dot_nn(d_scores, q))
            d_q.append(dot_tn(d_scores, k))
        first = lax.broadcasted_iota(jnp.int32, d_k[0].shape, 1) < HEAD
        d_k = jnp.where(first, d_k[0], d_k[1])
        d_v = jnp.where(first, d_v[0], d_v[1])
        if count == 0:
            keys_ref[:keys, :] = d_k
            values_ref[:keys, :] = d_v
        else:
            keys_ref[:keys, :] += d_k
            values_ref[:keys, :] += d_v
        out_ref[0, begin:end, :] = (jnp.where(left, d_q[0], d_q[1]) * 0.125).astype(bf16)
    out_ref[1] = keys_ref[...].astype(bf16)
    out_ref[2] = values_ref[...].astype(bf16)


def attend_backward(packed, d_context, lse, bias_t):
    slots, width = packed.shape[0], packed.shape[1] // 3
    pairs = width // 128
    assert slots == BACKWARD_TILES[-1][1]

    def block(offset):
        return pl.BlockSpec((slots, 128), lambda i: (0, offset + i))

    return pl.pallas_call(
        attend_back_kernel,
        grid=(pairs,),
        in_specs=[
            block(0),
            block(pairs),
            block(2 * pairs),
            block(0),
            pl.BlockSpec((1, 2, slots), lambda i: (i, 0, 0)),
            pl.BlockSpec((slots, slots), lambda i: (0, 0)),
        ],
        out_specs=pl.BlockSpec((3, slots, 128), lambda i: (0, 0, i)),
        out_shape=jax.ShapeDtypeStruct((3, slots, width), bf16),
        scratch_shapes=[pltpu.VMEM((slots, 128), f32), pltpu.VMEM((slots, 128), f32)],
        cost_estimate=pl.CostEstimate(
            flops=20 * slots * slots * width,
            bytes_accessed=16 * slots * width,
            transcendentals=slots * slots * HEADS,
        ),
        compiler_params=pltpu.CompilerParams(vmem_limit_bytes=56 << 20),
        name="attend_back",
    )(packed, packed, packed, d_context, lse, bias_t)


def gather_kernel(layout, place_ref, x_ref, *refs):
    depth, rows, left, half, chunk, gelu = layout
    outs = 2 if gelu else 1
    pieces, whole_ref, out_refs = refs[:8], refs[8], refs[9 : 9 + outs]
    w_ref, y_refs = refs[9 + outs], refs[10 + outs : 10 + 2 * outs]
    in_sems, whole_sems, out_sems = refs[10 + 2 * outs :]
    z, x, c, y = [place_ref[i] for i in range(4)]
    for color in range(2):
        for far in range(2):
            for core in range(2):
                piece = pieces[core * 4 + far * 2 + color]
                for near in range(2):
                    step_x, step_y = (far, near) if color == 0 else (near, far)
                    for step in range(depth):
                        at = lax.rem(z + depth - step, depth) * 2 + (x ^ step_x)
                        at = (at * 2 + (c ^ core)) * 2 + (y ^ step_y)
                        at = pl.multiple_of(at * rows, rows)
                        pltpu.make_async_copy(
                            piece.at[near, step, :, pl.ds(left, half)],
                            w_ref.at[color, pl.ds(at, rows), :],
                            in_sems.at[color],
                        ).start()
    waits = []
    for color in range(2):
        own = w_ref.at[color]
        pltpu.make_async_copy(own, own, in_sems.at[color]).wait()
        copy = pltpu.make_async_copy(
            own, whole_ref.at[:, pl.ds(color * half, half)], whole_sems.at[color]
        )
        copy.start()
        waits.append(copy)
        for begin in range(0, half, chunk):
            at = color * half + begin
            result = dot_nn(x_ref[...], w_ref[color, :, begin : begin + chunk])
            values = [result, gelu_tanh(result)] if gelu else [result]
            for i, value in enumerate(values):
                y_refs[i][:, at : at + chunk] = value.astype(y_refs[i].dtype)
                copy = pltpu.make_async_copy(
                    y_refs[i].at[:, pl.ds(at, chunk)],
                    out_refs[i].at[:, pl.ds(at, chunk)],
                    out_sems.at[i, at // chunk],
                )
                copy.start()
                waits.append(copy)
    for copy in waits:
        copy.wait()


def gather_dot(place, x, pieces, left, half, kinds, name):
    depth, rows = pieces[0].shape[1:3]
    whole, width = rows * depth * 8, 2 * half
    slots = x.shape[0]
    chunk = min(512, half)
    anywhere = pl.BlockSpec(memory_space=pl.ANY)
    return pl.pallas_call(
        functools.partial(gather_kernel, (depth, rows, left, half, chunk, len(kinds) == 2)),
        grid_spec=pltpu.PrefetchScalarGridSpec(
            num_scalar_prefetch=1,
            grid=(1,),
            in_specs=[pl.BlockSpec(x.shape, lambda i, place: (0, 0))] + [anywhere] * 8,
            out_specs=[anywhere] * (1 + len(kinds)),
            scratch_shapes=[pltpu.VMEM((2, whole, half), bf16)]
            + [pltpu.VMEM((slots, width), kind) for kind in kinds]
            + [
                pltpu.SemaphoreType.DMA((2,)),
                pltpu.SemaphoreType.DMA((2,)),
                pltpu.SemaphoreType.DMA((len(kinds), width // chunk)),
            ],
        ),
        out_shape=[jax.ShapeDtypeStruct((whole, width), bf16)]
        + [jax.ShapeDtypeStruct((slots, width), kind) for kind in kinds],
        cost_estimate=pl.CostEstimate(
            flops=3 * slots * whole * width,
            bytes_accessed=4 * whole * width + 4 * slots * width,
            transcendentals=0,
        ),
        compiler_params=pltpu.CompilerParams(vmem_limit_bytes=60 << 20),
        name=name,
    )(place, x, *pieces)


def gelu_back_kernel(half, place_ref, grad_ref, weight_ref, inner_ref, out_ref, give_ref):
    d_act = dot_nt(grad_ref[...], weight_ref[...])
    _, back = jax.vjp(gelu_tanh, inner_ref[...])
    value = back(d_act)[0].astype(bf16)
    out_ref[...] = value

    @pl.when(pl.program_id(0) < half)
    def _():
        give_ref[...] = value


def gelu_back_dot(place, grad, weight, inner):
    slots, width = inner.shape
    chunk = 512
    half = width // chunk // 2

    def at(i, place):
        return lax.rem(i + (1 - place[2]) * half, 2 * half)

    return pl.pallas_call(
        functools.partial(gelu_back_kernel, half),
        grid_spec=pltpu.PrefetchScalarGridSpec(
            num_scalar_prefetch=1,
            grid=(2 * half,),
            in_specs=[
                pl.BlockSpec(grad.shape, lambda i, place: (0, 0)),
                pl.BlockSpec((chunk, weight.shape[1]), lambda i, place: (at(i, place), 0)),
                pl.BlockSpec((slots, chunk), lambda i, place: (0, at(i, place))),
            ],
            out_specs=[
                pl.BlockSpec((slots, chunk), lambda i, place: (0, at(i, place))),
                pl.BlockSpec((slots, chunk), lambda i, place: (0, jnp.minimum(i, half - 1))),
            ],
        ),
        out_shape=[
            jax.ShapeDtypeStruct((slots, width), bf16),
            jax.ShapeDtypeStruct((slots, width // 2), bf16),
        ],
        cost_estimate=pl.CostEstimate(
            flops=3 * slots * width * weight.shape[1],
            bytes_accessed=8 * slots * width + 2 * width * weight.shape[1],
            transcendentals=slots * width,
        ),
        compiler_params=pltpu.CompilerParams(vmem_limit_bytes=48 << 20),
        name="gelu_back",
    )(place, grad, weight, inner)


def weight_grad_kernel(
    depth, rows, chunks, place_ref, own_ref, other_ref, mine_ref, take_ref, *out_refs
):
    step = pl.program_id(0)
    total = dot_tn(own_ref[...], mine_ref[0]) + dot_tn(other_ref[...], take_ref[0])
    total = total.reshape(depth, 2, 2, 2, rows, total.shape[-1])

    @pl.when(step < chunks // 2)
    def _():
        low, high = total[:, :, :, 0], total[:, :, :, 1]
        first = place_ref[3] == 0
        out_refs[0][...] = jnp.where(first, high, low).astype(bf16)
        out_refs[1][...] = jnp.where(first, low, high).astype(bf16)

    @pl.when(step >= chunks // 2)
    def _():
        low, high = total[:, 0], total[:, 1]
        first = place_ref[1] == 0
        out_refs[2][...] = jnp.where(first, high, low).astype(bf16)
        out_refs[3][...] = jnp.where(first, low, high).astype(bf16)


def weight_grad_call(place, own, other, rhs, take, rows):
    groups, slots, columns = rhs.shape
    half, width = columns // 2, own.shape[1]
    depth = width // rows // 8
    chunk = 512 if half % 1024 == 0 else 256
    per = half // chunk
    chunks = groups * per
    assert chunks % 2 == 0
    turn = chunks // 2
    all_rows = pl.BlockSpec(own.shape, lambda i, place: (0, 0))
    block = (depth, 2, 2, rows, chunk)
    early = pl.BlockSpec(block, lambda i, place: (0, 0, 0, 0, jnp.minimum(i, turn - 1)))
    late = pl.BlockSpec(block, lambda i, place: (0, 0, 0, 0, jnp.maximum(i - turn, 0)))
    shape = jax.ShapeDtypeStruct((depth, 2, 2, rows, groups * half // 2), bf16)
    return pl.pallas_call(
        functools.partial(weight_grad_kernel, depth, rows, chunks),
        grid_spec=pltpu.PrefetchScalarGridSpec(
            num_scalar_prefetch=1,
            grid=(chunks,),
            in_specs=[
                all_rows,
                all_rows,
                pl.BlockSpec(
                    (1, slots, chunk), lambda i, place: (i // per, 0, place[2] * per + i % per)
                ),
                pl.BlockSpec((1, slots, chunk), lambda i, place: (i // per, 0, i % per)),
            ],
            out_specs=[early, early, late, late],
        ),
        out_shape=[shape] * 4,
        cost_estimate=pl.CostEstimate(
            flops=6 * slots * width * groups * half,
            bytes_accessed=4 * slots * (width + groups * half) + 2 * width * groups * half,
            transcendentals=0,
        ),
        compiler_params=pltpu.CompilerParams(vmem_limit_bytes=60 << 20),
        name="weight_grad",
    )(place, own, other, rhs, take)


class Grid:
    def __init__(self, fsdp, grp):
        outer = fsdp // 2
        self.size = {"c": 2, "x": 2 if outer % 2 == 0 else 1, "y": grp}
        self.size["z"] = outer // self.size["x"]
        self.count = fsdp * grp
        self.fsdp = fsdp

    def here(self):
        place = lax.axis_index("fsdp")
        wide = self.size["x"]
        return {
            "c": place % 2,
            "x": (place // 2) % wide,
            "z": place // (2 * wide),
            "y": lax.axis_index("grp"),
        }

    def shift(self, array, axis, step):
        size = self.size[axis]
        if axis == "y":
            return lax.ppermute(array, "grp", [(i, (i + step) % size) for i in range(size)])
        stride = {"c": 1, "x": 2, "z": 2 * self.size["x"]}[axis]
        pairs = []
        for i in range(self.fsdp):
            at = (i // stride) % size
            pairs.append((i, i + ((at + step) % size - at) * stride))
        return lax.ppermute(array, "fsdp", pairs)

    def fits(self, rows):
        return self.size["x"] == 2 and self.size["y"] == 2 and rows % 32 == 0

    def gather_line(self, shards):
        lows = [shard[:, : shard.shape[1] // 2] for shard in shards]
        highs = [shard[:, shard.shape[1] // 2 :] for shard in shards]
        shard = jnp.concatenate(lows + highs, axis=1)
        half = shard.shape[1] // 2
        steps = [shard] + [self.shift(shard, "z", step) for step in range(1, self.size["z"])]
        return [jnp.stack([p[:, i * half : (i + 1) * half] for p in steps]) for i in range(2)]

    def gather_plane(self, line):
        orders = ("yx", "xy")
        plane = [
            jnp.stack([own, self.shift(own, order[0], 1)]) for own, order in zip(line, orders)
        ]
        far = [self.shift(own, order[1], 1) for own, order in zip(plane, orders)]
        mine = plane + far
        return mine + [self.shift(piece, "c", 1) for piece in mine]

    def scatter_sum(self, array, axis, dim, here, kind=bf16):
        size = self.size[axis]
        total = lax.dynamic_index_in_dim(array, here[axis], dim, keepdims=False)
        for step in range(1, size):
            piece = lax.dynamic_index_in_dim(array, (here[axis] + step) % size, dim, keepdims=False)
            total = total + self.shift(piece.astype(kind), axis, step).astype(f32)
        return total


def per_device(
    grid,
    block_in,
    cotangent,
    stop_scale,
    class_label,
    w_qkv,
    w_proj,
    w_fc1,
    w_fc2,
    w_ada,
    w_table,
    m_qkv,
    m_proj,
    m_fc1,
    m_fc2,
    m_ada,
    m_table,
    v_qkv,
    v_proj,
    v_fc1,
    v_fc2,
    v_ada,
    v_table,
):
    items, slots, width = block_in.shape
    assert items == 1
    here = grid.here()
    bounds, scale_ids = scale_layout(slots)
    picked = jnp.arange(SCALES) == stop_scale[0] - 1
    length = jnp.sum(jnp.where(picked, jnp.asarray(bounds), 0))
    position = jnp.arange(slots)
    valid = (position < length).astype(f32)[:, None]
    scale_table = jnp.asarray(scale_ids)
    allowed = (scale_table[None, :] <= scale_table[:, None]) & (position[None, :] < length)
    bias = jnp.where(allowed, f32(0), f32(-1e30))
    bias_t = bias.T
    place = jnp.stack([here[axis] for axis in "zxcy"]).astype(jnp.int32)
    fits = grid.fits(w_qkv.shape[0])
    cast_qkv, cast_proj, cast_fc1, cast_fc2 = [
        w.astype(bf16) for w in (w_qkv, w_proj, w_fc1, w_fc2)
    ]
    half_qkv, half_proj, half_fc1 = [w.shape[1] // 2 for w in (w_qkv, w_proj, w_fc1)]
    labels = lax.all_to_all(
        jnp.broadcast_to(class_label, (grid.count,)), AXES, 0, 0, tiled=True
    )
    cast_ada = w_ada.astype(bf16)
    cast_table = w_table.astype(bf16)
    onehot = (labels[:, None] == jnp.arange(cast_table.shape[0])[None, :]).astype(bf16)
    cond = jnp.dot(onehot, cast_table, preferred_element_type=f32)
    silu_out, silu_back = jax.vjp(jax.nn.silu, cond)
    lifted_low = silu_out.astype(bf16)

    def ada_part(begin, end):
        return jnp.dot(lifted_low, cast_ada[:, begin:end], preferred_element_type=f32)

    def ada_sum(part):
        mine = lax.all_to_all(part, AXES, 0, 0, tiled=True)
        return jnp.sum(mine, axis=0, keepdims=True)

    early = ada_part(width, 3 * width)
    late = jnp.concatenate([ada_part(0, width), ada_part(3 * width, 6 * width)], axis=1)
    if fits:
        line_qkv = grid.gather_line([cast_qkv])
        line_qkv, cast_proj, cast_fc1, early = lax.optimization_barrier(
            (line_qkv, cast_proj, cast_fc1, early)
        )
        line_rest = grid.gather_line([cast_proj, cast_fc1])
        pieces_qkv = grid.gather_plane(line_qkv)
    early = ada_sum(early)
    if fits:
        line_rest, cast_fc2, early, late, _ = lax.optimization_barrier(
            (line_rest, cast_fc2, early, late, pieces_qkv[2:4])
        )
        pieces_rest = grid.gather_plane(line_rest)
        line_fc2 = grid.gather_line([cast_fc2])
        line_fc2, _ = lax.optimization_barrier((line_fc2, pieces_rest[2:4]))
        pieces_fc2 = grid.gather_plane(line_fc2)
    late = ada_sum(late)
    scale_one, shift_one = early[:, :width], early[:, width:]
    gamma_one, gamma_two, scale_two, shift_two = [
        late[:, i * width : (i + 1) * width] for i in range(4)
    ]

    def weight_grad(lhs, rhs, other_lhs, give=None):
        groups, _, columns = rhs.shape
        half = columns // 2
        size = grid.size
        rows = lhs.shape[1] // grid.count
        if give is None:
            give = lax.dynamic_slice_in_dim(rhs, (1 - here["c"]) * half, half, 2)
        take = grid.shift(give, "c", 1)
        if grid.fits(rows):
            away_one, one, away_two, two = weight_grad_call(place, lhs, other_lhs, rhs, take, rows)
            first = away_one
            one = one.astype(f32) + grid.shift(away_one, "y", 1).astype(f32)
            two = two.astype(f32) + grid.shift(away_two, "x", 1).astype(f32)
        else:
            mine = lax.dynamic_slice_in_dim(rhs, here["c"] * half, half, 2)
            both = jnp.concatenate([mine, take], axis=1)
            both = jnp.concatenate([both[i] for i in range(groups)], axis=1)
            grad = contract_rows(jnp.concatenate([lhs, other_lhs], axis=0), both)
            first = grad
            grad = grad.reshape(size["z"], size["x"], 2, size["y"], rows, groups * half)
            middle = groups * half // 2
            one = grid.scatter_sum(grad[..., :middle], "y", 3, here)
            two = grid.scatter_sum(grad[..., middle:], "x", 1, here)
        one = grid.scatter_sum(one, "x", 1, here)
        two = grid.scatter_sum(two, "y", 2, here)
        both = grid.scatter_sum(jnp.concatenate([one, two], axis=-1), "z", 0, here)
        keep = lax.dynamic_index_in_dim(both, here["c"], 0, keepdims=False)
        give = lax.dynamic_index_in_dim(both, 1 - here["c"], 0, keepdims=False)
        take = grid.shift(give, "c", 1)
        low = jnp.where(here["c"] == 0, keep, take).reshape(rows, groups, 1, half)
        high = jnp.where(here["c"] == 0, take, keep).reshape(rows, groups, 1, half)
        return jnp.concatenate([low, high], axis=2).reshape(rows, groups * columns), first

    tokens = block_in[0].astype(f32)
    hidden, modulate_one = jax.vjp(modulate, tokens, scale_one, shift_one)
    hidden_low = hidden.astype(bf16)
    hidden_other = grid.shift(hidden_low, "c", 1)
    if fits:
        wide_qkv, packed = gather_dot(
            place, hidden_low, pieces_qkv, 0, half_qkv, [bf16], "gather_qkv"
        )
    else:
        wide_qkv = lax.all_gather(cast_qkv, AXES, axis=0, tiled=True)
        packed = jnp.dot(hidden_low, wide_qkv, preferred_element_type=f32).astype(bf16)
    context, lse = attend_forward(packed, bias)
    context_other = grid.shift(context, "c", 1)
    if fits:
        wide_proj, attended = gather_dot(
            place, context, pieces_rest, 0, half_proj, [f32], "gather_proj"
        )
    else:
        wide_proj = lax.all_gather(cast_proj, AXES, axis=0, tiled=True)
        attended = jnp.dot(context, wide_proj, preferred_element_type=f32)
    middle = tokens + gamma_one * attended
    second, modulate_two = jax.vjp(modulate, middle, scale_two, shift_two)
    second_low = second.astype(bf16)
    second_other = grid.shift(second_low, "c", 1)
    if fits:
        wide_fc1, inner, activated_low = gather_dot(
            place, second_low, pieces_rest, half_proj, half_fc1, [f32, bf16], "gather_fc1"
        )
    else:
        wide_fc1 = lax.all_gather(cast_fc1, AXES, axis=0, tiled=True)
        inner = jnp.dot(second_low, wide_fc1, preferred_element_type=f32)
        activated_low = gelu_tanh(inner).astype(bf16)
    activated_other = grid.shift(activated_low, "c", 1)
    if fits:
        wide_fc2, branch = gather_dot(
            place, activated_low, pieces_fc2, 0, width // 2, [f32], "gather_fc2"
        )
    else:
        wide_fc2 = lax.all_gather(cast_fc2, AXES, axis=0, tiled=True)
        branch = jnp.dot(activated_low, wide_fc2, preferred_element_type=f32)
    block_out = ((middle + gamma_two * branch) * valid).astype(bf16)
    upstream = cotangent[0].astype(f32) * valid
    d_gamma_two = jnp.sum(upstream * branch, axis=0, keepdims=True)
    d_branch = (upstream * gamma_two).astype(bf16)
    sum_fc2, begun = weight_grad(activated_low, d_branch[None], activated_other)
    d_branch, _ = lax.optimization_barrier((d_branch, begun))
    d_inner_low, give = gelu_back_dot(place, d_branch, wide_fc2, inner)
    d_second = contract_cols(d_inner_low, wide_fc1)
    sum_fc1, begun = weight_grad(second_low, d_inner_low[None], second_other, give[None])
    d_second, _ = lax.optimization_barrier((d_second, begun))
    d_middle_part, d_scale_two, d_shift_two = modulate_two(d_second)
    d_middle = upstream + d_middle_part
    d_gamma_one = jnp.sum(d_middle * attended, axis=0, keepdims=True)
    d_attended = (d_middle * gamma_one).astype(bf16)
    d_context = contract_cols(d_attended, wide_proj).astype(bf16)
    sum_proj, begun = weight_grad(context, d_attended[None], context_other)
    d_context, _ = lax.optimization_barrier((d_context, begun))
    d_packed = attend_backward(packed, d_context, lse, bias_t)
    sum_qkv, begun = weight_grad(hidden_low, d_packed, hidden_other)
    d_packed, _ = lax.optimization_barrier((d_packed, begun))
    d_packed = jnp.concatenate([d_packed[0], d_packed[1], d_packed[2]], axis=1)
    d_hidden = contract_cols(d_packed, wide_qkv)
    d_tokens, d_scale_one, d_shift_one = modulate_one(d_hidden)
    grad_in = d_middle + d_tokens
    d_ada = jnp.concatenate(
        [d_gamma_one, d_scale_one, d_shift_one, d_gamma_two, d_scale_two, d_shift_two], axis=1
    ).astype(bf16)
    every_ada = lax.all_to_all(
        jnp.broadcast_to(d_ada, (grid.count, 6 * width)), AXES, 0, 0, tiled=True
    )
    sum_ada = contract_rows(lifted_low, every_ada)
    (d_cond,) = silu_back(contract_cols(every_ada, cast_ada))
    sum_table = lax.dot_general(
        onehot.astype(f32), d_cond, (((0,), (0,)), ((), ())), precision=highest
    )
    counter = f32(STEP)
    bias_one = 1.0 - jnp.power(f32(0.5), counter)
    bias_two = 1.0 - jnp.power(f32(0.5), counter)
    rates = learn_rates()
    updates = [
        adamw(w, g, m, v, bias_one, bias_two, rate)
        for w, g, m, v, rate in zip(
            (w_qkv, w_proj, w_fc1, w_fc2, w_ada, w_table),
            (sum_qkv, sum_proj, sum_fc1, sum_fc2, sum_ada, sum_table),
            (m_qkv, m_proj, m_fc1, m_fc2, m_ada, m_table),
            (v_qkv, v_proj, v_fc1, v_fc2, v_ada, v_table),
            rates,
        )
    ]
    return (block_out[None], grad_in[None]) + tuple(
        update[kind] for kind in range(4) for update in updates
    )


def solution(mesh):
    grid = Grid(mesh.shape["fsdp"], mesh.shape["grp"])
    items = P(AXES, None, None)
    vector = P(AXES)
    rows = P(AXES, None)
    columns = P(None, AXES)
    weights = (rows, rows, rows, rows, rows, columns)

    def run(*arrays):
        return per_device(grid, *arrays)

    return jax.shard_map(
        run,
        mesh=mesh,
        in_specs=(items, items, vector, vector) + weights * 3,
        out_specs=(items, items) + weights * 4,
        check_vma=False,
    )
```

```python
import functools

import jax
import jax.numpy as jnp
import numpy as np
from jax import lax
from jax.experimental import pallas as pl
from jax.experimental.pallas import tpu as pltpu
from jax.sharding import PartitionSpec as P

D = 1024
HEADS = 16
HEAD = 64
FF = 4096
SCALES = 10
STEP = 3
AXES = ("fsdp", "grp")

patch_sides = (1, 2, 3, 4, 5, 6, 8, 10, 13, 16)
norm_eps = 1e-06
adam_eps = 1e-08
decay = 0.05
highest = lax.Precision.HIGHEST
bf16 = jnp.bfloat16
f32 = jnp.float32


def scale_layout(slots):
    squares = np.array(patch_sides[:SCALES], dtype=np.int64) ** 2
    bounds = np.cumsum(squares)
    scale_ids = np.searchsorted(bounds, np.arange(slots), side="right")
    return (bounds.astype(np.int32), scale_ids.astype(np.int32))


def norm_rows(values):
    centre = values - jnp.mean(values, axis=-1, keepdims=True)
    spread = jnp.mean(centre * centre, axis=-1, keepdims=True)
    return centre * lax.rsqrt(spread + norm_eps)


def modulate(values, scale_row, shift_row):
    return norm_rows(values) * (1.0 + scale_row) + shift_row


def gelu_tanh(values):
    return jax.nn.gelu(values, approximate=True)


def gelu_and_slope(v):
    root = np.float32(np.sqrt(2 / np.pi))
    square = v * v
    t = jnp.tanh(root * (v + 0.044715 * (v * square)))
    slope = 0.5 * (1.0 + t) + (0.5 * v) * (1.0 - t * t) * (root * (1.0 + 0.134145 * square))
    return [slope, 0.5 * v * (1.0 + t)]


def learn_rates():
    return (D ** (-0.5), (D // 16) ** (-0.5), D ** (-0.5), FF ** (-0.5), D ** (-0.5), 1.0)


def adamw(weight, gradient, first, second, bias_one, bias_two, rate):
    first_new = 0.5 * first + 0.5 * gradient
    second_new = 0.5 * second + 0.5 * gradient * gradient
    update = first_new / bias_one / (jnp.sqrt(second_new / bias_two) + adam_eps) + decay * weight
    weight_new = weight - rate * update
    return (weight_new, weight_new.astype(bf16), first_new, second_new)


def contract_rows(former, latter):
    return lax.dot_general(former, latter, (((0,), (0,)), ((), ())), preferred_element_type=f32)


def contract_cols(former, latter):
    return lax.dot_general(former, latter, (((1,), (1,)), ((), ())), preferred_element_type=f32)


def dot_nt(former, latter):
    return lax.dot_general(former, latter, (((1,), (1,)), ((), ())), preferred_element_type=f32)


def dot_nn(former, latter):
    return lax.dot_general(former, latter, (((1,), (0,)), ((), ())), preferred_element_type=f32)


def dot_tn(former, latter):
    return lax.dot_general(former, latter, (((0,), (0,)), ((), ())), preferred_element_type=f32)


FORWARD_TILES = ((0, 240, 256), (240, 416, 432), (416, 680, 680))
BACKWARD_TILES = ((0, 128, 160), (128, 384, 432), (384, 680, 680))


def attend_kernel(q_ref, k_ref, v_ref, bias_ref, context_ref, lse_ref):
    for begin, end, keys in FORWARD_TILES:
        q = q_ref[begin:end, :] * bf16(0.125)
        lane = lax.broadcasted_iota(jnp.int32, q.shape, 1)
        contexts, totals = [], []
        for head in range(2):
            own = jnp.where((lane < HEAD) == (head == 0), q, bf16(0))
            scores = dot_nt(own, k_ref[:keys, :]) + bias_ref[begin:end, :keys]
            largest = jnp.max(scores, axis=1, keepdims=True)
            expo = jnp.exp(scores - largest)
            total = jnp.sum(expo, axis=1, keepdims=True)
            probs = (expo * (1.0 / total)).astype(bf16)
            totals.append(largest + jnp.log(total))
            contexts.append(dot_nn(probs, v_ref[:keys, :]))
        left = lax.broadcasted_iota(jnp.int32, contexts[0].shape, 1) < HEAD
        context_ref[begin:end, :] = jnp.where(left, contexts[0], contexts[1]).astype(bf16)
        lse = jnp.where(left, totals[0], totals[1]).T
        lse_ref[0, 0:1, begin:end] = lse[0:1]
        lse_ref[0, 1:2, begin:end] = lse[HEAD : HEAD + 1]


def attend_forward(packed, bias, begin, end, so_far=None):
    slots, width = packed.shape[0], packed.shape[1] // 3
    pairs = width // 128
    assert slots == FORWARD_TILES[-1][1]

    def block(offset):
        return pl.BlockSpec((slots, 128), lambda i: (0, offset + begin + i))

    more = list(so_far) if so_far else []

    def kernel(q_ref, k_ref, v_ref, bias_ref, *refs):
        attend_kernel(q_ref, k_ref, v_ref, bias_ref, *refs[len(more) :])

    return pl.pallas_call(
        kernel,
        grid=(end - begin,),
        in_specs=[
            block(0),
            block(pairs),
            block(2 * pairs),
            pl.BlockSpec((slots, slots), lambda i: (0, 0), pipeline_mode=pl.Buffered(1)),
        ]
        + [pl.BlockSpec(memory_space=pl.ANY)] * len(more),
        out_specs=[block(0), pl.BlockSpec((1, 2, slots), lambda i: (begin + i, 0, 0))],
        out_shape=[
            jax.ShapeDtypeStruct((slots, width), bf16),
            jax.ShapeDtypeStruct((pairs, 2, slots), f32),
        ],
        input_output_aliases={4 + i: i for i in range(len(more))},
        cost_estimate=estimate(
            flops=5 * slots * slots * width,
            bytes_accessed=6 * slots * width,
            transcendentals=slots * slots * HEADS // 2,
        ),
        compiler_params=pltpu.CompilerParams(vmem_limit_bytes=20 << 20),
        name="attend",
    )(packed, packed, packed, bias, *more)


def attend_back_kernel(
    half, place_ref, q_ref, k_ref, v_ref, grad_ref, lse_ref, bias_ref, out_ref, give_ref, *refs
):
    keys_ref, values_ref, y_ref, out_sems, give_sems = refs
    step = pl.program_id(0)
    slot = lax.rem(step, 2)
    width = 2 * half * 128

    def copies(step, slot, run):
        pair = lax.rem(step + (1 - place_ref[2]) * half, 2 * half)
        for i in range(3):
            at = pl.multiple_of(i * width + pair * 128, 128)
            run(
                pltpu.make_async_copy(
                    y_ref.at[slot, i], out_ref.at[:, pl.ds(at, 128)], out_sems.at[slot, i]
                )
            )

        @pl.when(step < half)
        def _():
            for i in range(3):
                at = pl.multiple_of((i * half + step) * 128, 128)
                run(
                    pltpu.make_async_copy(
                        y_ref.at[slot, i], give_ref.at[:, pl.ds(at, 128)], give_sems.at[slot, i]
                    )
                )

    @pl.when(step >= 2)
    def _():
        copies(step - 2, slot, lambda copy: copy.wait())

    for count, (begin, end, keys) in enumerate(reversed(BACKWARD_TILES)):
        q = q_ref[begin:end, :] * bf16(0.125)
        grad = grad_ref[begin:end, :]
        k = k_ref[:keys, :]
        v = v_ref[:keys, :]
        left = lax.broadcasted_iota(jnp.int32, q.shape, 1) < HEAD
        d_q, d_k, d_v = [], [], []
        for head in range(2):
            own = left == (head == 0)
            scores = dot_nt(k, jnp.where(own, q, bf16(0))) + bias_ref[:keys, begin:end]
            probs = jnp.exp(scores - lse_ref[0, head : head + 1, begin:end])
            d_probs = dot_nt(v, jnp.where(own, grad, bf16(0)))
            inner = jnp.sum(probs * d_probs, axis=0, keepdims=True)
            d_scores = (probs * (d_probs - inner)).astype(bf16)
            d_v.append(dot_nn(probs.astype(bf16), grad))
            d_k.append(dot_nn(d_scores, q))
            d_q.append(dot_tn(d_scores, k))
        first = lax.broadcasted_iota(jnp.int32, d_k[0].shape, 1) < HEAD
        d_k = jnp.where(first, d_k[0], d_k[1])
        d_v = jnp.where(first, d_v[0], d_v[1])
        if count == 0:
            keys_ref[:keys, :] = d_k
            values_ref[:keys, :] = d_v
        else:
            keys_ref[:keys, :] += d_k
            values_ref[:keys, :] += d_v
        y_ref[slot, 0, begin:end, :] = (jnp.where(left, d_q[0], d_q[1]) * 0.125).astype(bf16)
    y_ref[slot, 1] = keys_ref[...].astype(bf16)
    y_ref[slot, 2] = values_ref[...].astype(bf16)
    copies(step, slot, lambda copy: copy.start())

    @pl.when(step == 2 * half - 1)
    def _():
        copies(step - 1, 1 - slot, lambda copy: copy.wait())
        copies(step, slot, lambda copy: copy.wait())


def attend_backward(place, packed, d_context, lse, bias_t):
    slots, width = packed.shape[0], packed.shape[1] // 3
    pairs = width // 128
    half = pairs // 2
    assert slots == BACKWARD_TILES[-1][1] and pairs >= 2

    def at(i, place):
        return lax.rem(i + (1 - place[2]) * half, pairs)

    def block(offset):
        return pl.BlockSpec((slots, 128), lambda i, place: (0, offset + at(i, place)))

    return pl.pallas_call(
        functools.partial(attend_back_kernel, half),
        grid_spec=pltpu.PrefetchScalarGridSpec(
            num_scalar_prefetch=1,
            grid=(pairs,),
            in_specs=[
                block(0),
                block(pairs),
                block(2 * pairs),
                block(0),
                pl.BlockSpec((1, 2, slots), lambda i, place: (at(i, place), 0, 0)),
                pl.BlockSpec((slots, slots), lambda i, place: (0, 0), pipeline_mode=pl.Buffered(1)),
            ],
            out_specs=[pl.BlockSpec(memory_space=pl.ANY)] * 2,
            scratch_shapes=[
                pltpu.VMEM((slots, 128), f32),
                pltpu.VMEM((slots, 128), f32),
                pltpu.VMEM((2, 3, slots, 128), bf16),
                pltpu.SemaphoreType.DMA((2, 3)),
                pltpu.SemaphoreType.DMA((2, 3)),
            ],
        ),
        out_shape=[
            jax.ShapeDtypeStruct((slots, 3 * width), bf16),
            jax.ShapeDtypeStruct((slots, 3 * width // 2), bf16),
        ],
        cost_estimate=estimate(
            flops=20 * slots * slots * width,
            bytes_accessed=16 * slots * width,
            transcendentals=slots * slots * HEADS,
        ),
        compiler_params=pltpu.CompilerParams(vmem_limit_bytes=28 << 20),
        name="attend_back",
    )(place, packed, packed, packed, d_context, lse, bias_t)


def start_pieces(place_ref, pieces, w_ref, sems, rows, left, half, color):
    z, x, c, y = [place_ref[i] for i in range(4)]
    for far in range(2):
        for core in range(2):
            piece = pieces[core * 4 + far * 2 + color]
            for near in range(2):
                step_x, step_y = (far, near) if color == 0 else (near, far)
                for step in range(4):
                    at = (z ^ FLIPS[step]) * 2 + (x ^ step_x)
                    at = (at * 2 + (c ^ core)) * 2 + (y ^ step_y)
                    at = pl.multiple_of(at * rows, rows)
                    pltpu.make_async_copy(
                        piece.at[near, step, :, pl.ds(left, half)],
                        w_ref.at[color, pl.ds(at, rows), :],
                        sems.at[color],
                    ).start()


def gather_kernel(layout, place_ref, x_ref, *refs):
    rows, left, half, chunk, gelu, keep = layout
    outs = 2 if gelu else 1
    pieces, refs = refs[:8], refs[8:]
    whole_ref, refs = (refs[0], refs[1:]) if keep else (None, refs)
    out_refs, w_ref, y_refs = refs[:outs], refs[outs], refs[outs + 1 : 2 * outs + 1]
    in_sems, whole_sems, out_sems = refs[2 * outs + 1 :]
    start = functools.partial(start_pieces, place_ref, pieces, w_ref, in_sems, rows, left, half)
    start(0)
    waits = []
    for color in range(2):
        own = w_ref.at[color]
        pltpu.make_async_copy(own, own, in_sems.at[color]).wait()
        if color == 0:
            start(1)
        if keep:
            copy = pltpu.make_async_copy(
                own, whole_ref.at[:, pl.ds(color * half, half)], whole_sems.at[color]
            )
            copy.start()
            waits.append(copy)
        for begin in range(0, half, chunk):
            at = color * half + begin
            result = dot_nn(x_ref[...], w_ref[color, :, begin : begin + chunk])
            values = gelu_and_slope(result) if gelu else [result]
            for i, value in enumerate(values):
                y_refs[i][:, at : at + chunk] = value.astype(y_refs[i].dtype)
                copy = pltpu.make_async_copy(
                    y_refs[i].at[:, pl.ds(at, chunk)],
                    out_refs[i].at[:, pl.ds(at, chunk)],
                    out_sems.at[i, at // chunk],
                )
                copy.start()
                waits.append(copy)
    for copy in waits:
        copy.wait()


def gather_dot(place, x, pieces, left, half, kinds, keep, name):
    rows = pieces[0].shape[2]
    whole, width = rows * 32, 2 * half
    slots = x.shape[0]
    chunk = min(512, half)
    anywhere = pl.BlockSpec(memory_space=pl.ANY)
    shapes = [jax.ShapeDtypeStruct((whole, width), bf16)] * keep
    shapes += [jax.ShapeDtypeStruct((slots, width), kind) for kind in kinds]
    return pl.pallas_call(
        functools.partial(gather_kernel, (rows, left, half, chunk, len(kinds) == 2, keep)),
        grid_spec=pltpu.PrefetchScalarGridSpec(
            num_scalar_prefetch=1,
            grid=(1,),
            in_specs=[pl.BlockSpec(x.shape, lambda i, place: (0, 0))] + [anywhere] * 8,
            out_specs=[anywhere] * len(shapes),
            scratch_shapes=[pltpu.VMEM((2, whole, half), bf16)]
            + [pltpu.VMEM((slots, width), kind) for kind in kinds]
            + [
                pltpu.SemaphoreType.DMA((2,)),
                pltpu.SemaphoreType.DMA((2,)),
                pltpu.SemaphoreType.DMA((len(kinds), width // chunk)),
            ],
        ),
        out_shape=shapes,
        cost_estimate=estimate(
            flops=3 * slots * whole * width,
            bytes_accessed=2 * whole * width + 4 * slots * width,
            transcendentals=0,
        ),
        compiler_params=pltpu.CompilerParams(vmem_limit_bytes=56 << 20),
        name=name,
    )(place, x, *pieces)


def modulate_back_kernel(steps, more, place_ref, x_ref, w_ref, rows_ref, *refs):
    value_hbm, add_hbm, refs = refs[0], refs[1], refs[2:]
    if more:
        attended_hbm, proj_hbm, refs = refs[0], refs[1], refs[2:]
        out_hbm, low_hbm, give_hbm, context_hbm, sums_ref, refs = *refs[:5], refs[5:]
        total_ref, value_ref, add_ref, attended_ref, proj_ref, low_ref, context_ref, sems = refs
    else:
        out_hbm, sums_ref, total_ref, value_ref, add_ref, sems = refs
    step = pl.program_id(0)
    pairs = [(value_hbm, value_ref), (add_hbm, add_ref)]
    if more:
        pairs += [(attended_hbm, attended_ref), (proj_hbm, proj_ref)]
    loads = [pltpu.make_async_copy(a, b, sems.at[i]) for i, (a, b) in enumerate(pairs)]
    part = dot_nt(x_ref[...], w_ref[...])

    @pl.when(step == 0)
    def _():
        for load in loads:
            load.start()
        total_ref[...] = part

    @pl.when(step > 0)
    def _():
        total_ref[...] += part

    @pl.when(step == steps - 1)
    def _():
        for load in loads:
            load.wait()
        slots, width = total_ref.shape
        gain = rows_ref[0:1, :]
        length = place_ref[4]

        def block(at, count, sums):
            value = value_ref[pl.ds(at, count), :].astype(f32)
            centre = value - jnp.mean(value, axis=1, keepdims=True)
            rate = lax.rsqrt(jnp.mean(centre * centre, axis=1, keepdims=True) + norm_eps)
            normal = centre * rate
            grad = total_ref[pl.ds(at, count), :]
            scaled = grad * gain
            inner = jnp.mean(scaled * normal, axis=1, keepdims=True)
            result = rate * (scaled - jnp.mean(scaled, axis=1, keepdims=True) - normal * inner)
            add = add_ref[pl.ds(at, count), :].astype(f32)
            sums = [
                sums[0] + jnp.sum(grad * normal, axis=0, keepdims=True),
                sums[1] + jnp.sum(grad, axis=0, keepdims=True),
            ] + sums[2:]
            if more:
                slot = at + lax.broadcasted_iota(jnp.int32, (count, 1), 0)
                add = add * (slot < length).astype(f32)
            result = add + result
            total_ref[pl.ds(at, count), :] = result
            if more:
                attended = attended_ref[pl.ds(at, count), :]
                sums[2] = sums[2] + jnp.sum(result * attended, axis=0, keepdims=True)
                low_ref[pl.ds(at, count), :] = (result * rows_ref[1:2, :]).astype(bf16)
            return sums

        count = 32
        whole = slots // count
        sums = [jnp.zeros((1, width), f32) for _ in range(3 if more else 2)]
        sums = lax.fori_loop(
            0, whole, lambda i, sums: block(pl.multiple_of(i * count, count), count, sums), sums
        )
        if slots % count:
            sums = block(whole * count, slots % count, sums)
        sums_ref[...] = jnp.concatenate(
            sums + [jnp.zeros((8 - len(sums), width), f32)], axis=0
        )
        stores = [pltpu.make_async_copy(total_ref, out_hbm, sems.at[4])]
        if more:
            half = width // 2
            other = pl.multiple_of((1 - place_ref[2]) * half, half)
            stores += [
                pltpu.make_async_copy(low_ref.at[:, pl.ds(other, half)], give_hbm, sems.at[5]),
                pltpu.make_async_copy(low_ref, low_hbm, sems.at[6]),
            ]
        for store in stores:
            store.start()
        if more:
            context_ref[...] = dot_nt(low_ref[...], proj_ref[...]).astype(bf16)
            stores.append(pltpu.make_async_copy(context_ref, context_hbm, sems.at[7]))
            stores[-1].start()
        for store in stores:
            store.wait()


def modulate_back(place, x, weight, rows, value, add, attended=None, proj=None):
    more = proj is not None
    slots, depth = x.shape
    width = weight.shape[0]
    chunk = 1024
    assert depth % chunk == 0
    anywhere = pl.BlockSpec(memory_space=pl.ANY)
    operands = [value, add] + ([attended, proj] if more else [])
    shapes = [jax.ShapeDtypeStruct((slots, width), f32)]
    scratch = [
        pltpu.VMEM((slots, width), f32),
        pltpu.VMEM((slots, width), value.dtype),
        pltpu.VMEM((slots, width), add.dtype),
    ]
    if more:
        shapes += [
            jax.ShapeDtypeStruct((slots, width), bf16),
            jax.ShapeDtypeStruct((slots, width // 2), bf16),
            jax.ShapeDtypeStruct((slots, width), bf16),
        ]
        scratch += [
            pltpu.VMEM((slots, width), f32),
            pltpu.VMEM(proj.shape, bf16),
            pltpu.VMEM((slots, width), bf16),
            pltpu.VMEM((slots, width), bf16),
        ]
    return pl.pallas_call(
        functools.partial(modulate_back_kernel, depth // chunk, more),
        grid_spec=pltpu.PrefetchScalarGridSpec(
            num_scalar_prefetch=1,
            grid=(depth // chunk,),
            in_specs=[
                pl.BlockSpec((slots, chunk), lambda i, place: (0, i)),
                pl.BlockSpec((width, chunk), lambda i, place: (0, i)),
                pl.BlockSpec((8, width), lambda i, place: (0, 0)),
            ]
            + [anywhere] * len(operands),
            out_specs=[anywhere] * len(shapes)
            + [pl.BlockSpec((8, width), lambda i, place: (0, 0))],
            scratch_shapes=scratch + [pltpu.SemaphoreType.DMA((8,))],
        ),
        out_shape=shapes + [jax.ShapeDtypeStruct((8, width), f32)],
        cost_estimate=estimate(
            flops=3 * slots * width * (depth + width * more),
            bytes_accessed=2 * (slots + width) * depth + 16 * slots * width,
            transcendentals=0,
        ),
        compiler_params=pltpu.CompilerParams(vmem_limit_bytes=48 << 20),
        name="modulate_back",
    )(place, x, weight, rows, *operands)


def gelu_back_kernel(rows, place_ref, grad_ref, slope_ref, *refs):
    pieces, (out_ref, give_ref), refs = refs[:8], refs[8:10], refs[10:]
    w_ref, s_ref, y_ref, in_sems, s_sems, y_sems, give_sems = refs
    z, x, c, y = [place_ref[i] for i in range(4)]
    block = 4 * rows
    chunks = [(step, far_x) for step in range(4) for far_x in range(2)]
    where = [
        pl.multiple_of(((z ^ FLIPS[step]) * 2 + (x ^ far_x)) * block, block) for step, far_x in chunks
    ]
    half = pieces[0].shape[-1]

    def start(n):
        step, far_x = chunks[n]
        for core in range(2):
            for far_y in range(2):
                at = pl.multiple_of(((c ^ core) * 2 + (y ^ far_y)) * rows, rows)
                for color in range(2):
                    far, near = (far_x, far_y) if color == 0 else (far_y, far_x)
                    pltpu.make_async_copy(
                        pieces[core * 4 + far * 2 + color].at[near, step],
                        w_ref.at[n, pl.ds(at, rows), pl.ds(color * half, half)],
                        in_sems.at[n],
                    ).start()
        pltpu.make_async_copy(
            slope_ref.at[:, pl.ds(where[n], block)], s_ref.at[n], s_sems.at[n]
        ).start()

    ahead = 2
    for n in range(ahead):
        start(n)
    waits = []
    for n in range(len(chunks)):
        pltpu.make_async_copy(w_ref.at[n], w_ref.at[n], in_sems.at[n]).wait()
        pltpu.make_async_copy(s_ref.at[n], s_ref.at[n], s_sems.at[n]).wait()
        if n + ahead < len(chunks):
            start(n + ahead)
        y_ref[n] = (dot_nt(grad_ref[...], w_ref[n]) * s_ref[n].astype(f32)).astype(bf16)
        copy = pltpu.make_async_copy(
            y_ref.at[n], out_ref.at[:, pl.ds(where[n], block)], y_sems.at[n]
        )
        copy.start()
        waits.append(copy)
    for n, (step, far_x) in enumerate(chunks):
        other = lax.shift_right_logical(z ^ FLIPS[step], 1) != c

        @pl.when(other)
        def _(n=n):
            at = pl.multiple_of(where[n] - (1 - c) * (4 * block), block)
            copy = pltpu.make_async_copy(
                y_ref.at[n], give_ref.at[:, pl.ds(at, block)], give_sems.at[n]
            )
            copy.start()
            copy.wait()

    for copy in waits:
        copy.wait()


def gelu_back_dot(place, grad, slope, pieces):
    slots, width = slope.shape
    rows = pieces[0].shape[2]
    assert width == 32 * rows and grad.shape[1] == 2 * pieces[0].shape[3]
    anywhere = pl.BlockSpec(memory_space=pl.ANY)
    block = 4 * rows
    return pl.pallas_call(
        functools.partial(gelu_back_kernel, rows),
        grid_spec=pltpu.PrefetchScalarGridSpec(
            num_scalar_prefetch=1,
            grid=(1,),
            in_specs=[pl.BlockSpec(grad.shape, lambda i, place: (0, 0))] + [anywhere] * 9,
            out_specs=[anywhere] * 2,
            scratch_shapes=[
                pltpu.VMEM((8, block, grad.shape[1]), bf16),
                pltpu.VMEM((8, slots, block), slope.dtype),
                pltpu.VMEM((8, slots, block), bf16),
            ]
            + [pltpu.SemaphoreType.DMA((8,))] * 4,
        ),
        out_shape=[
            jax.ShapeDtypeStruct((slots, width), bf16),
            jax.ShapeDtypeStruct((slots, width // 2), bf16),
        ],
        cost_estimate=estimate(
            flops=3 * slots * width * grad.shape[1],
            bytes_accessed=8 * slots * width + 4 * width * grad.shape[1],
            transcendentals=0,
        ),
        compiler_params=pltpu.CompilerParams(vmem_limit_bytes=56 << 20),
        name="gelu_back",
    )(place, grad, slope, *pieces)


def weight_grad_kernel(depth, rows, turn, firsts, place_ref, *refs):
    products = len(firsts)
    ins, out_refs = refs[: 4 * products], refs[4 * products :]
    step = pl.program_id(0)
    inner = lax.rem(step, turn)

    def product(own_ref, other_ref, mine_ref, take_ref):
        total = dot_tn(own_ref[...], mine_ref[...]) + dot_tn(other_ref[...], take_ref[...])
        total = total.reshape(depth, 2, 2, 2, rows, total.shape[-1])

        @pl.when(step < turn)
        def _():
            first = place_ref[3] == 0
            for x in range(2):
                low, high = total[:, x, :, 0], total[:, x, :, 1]
                out_refs[0][x] = jnp.where(first, high, low).astype(bf16)
                out_refs[1][x] = jnp.where(first, low, high).astype(bf16)

        @pl.when(step >= turn)
        def _():
            first = place_ref[1] == 0
            for y in range(2):
                low, high = total[:, 0, :, y], total[:, 1, :, y]
                out_refs[2][y] = jnp.where(first, high, low).astype(bf16)
                out_refs[3][y] = jnp.where(first, low, high).astype(bf16)

    if products == 1:
        product(*ins)
        return
    for n, (begin, end) in enumerate(firsts):

        @pl.when((inner >= begin) & (inner < end))
        def _(n=n):
            product(*ins[4 * n : 4 * n + 4])


def weight_grad_call(place, products, rows, chunk):
    specs, operands, firsts = [], [], []
    turn = flops = 0
    for own, other, rhs, take, groups in products:
        slots, columns = rhs.shape[0], rhs.shape[1] // groups
        per = columns // 2 // chunk
        count = groups * per // 2
        assert groups * per % 2 == 0 and columns % (2 * chunk) == 0
        flops += 6 * slots * own.shape[1] * groups * columns // 2
        firsts.append((turn, turn + count))
        specs.append((per, count, turn))
        turn += count
        operands += [own, other, rhs, take]
    in_specs = []
    for (own, *_), (per, count, begin) in zip(products, specs):
        slots = own.shape[0]

        def which(i, count=count, begin=begin):
            color = i // turn
            return color * count + jnp.clip(i - color * turn - begin, 0, count - 1)

        once = pl.Buffered(1)
        in_specs += [pl.BlockSpec(own.shape, lambda i, place: (0, 0), pipeline_mode=once)] * 2
        in_specs.append(
            pl.BlockSpec(
                (slots, chunk),
                lambda i, place, which=which, per=per: (
                    0,
                    (which(i) // per * 2 + place[2]) * per + lax.rem(which(i), per),
                ),
            )
        )
        in_specs.append(
            pl.BlockSpec((slots, chunk), lambda i, place, which=which: (0, which(i)))
        )
    width = products[0][0].shape[1]
    depth = width // rows // 8
    block = (2, depth, 2, rows, chunk)
    early = pl.BlockSpec(block, lambda i, place: (0, 0, 0, 0, jnp.minimum(i, turn - 1)))
    late = pl.BlockSpec(block, lambda i, place: (0, 0, 0, 0, jnp.maximum(i - turn, 0)))
    shape = jax.ShapeDtypeStruct((2, depth, 2, rows, turn * chunk), bf16)
    return pl.pallas_call(
        functools.partial(weight_grad_kernel, depth, rows, turn, tuple(firsts)),
        grid_spec=pltpu.PrefetchScalarGridSpec(
            num_scalar_prefetch=1,
            grid=(2 * turn,),
            in_specs=in_specs,
            out_specs=[early, early, late, late],
        ),
        out_shape=[shape] * 4,
        cost_estimate=estimate(
            flops=flops,
            bytes_accessed=sum(2 * v.size for v in operands) + 4 * width * turn * chunk,
            transcendentals=0,
        ),
        compiler_params=pltpu.CompilerParams(vmem_limit_bytes=60 << 20),
        name="weight_grad",
    )(place, *operands)


def estimate(flops, bytes_accessed, transcendentals):
    return pl.CostEstimate(
        flops=flops // 64, bytes_accessed=bytes_accessed // 64, transcendentals=transcendentals // 64
    )


class Line:
    def __init__(self):
        self.last = jnp.zeros((8, 128), f32)

    def __call__(self, *values):
        self.last, values = lax.optimization_barrier((self.last, values))
        return values[0] if len(values) == 1 else values

    def arrive(self, movers, *values):
        gots, values = self([mover.got for mover in movers], values)
        for mover, got in zip(movers, gots):
            mover.got = got
        return values[0] if len(values) == 1 else values


class Scatter:
    def __init__(self, grid, line, rows):
        self.grid, self.line, self.flips = grid, line, grid.bits()
        self.rows = rows.reshape([2] * len(self.flips) + list(rows.shape[1:]))

    def start(self):
        dim = len(self.flips) - 1
        axis, bit = self.flips.pop(0)
        self.own = lax.index_in_dim(self.rows, 0, dim, keepdims=False)
        away = self.line(lax.index_in_dim(self.rows, 1, dim, keepdims=False))
        self.got = self.grid.flip(away, axis, bit)

    def add(self):
        self.rows = self.own + self.got


class Gather:
    orders = ("yx", "xy")

    def __init__(self, grid, line, shards):
        self.grid, self.line = grid, line
        lows = [shard[:, : shard.shape[1] // 2] for shard in shards]
        highs = [shard[:, shard.shape[1] // 2 :] for shard in shards]
        self.shard = jnp.concatenate(lows + highs, axis=1)

    def first(self):
        self.shard = self.line(self.shard)
        self.got = self.grid.flip(self.shard, "z", 2)

    def second(self):
        self.pair = self.line(jnp.stack([self.shard, self.got]))
        self.got = self.grid.flip(self.pair, "z", 1)

    def third(self):
        half = self.shard.shape[1] // 2
        pairs = (self.pair, self.got)
        rows = [
            jnp.concatenate([p[:, :, i * half : (i + 1) * half] for p in pairs], axis=0)
            for i in range(2)
        ]
        self.rows = self.line(*rows)
        self.got = [self.grid.flip(v, o[0], 1) for v, o in zip(self.rows, self.orders)]

    def fourth(self):
        plane = [
            jnp.concatenate([own[None], new[None]], axis=0) for own, new in zip(self.rows, self.got)
        ]
        self.plane = self.line(*plane)
        self.got = [self.grid.flip(v, o[1], 1) for v, o in zip(self.plane, self.orders)]

    def pieces(self):
        mine = list(self.plane) + list(self.got)
        return mine + [self.grid.flip(v, "c", 1) for v in mine]


FLIPS = (0, 2, 1, 3)


class GradSum:
    def __init__(self, grid, line, here, place, products, rows, chunk):
        self.grid, self.line, self.here, self.rows = grid, line, here, rows
        self.shapes = [(groups, rhs.shape[1] // groups) for _, _, rhs, _, groups in products]
        away_one, self.one, away_two, self.two = line(
            *weight_grad_call(place, products, rows, chunk)
        )
        self.got = [grid.flip(away_one, "y", 1), grid.flip(away_two, "x", 1)]

    def sums(self):
        got_one, got_two = self.got
        one = self.one.astype(f32) + got_one.astype(f32)
        return one, self.two.astype(f32) + got_two.astype(f32)

    def second(self):
        one, two = self.sums()
        away = []
        for total, axis in ((one, "x"), (two, "y")):
            give = lax.dynamic_index_in_dim(total, 1 - self.here[axis], 0, keepdims=False)
            away.append(give.astype(bf16))
        self.one = lax.dynamic_index_in_dim(one, self.here["x"], 0, keepdims=False)
        self.two = lax.dynamic_index_in_dim(two, self.here["y"], 0, keepdims=False)
        away = self.line(*away)
        self.got = [self.grid.flip(away[0], "x", 1), self.grid.flip(away[1], "y", 1)]

    def third(self):
        both = jnp.concatenate(self.sums(), axis=-1)
        both = both.reshape((2, 2) + both.shape[1:])
        low = self.here["z"] % 2
        self.both = lax.dynamic_index_in_dim(both, low, 1, keepdims=False)
        away = lax.dynamic_index_in_dim(both, 1 - low, 1, keepdims=False).astype(bf16)
        self.got = self.grid.flip(self.line(away), "z", 1)

    def fourth(self):
        both = self.both + self.got.astype(f32)
        high = self.here["z"] // 2
        self.both = lax.dynamic_index_in_dim(both, high, 0, keepdims=False)
        away = lax.dynamic_index_in_dim(both, 1 - high, 0, keepdims=False).astype(bf16)
        self.got = self.grid.flip(self.line(away), "z", 2)

    def fifth(self):
        both = self.both + self.got.astype(f32)
        core = self.here["c"]
        self.keep = lax.dynamic_index_in_dim(both, core, 0, keepdims=False)
        give = lax.dynamic_index_in_dim(both, 1 - core, 0, keepdims=False)
        self.take = self.grid.flip(self.line(give), "c", 1)

    def result(self):
        first = self.here["c"] == 0
        low = jnp.where(first, self.keep, self.take)
        high = jnp.where(first, self.take, self.keep)
        sums, left, middle = [], 0, low.shape[1] // 2
        for groups, columns in self.shapes:
            part = groups * columns // 4
            sides = []
            for side in (low, high):
                colors = [side[:, left : left + part], side[:, middle + left : middle + left + part]]
                side = jnp.concatenate(colors, axis=1)
                sides.append(side.reshape(self.rows, groups, 1, columns // 2))
            sums.append(jnp.concatenate(sides, axis=2).reshape(self.rows, groups * columns))
            left += part
        return sums


class Grid:
    def __init__(self, fsdp, grp):
        outer = fsdp // 2
        self.size = {"c": 2, "x": 2 if outer % 2 == 0 else 1, "y": grp}
        self.size["z"] = outer // self.size["x"]
        self.count = fsdp * grp
        self.fsdp = fsdp

    def here(self):
        place = lax.axis_index("fsdp")
        wide = self.size["x"]
        return {
            "c": place % 2,
            "x": (place // 2) % wide,
            "z": place // (2 * wide),
            "y": lax.axis_index("grp"),
        }

    def shift(self, array, axis, step):
        size = self.size[axis]
        if axis == "y":
            return lax.ppermute(array, "grp", [(i, (i + step) % size) for i in range(size)])
        stride = {"c": 1, "x": 2, "z": 2 * self.size["x"]}[axis]
        pairs = []
        for i in range(self.fsdp):
            at = (i // stride) % size
            pairs.append((i, i + ((at + step) % size - at) * stride))
        return lax.ppermute(array, "fsdp", pairs)

    def fits(self, rows):
        size = self.size
        return size["x"] == 2 and size["y"] == 2 and size["z"] == 4 and rows % 32 == 0

    def bits(self):
        flips = []
        for axis in "cxyz":
            size = self.size[axis]
            assert size & (size - 1) == 0
            bit = size // 2
            while bit:
                flips.append((axis, bit))
                bit //= 2
        return flips

    def gather_all(self, row, flips):
        for axis, bit in flips:
            row = jnp.concatenate([row[None], self.flip(row, axis, bit)[None]], axis=0)
        return row

    def sources(self, here):
        flips = self.bits()
        turn = {axis: np.zeros(self.count, np.int32) for axis in "cxyz"}
        for n in range(self.count):
            for k, (axis, bit) in enumerate(flips):
                if n >> k & 1:
                    turn[axis][n] ^= bit
        z, x, c, y = [here[axis] ^ turn[axis] for axis in "zxcy"]
        return ((z * self.size["x"] + x) * 2 + c) * self.size["y"] + y

    def flip(self, array, axis, bit):
        size = self.size[axis]
        if axis == "y":
            return lax.ppermute(array, "grp", [(i, i ^ bit) for i in range(size)])
        stride = {"c": 1, "x": 2, "z": 2 * self.size["x"]}[axis]
        pairs = [
            (i, i + (((i // stride) % size ^ bit) - (i // stride) % size) * stride)
            for i in range(self.fsdp)
        ]
        return lax.ppermute(array, "fsdp", pairs)

    def scatter_sum(self, array, axis, dim, here, kind=bf16):
        size = self.size[axis]
        total = lax.dynamic_index_in_dim(array, here[axis], dim, keepdims=False)
        for step in range(1, size):
            piece = lax.dynamic_index_in_dim(array, (here[axis] + step) % size, dim, keepdims=False)
            total = total + self.shift(piece.astype(kind), axis, step).astype(f32)
        return total


def per_device(
    grid,
    block_in,
    cotangent,
    stop_scale,
    class_label,
    w_qkv,
    w_proj,
    w_fc1,
    w_fc2,
    w_ada,
    w_table,
    m_qkv,
    m_proj,
    m_fc1,
    m_fc2,
    m_ada,
    m_table,
    v_qkv,
    v_proj,
    v_fc1,
    v_fc2,
    v_ada,
    v_table,
):
    items, slots, width = block_in.shape
    assert items == 1
    here = grid.here()
    bounds, scale_ids = scale_layout(slots)
    picked = jnp.arange(SCALES) == stop_scale[0] - 1
    length = jnp.sum(jnp.where(picked, jnp.asarray(bounds), 0))
    position = jnp.arange(slots)
    valid = (position < length).astype(f32)[:, None]
    scale_table = jnp.asarray(scale_ids)
    allowed = (scale_table[None, :] <= scale_table[:, None]) & (position[None, :] < length)
    bias = jnp.where(allowed, f32(0), f32(-1e30))
    bias_t = bias.T
    place = jnp.stack([here[axis] for axis in "zxcy"] + [length]).astype(jnp.int32)
    fits = grid.fits(w_qkv.shape[0])
    cast_qkv, cast_proj, cast_fc1, cast_fc2 = [
        w.astype(bf16) for w in (w_qkv, w_proj, w_fc1, w_fc2)
    ]
    half_qkv, half_proj, half_fc1 = [w.shape[1] // 2 for w in (w_qkv, w_proj, w_fc1)]
    line = Line()
    if fits:
        all_qkv = Gather(grid, line, [cast_qkv])
        all_qkv.first()
    labels = lax.all_to_all(
        jnp.broadcast_to(class_label, (grid.count,)), AXES, 0, 0, tiled=True
    )
    labels = jnp.take(labels, grid.sources(here))
    cast_ada = w_ada.astype(bf16)
    cast_table = w_table.astype(bf16)
    onehot = (labels[:, None] == jnp.arange(cast_table.shape[0])[None, :]).astype(bf16)
    cond = jnp.dot(onehot, cast_table, preferred_element_type=f32)
    silu_out, silu_back = jax.vjp(jax.nn.silu, cond)
    lifted_low = silu_out.astype(bf16)

    ada = jnp.dot(lifted_low, cast_ada, preferred_element_type=f32)
    flips = grid.bits()
    along = len(flips) - 2
    ada = Scatter(grid, line, ada.reshape(grid.count, -1, 128))
    if fits:
        ada.start()
        line.arrive([ada, all_qkv])
        ada.add()
        all_qkv.second()
        ada.start()
        line.arrive([ada])
        ada.add()
        line.arrive([all_qkv])
        all_qkv.third()
        all_rest = Gather(grid, line, [cast_proj, cast_fc1])
        all_rest.first()
        ada.start()
        line.arrive([ada])
        ada.add()
        line.arrive([all_qkv])
        all_qkv.fourth()
        ada.start()
        line.arrive([ada, all_rest])
        ada.add()
        ada.start()
        all_rest.second()
        line.arrive([ada])
        ada.add()
    else:
        while ada.flips:
            ada.start()
            ada.add()
    ada = ada.rows.reshape(1, 6 * width)
    gamma_one, scale_one, shift_one, gamma_two, scale_two, shift_two = [
        ada[:, i * width : (i + 1) * width] for i in range(6)
    ]

    def half_columns(rhs, core, groups=1):
        half = rhs.shape[1] // groups // 2
        parts = [
            lax.dynamic_slice_in_dim(rhs, (2 * i + core) * half, half, 1) for i in range(groups)
        ]
        return jnp.concatenate(parts, axis=1)

    def weight_grad(lhs, other_lhs, rhs, take, groups):
        half = take.shape[1]
        size = grid.size
        rows = lhs.shape[1] // grid.count
        mine = half_columns(rhs, here["c"], groups)
        both = jnp.concatenate([mine, take], axis=0)
        grad = contract_rows(jnp.concatenate([lhs, other_lhs], axis=0), both)
        grad = grad.reshape(size["z"], size["x"], 2, size["y"], rows, half)
        middle = half // 2
        one = grid.scatter_sum(grad[..., :middle], "y", 3, here)
        two = grid.scatter_sum(grad[..., middle:], "x", 1, here)
        one = grid.scatter_sum(one, "x", 1, here)
        two = grid.scatter_sum(two, "y", 2, here)
        both = grid.scatter_sum(jnp.concatenate([one, two], axis=-1), "z", 0, here)
        keep = lax.dynamic_index_in_dim(both, here["c"], 0, keepdims=False)
        give = lax.dynamic_index_in_dim(both, 1 - here["c"], 0, keepdims=False)
        take = grid.shift(give, "c", 1)
        low = jnp.where(here["c"] == 0, keep, take).reshape(rows, groups, 1, half // groups)
        high = jnp.where(here["c"] == 0, take, keep).reshape(rows, groups, 1, half // groups)
        return jnp.concatenate([low, high], axis=2).reshape(rows, 2 * half)

    tokens = block_in[0].astype(f32)
    hidden, modulate_one = jax.vjp(modulate, tokens, scale_one, shift_one)
    hidden_low = hidden.astype(bf16)
    hidden_other = grid.shift(hidden_low, "c", 1)
    if fits:
        hidden_low = line.arrive([all_qkv, all_rest], hidden_low)
        pieces_qkv = all_qkv.pieces()
        all_rest.third()
        all_fc2 = Gather(grid, line, [cast_fc2])
        all_fc2.first()
        hidden_low, pieces_qkv[4:] = line(hidden_low, pieces_qkv[4:])
        wide_qkv, packed = gather_dot(
            place, hidden_low, pieces_qkv, 0, half_qkv, [bf16], True, "gather_qkv"
        )
        packed = line.arrive([all_rest, all_fc2], packed)
        all_rest.fourth()
        all_fc2.second()
        packed = line(packed)
    else:
        wide_qkv = lax.all_gather(cast_qkv, AXES, axis=0, tiled=True)
        packed = jnp.dot(hidden_low, wide_qkv, preferred_element_type=f32).astype(bf16)
    pairs = width // 128
    heads = line(*attend_forward(packed, bias, 0, pairs // 2))
    if fits:
        line.arrive([all_fc2])
        all_fc2.third()
    packed = line(packed)
    heads = line(*attend_forward(packed, bias, pairs // 2, pairs, heads))
    if fits:
        line.arrive([all_rest])
        pieces_rest = all_rest.pieces()
    context, lse = heads
    context_other = grid.shift(context, "c", 1)
    if fits:
        context, pieces_rest[4:] = line(context, pieces_rest[4:])
        wide_proj, attended = gather_dot(
            place, context, pieces_rest, 0, half_proj, [f32], True, "gather_proj"
        )
    else:
        wide_proj = lax.all_gather(cast_proj, AXES, axis=0, tiled=True)
        attended = jnp.dot(context, wide_proj, preferred_element_type=f32)
    if fits:
        attended = line.arrive([all_fc2], attended)
        all_fc2.fourth()
        attended = line(attended)
    middle = tokens + gamma_one * attended
    second, modulate_two = jax.vjp(modulate, middle, scale_two, shift_two)
    upstream = cotangent[0].astype(f32) * valid
    d_branch = (upstream * gamma_two).astype(bf16)
    second_low, d_branch, give = line(
        second.astype(bf16), d_branch, half_columns(d_branch, 1 - here["c"])
    )
    second_other = grid.shift(second_low, "c", 1)
    take = grid.shift(give, "c", 1)
    if fits:
        wide_fc1, slope, activated_low = gather_dot(
            place, second_low, pieces_rest, half_proj, half_fc1, [bf16, bf16], True, "gather_fc1"
        )
        slope, activated_low = line.arrive([all_fc2], slope, activated_low)
        pieces_fc2 = all_fc2.pieces()
        pieces_fc2[4:] = line(pieces_fc2[4:])
    else:
        wide_fc1 = lax.all_gather(cast_fc1, AXES, axis=0, tiled=True)
        inner = jnp.dot(second_low, wide_fc1, preferred_element_type=f32)
        slope, activated = gelu_and_slope(inner)
        activated_low = activated.astype(bf16)
    activated_low = line(activated_low)
    activated_other = grid.shift(activated_low, "c", 1)
    if fits:
        rows_in, rows_out = w_qkv.shape[0], w_fc2.shape[0]
        d_branch = line(d_branch)
        d_inner_low, give, take, activated_other = line(
            *gelu_back_dot(place, d_branch, slope, pieces_fc2), take, activated_other
        )
        pair_fc2 = (activated_low, activated_other, d_branch, take, 1)
        sum_two = GradSum(grid, line, here, place, [pair_fc2], rows_out, 256)
    else:
        wide_fc2 = lax.all_gather(cast_fc2, AXES, axis=0, tiled=True)
        sum_fc2 = weight_grad(activated_low, activated_other, d_branch, take, 1)
        d_inner_low = (contract_cols(d_branch, wide_fc2) * slope).astype(bf16)
        give = half_columns(d_inner_low, 1 - here["c"])
    take_inner = grid.shift(give, "c", 1)
    d_inner_low = line(d_inner_low)
    if fits:
        rows = [1.0 + scale_two, gamma_one, jnp.zeros((6, width), f32)]
        d_middle, d_attended, give, d_context, sums = line(
            *modulate_back(
                place,
                d_inner_low,
                wide_fc1,
                jnp.concatenate(rows, axis=0),
                middle,
                cotangent[0],
                attended,
                wide_proj,
            )
        )
        d_scale_two, d_shift_two, d_gamma_one = sums[0:1], sums[1:2], sums[2:3]
    else:
        d_second = contract_cols(d_inner_low, wide_fc1)
        d_middle_part, d_scale_two, d_shift_two = modulate_two(d_second)
        d_middle = upstream + d_middle_part
        d_gamma_one = jnp.sum(d_middle * attended, axis=0, keepdims=True)
        d_attended = (d_middle * gamma_one).astype(bf16)
        give = half_columns(d_attended, 1 - here["c"])
        d_context = contract_cols(d_attended, wide_proj).astype(bf16)
    take = grid.shift(give, "c", 1)
    if fits:
        take, take_inner = line.arrive([sum_two], take, take_inner)
        sum_two.second()
    pair_fc1 = (second_low, second_other, d_inner_low, take_inner, 1)
    pair_proj = (context, context_other, d_attended, take, 1)
    if fits:
        sum_mid = GradSum(grid, line, here, place, [pair_fc1, pair_proj], rows_in, 256)
        line.arrive([sum_two])
        sum_two.third()
    else:
        sum_fc1, sum_proj = weight_grad(*pair_fc1), weight_grad(*pair_proj)
    d_context = line(d_context)
    d_packed, give = attend_backward(place, packed, d_context, lse, bias_t)
    if fits:
        d_packed, give = line.arrive([sum_two, sum_mid], d_packed, give)
    take = grid.shift(give, "c", 1)
    if fits:
        sum_mid.second()
        sum_two.fourth()
        take = line(take)
        pair_qkv = (hidden_low, hidden_other, d_packed, take, 3)
        sum_last = GradSum(grid, line, here, place, [pair_qkv], rows_in, 256)
        line.arrive([sum_two, sum_mid])
        sum_mid.third()
        sum_two.fifth()
    else:
        sum_qkv = weight_grad(hidden_low, hidden_other, d_packed, take, 3)
    d_packed = line(d_packed)
    if fits:
        rows = [1.0 + scale_one, jnp.zeros((7, width), f32)]
        grad_in, sums = line(
            *modulate_back(
                place, d_packed, wide_qkv, jnp.concatenate(rows, axis=0), block_in[0], d_middle
            )
        )
        d_scale_one, d_shift_one = sums[0:1], sums[1:2]
    else:
        d_hidden = contract_cols(d_packed, wide_qkv)
        d_tokens, d_scale_one, d_shift_one = modulate_one(d_hidden)
        grad_in = d_middle + d_tokens
    if fits:
        line.arrive([sum_last, sum_mid])
        sum_last.second()
        sum_mid.fourth()
        activated_low = line(activated_low)
        (branch,) = gather_dot(
            place, activated_low, pieces_fc2, 0, width // 2, [f32], False, "gather_fc2"
        )
        branch = line.arrive([sum_last, sum_mid], branch)
        sum_last.third()
        sum_mid.fifth()
        branch = line(branch)
    else:
        branch = jnp.dot(activated_low, wide_fc2, preferred_element_type=f32)
    block_out = ((middle + gamma_two * branch) * valid).astype(bf16)
    d_gamma_two = jnp.sum(upstream * branch, axis=0, keepdims=True)
    d_ada = jnp.concatenate(
        [d_gamma_one, d_scale_one, d_shift_one, d_gamma_two, d_scale_two, d_shift_two], axis=0
    ).astype(bf16)
    every_ada = grid.gather_all(line(d_ada.reshape(-1, 128)), flips[:along])
    if fits:
        every_ada = line.arrive([sum_last], every_ada)
        sum_last.fourth()
    every_ada = grid.gather_all(every_ada, flips[along:])
    if fits:
        every_ada = line.arrive([sum_last], every_ada)
        sum_last.fifth()
    every_ada = every_ada.reshape(grid.count, 6 * width)
    sum_ada = contract_rows(lifted_low, every_ada)
    (d_cond,) = silu_back(contract_cols(every_ada, cast_ada))
    sum_table = lax.dot_general(
        onehot.astype(f32), d_cond, (((0,), (0,)), ((), ())), precision=highest
    )
    if fits:
        (sum_fc2,) = sum_two.result()
        sum_fc1, sum_proj = sum_mid.result()
        (sum_qkv,) = sum_last.result()
        sum_qkv = sum_qkv + line.last[0, 0]
    counter = f32(STEP)
    bias_one = 1.0 - jnp.power(f32(0.5), counter)
    bias_two = 1.0 - jnp.power(f32(0.5), counter)
    rates = learn_rates()
    updates = [
        adamw(w, g, m, v, bias_one, bias_two, rate)
        for w, g, m, v, rate in zip(
            (w_qkv, w_proj, w_fc1, w_fc2, w_ada, w_table),
            (sum_qkv, sum_proj, sum_fc1, sum_fc2, sum_ada, sum_table),
            (m_qkv, m_proj, m_fc1, m_fc2, m_ada, m_table),
            (v_qkv, v_proj, v_fc1, v_fc2, v_ada, v_table),
            rates,
        )
    ]
    return (block_out[None], grad_in[None]) + tuple(
        update[kind] for kind in range(4) for update in updates
    )


def solution(mesh):
    grid = Grid(mesh.shape["fsdp"], mesh.shape["grp"])
    items = P(AXES, None, None)
    vector = P(AXES)
    rows = P(AXES, None)
    columns = P(None, AXES)
    weights = (rows, rows, rows, rows, rows, columns)

    def run(*arrays):
        return per_device(grid, *arrays)

    return jax.shard_map(
        run,
        mesh=mesh,
        in_specs=(items, items, vector, vector) + weights * 3,
        out_specs=(items, items) + weights * 4,
        check_vma=False,
    )
```

```python
import functools

import jax
import jax.numpy as jnp
import numpy as np
from jax import lax
from jax.experimental import pallas as pl
from jax.experimental.pallas import tpu as pltpu
from jax.sharding import PartitionSpec as P

D = 1024
HEADS = 16
HEAD = 64
FF = 4096
SCALES = 10
STEP = 3
AXES = ("fsdp", "grp")

patch_sides = (1, 2, 3, 4, 5, 6, 8, 10, 13, 16)
norm_eps = 1e-06
adam_eps = 1e-08
decay = 0.05
highest = lax.Precision.HIGHEST
bf16 = jnp.bfloat16
f32 = jnp.float32


def scale_layout(slots):
    squares = np.array(patch_sides[:SCALES], dtype=np.int64) ** 2
    bounds = np.cumsum(squares)
    scale_ids = np.searchsorted(bounds, np.arange(slots), side="right")
    return (bounds.astype(np.int32), scale_ids.astype(np.int32))


def norm_rows(values):
    centre = values - jnp.mean(values, axis=-1, keepdims=True)
    spread = jnp.mean(centre * centre, axis=-1, keepdims=True)
    return centre * lax.rsqrt(spread + norm_eps)


def modulate(values, scale_row, shift_row):
    return norm_rows(values) * (1.0 + scale_row) + shift_row


def gelu_tanh(values):
    return jax.nn.gelu(values, approximate=True)


def gelu_and_slope(v):
    root = np.float32(np.sqrt(2 / np.pi))
    cube = np.float32(0.044715) * root
    square = v * v
    t = jnp.tanh(v * (root + cube * square))
    half = 0.5 + 0.5 * t
    act = v * half
    return [half + act * ((1.0 - t) * (root + (3 * cube) * square)), act]


def learn_rates():
    return (D ** (-0.5), (D // 16) ** (-0.5), D ** (-0.5), FF ** (-0.5), D ** (-0.5), 1.0)


def adamw(weight, gradient, first, second, bias_one, bias_two, rate):
    first_new = 0.5 * first + 0.5 * gradient
    second_new = 0.5 * second + 0.5 * gradient * gradient
    update = first_new / bias_one / (jnp.sqrt(second_new / bias_two) + adam_eps) + decay * weight
    weight_new = weight - rate * update
    return (weight_new, weight_new.astype(bf16), first_new, second_new)


def contract_rows(former, latter):
    return lax.dot_general(former, latter, (((0,), (0,)), ((), ())), preferred_element_type=f32)


def contract_cols(former, latter):
    return lax.dot_general(former, latter, (((1,), (1,)), ((), ())), preferred_element_type=f32)


def dot_nt(former, latter):
    return lax.dot_general(former, latter, (((1,), (1,)), ((), ())), preferred_element_type=f32)


def dot_nn(former, latter):
    return lax.dot_general(former, latter, (((1,), (0,)), ((), ())), preferred_element_type=f32)


def dot_tn(former, latter):
    return lax.dot_general(former, latter, (((0,), (0,)), ((), ())), preferred_element_type=f32)


FORWARD_TILES = ((0, 240, 256), (240, 416, 432), (416, 680, 680))
BACKWARD_TILES = ((0, 128, 160), (128, 384, 432), (384, 680, 680))


def attend_kernel(q_ref, k_ref, v_ref, bias_ref, context_ref, lse_ref):
    for begin, end, keys in FORWARD_TILES:
        q = q_ref[begin:end, :] * bf16(0.125)
        lane = lax.broadcasted_iota(jnp.int32, q.shape, 1)
        contexts, totals = [], []
        for head in range(2):
            own = jnp.where((lane < HEAD) == (head == 0), q, bf16(0))
            scores = dot_nt(own, k_ref[:keys, :]) + bias_ref[begin:end, :keys]
            largest = jnp.max(scores, axis=1, keepdims=True)
            expo = jnp.exp(scores - largest)
            total = jnp.sum(expo, axis=1, keepdims=True)
            probs = (expo * (1.0 / total)).astype(bf16)
            totals.append(largest + jnp.log(total))
            contexts.append(dot_nn(probs, v_ref[:keys, :]))
        left = lax.broadcasted_iota(jnp.int32, contexts[0].shape, 1) < HEAD
        context_ref[begin:end, :] = jnp.where(left, contexts[0], contexts[1]).astype(bf16)
        lse = jnp.where(left, totals[0], totals[1]).T
        lse_ref[0, 0:1, begin:end] = lse[0:1]
        lse_ref[0, 1:2, begin:end] = lse[HEAD : HEAD + 1]


def attend_forward(packed, bias, begin, end, so_far=None):
    slots, width = packed.shape[0], packed.shape[1] // 3
    pairs = width // 128
    assert slots == FORWARD_TILES[-1][1]

    def block(offset):
        return pl.BlockSpec((slots, 128), lambda i: (0, offset + begin + i))

    more = list(so_far) if so_far else []

    def kernel(q_ref, k_ref, v_ref, bias_ref, *refs):
        attend_kernel(q_ref, k_ref, v_ref, bias_ref, *refs[len(more) :])

    return pl.pallas_call(
        kernel,
        grid=(end - begin,),
        in_specs=[
            block(0),
            block(pairs),
            block(2 * pairs),
            pl.BlockSpec((slots, slots), lambda i: (0, 0), pipeline_mode=pl.Buffered(1)),
        ]
        + [pl.BlockSpec(memory_space=pl.ANY)] * len(more),
        out_specs=[block(0), pl.BlockSpec((1, 2, slots), lambda i: (begin + i, 0, 0))],
        out_shape=[
            jax.ShapeDtypeStruct((slots, width), bf16),
            jax.ShapeDtypeStruct((pairs, 2, slots), f32),
        ],
        input_output_aliases={4 + i: i for i in range(len(more))},
        cost_estimate=estimate(
            flops=5 * slots * slots * width,
            bytes_accessed=6 * slots * width,
            transcendentals=slots * slots * HEADS // 2,
        ),
        compiler_params=pltpu.CompilerParams(vmem_limit_bytes=20 << 20),
        name="attend",
    )(packed, packed, packed, bias, *more)


def attend_back_kernel(
    half, place_ref, q_ref, k_ref, v_ref, grad_ref, lse_ref, bias_ref, out_ref, give_ref, *refs
):
    keys_ref, values_ref, y_ref, out_sems, give_sems = refs
    step = pl.program_id(0)
    slot = lax.rem(step, 2)
    width = 2 * half * 128

    def copies(step, slot, run):
        pair = lax.rem(step + (1 - place_ref[2]) * half, 2 * half)
        for i in range(3):
            at = pl.multiple_of(i * width + pair * 128, 128)
            run(
                pltpu.make_async_copy(
                    y_ref.at[slot, i], out_ref.at[:, pl.ds(at, 128)], out_sems.at[slot, i]
                )
            )

        @pl.when(step < half)
        def _():
            for i in range(3):
                at = pl.multiple_of((i * half + step) * 128, 128)
                run(
                    pltpu.make_async_copy(
                        y_ref.at[slot, i], give_ref.at[:, pl.ds(at, 128)], give_sems.at[slot, i]
                    )
                )

    @pl.when(step >= 2)
    def _():
        copies(step - 2, slot, lambda copy: copy.wait())

    for count, (begin, end, keys) in enumerate(reversed(BACKWARD_TILES)):
        q = q_ref[begin:end, :] * bf16(0.125)
        grad = grad_ref[begin:end, :]
        k = k_ref[:keys, :]
        v = v_ref[:keys, :]
        left = lax.broadcasted_iota(jnp.int32, q.shape, 1) < HEAD
        d_q, d_k, d_v = [], [], []
        for head in range(2):
            own = left == (head == 0)
            scores = dot_nt(k, jnp.where(own, q, bf16(0))) + bias_ref[:keys, begin:end]
            probs = jnp.exp(scores - lse_ref[0, head : head + 1, begin:end])
            d_probs = dot_nt(v, jnp.where(own, grad, bf16(0)))
            inner = jnp.sum(probs * d_probs, axis=0, keepdims=True)
            d_scores = (probs * (d_probs - inner)).astype(bf16)
            d_v.append(dot_nn(probs.astype(bf16), grad))
            d_k.append(dot_nn(d_scores, q))
            d_q.append(dot_tn(d_scores, k))
        first = lax.broadcasted_iota(jnp.int32, d_k[0].shape, 1) < HEAD
        d_k = jnp.where(first, d_k[0], d_k[1])
        d_v = jnp.where(first, d_v[0], d_v[1])
        if count == 0:
            keys_ref[:keys, :] = d_k
            values_ref[:keys, :] = d_v
        else:
            keys_ref[:keys, :] += d_k
            values_ref[:keys, :] += d_v
        y_ref[slot, 0, begin:end, :] = (jnp.where(left, d_q[0], d_q[1]) * 0.125).astype(bf16)
    y_ref[slot, 1] = keys_ref[...].astype(bf16)
    y_ref[slot, 2] = values_ref[...].astype(bf16)
    copies(step, slot, lambda copy: copy.start())

    @pl.when(step == 2 * half - 1)
    def _():
        copies(step - 1, 1 - slot, lambda copy: copy.wait())
        copies(step, slot, lambda copy: copy.wait())


def attend_backward(place, packed, d_context, lse, bias_t):
    slots, width = packed.shape[0], packed.shape[1] // 3
    pairs = width // 128
    half = pairs // 2
    assert slots == BACKWARD_TILES[-1][1] and pairs >= 2

    def at(i, place):
        return lax.rem(i + (1 - place[2]) * half, pairs)

    def block(offset):
        return pl.BlockSpec((slots, 128), lambda i, place: (0, offset + at(i, place)))

    return pl.pallas_call(
        functools.partial(attend_back_kernel, half),
        grid_spec=pltpu.PrefetchScalarGridSpec(
            num_scalar_prefetch=1,
            grid=(pairs,),
            in_specs=[
                block(0),
                block(pairs),
                block(2 * pairs),
                block(0),
                pl.BlockSpec((1, 2, slots), lambda i, place: (at(i, place), 0, 0)),
                pl.BlockSpec((slots, slots), lambda i, place: (0, 0), pipeline_mode=pl.Buffered(1)),
            ],
            out_specs=[pl.BlockSpec(memory_space=pl.ANY)] * 2,
            scratch_shapes=[
                pltpu.VMEM((slots, 128), f32),
                pltpu.VMEM((slots, 128), f32),
                pltpu.VMEM((2, 3, slots, 128), bf16),
                pltpu.SemaphoreType.DMA((2, 3)),
                pltpu.SemaphoreType.DMA((2, 3)),
            ],
        ),
        out_shape=[
            jax.ShapeDtypeStruct((slots, 3 * width), bf16),
            jax.ShapeDtypeStruct((slots, 3 * width // 2), bf16),
        ],
        cost_estimate=estimate(
            flops=20 * slots * slots * width,
            bytes_accessed=16 * slots * width,
            transcendentals=slots * slots * HEADS,
        ),
        compiler_params=pltpu.CompilerParams(vmem_limit_bytes=28 << 20),
        name="attend_back",
    )(place, packed, packed, packed, d_context, lse, bias_t)


def start_pieces(place_ref, pieces, w_ref, sems, rows, left, half, color):
    z, x, c, y = [place_ref[i] for i in range(4)]
    for far in range(2):
        for core in range(2):
            piece = pieces[core * 4 + far * 2 + color]
            for near in range(2):
                step_x, step_y = (far, near) if color == 0 else (near, far)
                for step in range(4):
                    at = (z ^ FLIPS[step]) * 2 + (x ^ step_x)
                    at = (at * 2 + (c ^ core)) * 2 + (y ^ step_y)
                    at = pl.multiple_of(at * rows, rows)
                    pltpu.make_async_copy(
                        piece.at[near, step, :, pl.ds(left, half)],
                        w_ref.at[color, pl.ds(at, rows), :],
                        sems.at[color],
                    ).start()


def gather_kernel(layout, place_ref, x_ref, *refs):
    rows, left, half, chunk, gelu, keep = layout
    outs = 2 if gelu else 1
    pieces, refs = refs[:8], refs[8:]
    whole_ref, refs = (refs[0], refs[1:]) if keep else (None, refs)
    out_refs, w_ref, y_refs = refs[:outs], refs[outs], refs[outs + 1 : 2 * outs + 1]
    in_sems, whole_sems, out_sems = refs[2 * outs + 1 :]
    start = functools.partial(start_pieces, place_ref, pieces, w_ref, in_sems, rows, left, half)
    start(0)
    waits = []
    for color in range(2):
        own = w_ref.at[color]
        pltpu.make_async_copy(own, own, in_sems.at[color]).wait()
        if color == 0:
            start(1)
        if keep:
            copy = pltpu.make_async_copy(
                own, whole_ref.at[:, pl.ds(color * half, half)], whole_sems.at[color]
            )
            copy.start()
            waits.append(copy)
        for begin in range(0, half, chunk):
            at = color * half + begin
            result = dot_nn(x_ref[...], w_ref[color, :, begin : begin + chunk])
            values = gelu_and_slope(result) if gelu else [result]
            for i, value in enumerate(values):
                y_refs[i][:, at : at + chunk] = value.astype(y_refs[i].dtype)
                copy = pltpu.make_async_copy(
                    y_refs[i].at[:, pl.ds(at, chunk)],
                    out_refs[i].at[:, pl.ds(at, chunk)],
                    out_sems.at[i, at // chunk],
                )
                copy.start()
                waits.append(copy)
    for copy in waits:
        copy.wait()


def gather_dot(place, x, pieces, left, half, kinds, keep, name):
    rows = pieces[0].shape[2]
    whole, width = rows * 32, 2 * half
    slots = x.shape[0]
    chunk = min(512, half)
    anywhere = pl.BlockSpec(memory_space=pl.ANY)
    shapes = [jax.ShapeDtypeStruct((whole, width), bf16)] * keep
    shapes += [jax.ShapeDtypeStruct((slots, width), kind) for kind in kinds]
    return pl.pallas_call(
        functools.partial(gather_kernel, (rows, left, half, chunk, len(kinds) == 2, keep)),
        grid_spec=pltpu.PrefetchScalarGridSpec(
            num_scalar_prefetch=1,
            grid=(1,),
            in_specs=[pl.BlockSpec(x.shape, lambda i, place: (0, 0))] + [anywhere] * 8,
            out_specs=[anywhere] * len(shapes),
            scratch_shapes=[pltpu.VMEM((2, whole, half), bf16)]
            + [pltpu.VMEM((slots, width), kind) for kind in kinds]
            + [
                pltpu.SemaphoreType.DMA((2,)),
                pltpu.SemaphoreType.DMA((2,)),
                pltpu.SemaphoreType.DMA((len(kinds), width // chunk)),
            ],
        ),
        out_shape=shapes,
        cost_estimate=estimate(
            flops=3 * slots * whole * width,
            bytes_accessed=2 * whole * width + 4 * slots * width,
            transcendentals=0,
        ),
        compiler_params=pltpu.CompilerParams(vmem_limit_bytes=56 << 20),
        name=name,
    )(place, x, *pieces)


def modulate_back_kernel(steps, more, place_ref, x_ref, w_ref, rows_ref, *refs):
    value_hbm, add_hbm, refs = refs[0], refs[1], refs[2:]
    if more:
        attended_hbm, proj_hbm, refs = refs[0], refs[1], refs[2:]
        out_hbm, low_hbm, give_hbm, context_hbm, sums_ref, refs = *refs[:5], refs[5:]
        total_ref, value_ref, add_ref, attended_ref, proj_ref, low_ref, context_ref, sems = refs
    else:
        out_hbm, sums_ref, total_ref, value_ref, add_ref, sems = refs
    step = pl.program_id(0)
    pairs = [(value_hbm, value_ref), (add_hbm, add_ref)]
    if more:
        pairs += [(attended_hbm, attended_ref), (proj_hbm, proj_ref)]
    loads = [pltpu.make_async_copy(a, b, sems.at[i]) for i, (a, b) in enumerate(pairs)]
    part = dot_nt(x_ref[...], w_ref[...])

    @pl.when(step == 0)
    def _():
        for load in loads:
            load.start()
        total_ref[...] = part

    @pl.when(step > 0)
    def _():
        total_ref[...] += part

    @pl.when(step == steps - 1)
    def _():
        for load in loads:
            load.wait()
        slots, width = total_ref.shape
        gain = rows_ref[0:1, :]
        length = place_ref[4]

        def block(at, count, sums):
            value = value_ref[pl.ds(at, count), :].astype(f32)
            centre = value - jnp.mean(value, axis=1, keepdims=True)
            rate = lax.rsqrt(jnp.mean(centre * centre, axis=1, keepdims=True) + norm_eps)
            normal = centre * rate
            grad = total_ref[pl.ds(at, count), :]
            scaled = grad * gain
            inner = jnp.mean(scaled * normal, axis=1, keepdims=True)
            result = rate * (scaled - jnp.mean(scaled, axis=1, keepdims=True) - normal * inner)
            add = add_ref[pl.ds(at, count), :].astype(f32)
            sums = [
                sums[0] + jnp.sum(grad * normal, axis=0, keepdims=True),
                sums[1] + jnp.sum(grad, axis=0, keepdims=True),
            ] + sums[2:]
            if more:
                slot = at + lax.broadcasted_iota(jnp.int32, (count, 1), 0)
                add = add * (slot < length).astype(f32)
            result = add + result
            total_ref[pl.ds(at, count), :] = result
            if more:
                attended = attended_ref[pl.ds(at, count), :]
                sums[2] = sums[2] + jnp.sum(result * attended, axis=0, keepdims=True)
                low_ref[pl.ds(at, count), :] = (result * rows_ref[1:2, :]).astype(bf16)
            return sums

        count = 32
        whole = slots // count
        sums = [jnp.zeros((1, width), f32) for _ in range(3 if more else 2)]
        sums = lax.fori_loop(
            0, whole, lambda i, sums: block(pl.multiple_of(i * count, count), count, sums), sums
        )
        if slots % count:
            sums = block(whole * count, slots % count, sums)
        sums_ref[...] = jnp.concatenate(
            sums + [jnp.zeros((8 - len(sums), width), f32)], axis=0
        )
        stores = [pltpu.make_async_copy(total_ref, out_hbm, sems.at[4])]
        if more:
            half = width // 2
            other = pl.multiple_of((1 - place_ref[2]) * half, half)
            stores += [
                pltpu.make_async_copy(low_ref.at[:, pl.ds(other, half)], give_hbm, sems.at[5]),
                pltpu.make_async_copy(low_ref, low_hbm, sems.at[6]),
            ]
        for store in stores:
            store.start()
        if more:
            context_ref[...] = dot_nt(low_ref[...], proj_ref[...]).astype(bf16)
            stores.append(pltpu.make_async_copy(context_ref, context_hbm, sems.at[7]))
            stores[-1].start()
        for store in stores:
            store.wait()


def modulate_back(place, x, weight, rows, value, add, attended=None, proj=None):
    more = proj is not None
    slots, depth = x.shape
    width = weight.shape[0]
    chunk = 1024
    assert depth % chunk == 0
    anywhere = pl.BlockSpec(memory_space=pl.ANY)
    operands = [value, add] + ([attended, proj] if more else [])
    shapes = [jax.ShapeDtypeStruct((slots, width), f32)]
    scratch = [
        pltpu.VMEM((slots, width), f32),
        pltpu.VMEM((slots, width), value.dtype),
        pltpu.VMEM((slots, width), add.dtype),
    ]
    if more:
        shapes += [
            jax.ShapeDtypeStruct((slots, width), bf16),
            jax.ShapeDtypeStruct((slots, width // 2), bf16),
            jax.ShapeDtypeStruct((slots, width), bf16),
        ]
        scratch += [
            pltpu.VMEM((slots, width), f32),
            pltpu.VMEM(proj.shape, bf16),
            pltpu.VMEM((slots, width), bf16),
            pltpu.VMEM((slots, width), bf16),
        ]
    return pl.pallas_call(
        functools.partial(modulate_back_kernel, depth // chunk, more),
        grid_spec=pltpu.PrefetchScalarGridSpec(
            num_scalar_prefetch=1,
            grid=(depth // chunk,),
            in_specs=[
                pl.BlockSpec((slots, chunk), lambda i, place: (0, i)),
                pl.BlockSpec((width, chunk), lambda i, place: (0, i)),
                pl.BlockSpec((8, width), lambda i, place: (0, 0)),
            ]
            + [anywhere] * len(operands),
            out_specs=[anywhere] * len(shapes)
            + [pl.BlockSpec((8, width), lambda i, place: (0, 0))],
            scratch_shapes=scratch + [pltpu.SemaphoreType.DMA((8,))],
        ),
        out_shape=shapes + [jax.ShapeDtypeStruct((8, width), f32)],
        cost_estimate=estimate(
            flops=3 * slots * width * (depth + width * more),
            bytes_accessed=2 * (slots + width) * depth + 16 * slots * width,
            transcendentals=0,
        ),
        compiler_params=pltpu.CompilerParams(vmem_limit_bytes=48 << 20),
        name="modulate_back",
    )(place, x, weight, rows, *operands)


def gelu_back_kernel(rows, place_ref, grad_ref, slope_ref, *refs):
    pieces, (out_ref, give_ref), refs = refs[:8], refs[8:10], refs[10:]
    w_ref, s_ref, y_ref, in_sems, s_sems, y_sems, give_sems = refs
    z, x, c, y = [place_ref[i] for i in range(4)]
    block = 4 * rows
    chunks = [(step, far_x) for step in range(4) for far_x in range(2)]
    where = [
        pl.multiple_of(((z ^ FLIPS[step]) * 2 + (x ^ far_x)) * block, block) for step, far_x in chunks
    ]
    half = pieces[0].shape[-1]

    def start(n):
        step, far_x = chunks[n]
        for core in range(2):
            for far_y in range(2):
                at = pl.multiple_of(((c ^ core) * 2 + (y ^ far_y)) * rows, rows)
                for color in range(2):
                    far, near = (far_x, far_y) if color == 0 else (far_y, far_x)
                    pltpu.make_async_copy(
                        pieces[core * 4 + far * 2 + color].at[near, step],
                        w_ref.at[n, pl.ds(at, rows), pl.ds(color * half, half)],
                        in_sems.at[n],
                    ).start()
        pltpu.make_async_copy(
            slope_ref.at[:, pl.ds(where[n], block)], s_ref.at[n], s_sems.at[n]
        ).start()

    ahead = 2
    for n in range(ahead):
        start(n)
    waits = []
    for n in range(len(chunks)):
        pltpu.make_async_copy(w_ref.at[n], w_ref.at[n], in_sems.at[n]).wait()
        pltpu.make_async_copy(s_ref.at[n], s_ref.at[n], s_sems.at[n]).wait()
        if n + ahead < len(chunks):
            start(n + ahead)
        y_ref[n] = (dot_nt(grad_ref[...], w_ref[n]) * s_ref[n].astype(f32)).astype(bf16)
        copy = pltpu.make_async_copy(
            y_ref.at[n], out_ref.at[:, pl.ds(where[n], block)], y_sems.at[n]
        )
        copy.start()
        waits.append(copy)
    for n, (step, far_x) in enumerate(chunks):
        other = lax.shift_right_logical(z ^ FLIPS[step], 1) != c

        @pl.when(other)
        def _(n=n):
            at = pl.multiple_of(where[n] - (1 - c) * (4 * block), block)
            copy = pltpu.make_async_copy(
                y_ref.at[n], give_ref.at[:, pl.ds(at, block)], give_sems.at[n]
            )
            copy.start()
            copy.wait()

    for copy in waits:
        copy.wait()


def gelu_back_dot(place, grad, slope, pieces):
    slots, width = slope.shape
    rows = pieces[0].shape[2]
    assert width == 32 * rows and grad.shape[1] == 2 * pieces[0].shape[3]
    anywhere = pl.BlockSpec(memory_space=pl.ANY)
    block = 4 * rows
    return pl.pallas_call(
        functools.partial(gelu_back_kernel, rows),
        grid_spec=pltpu.PrefetchScalarGridSpec(
            num_scalar_prefetch=1,
            grid=(1,),
            in_specs=[pl.BlockSpec(grad.shape, lambda i, place: (0, 0))] + [anywhere] * 9,
            out_specs=[anywhere] * 2,
            scratch_shapes=[
                pltpu.VMEM((8, block, grad.shape[1]), bf16),
                pltpu.VMEM((8, slots, block), slope.dtype),
                pltpu.VMEM((8, slots, block), bf16),
            ]
            + [pltpu.SemaphoreType.DMA((8,))] * 4,
        ),
        out_shape=[
            jax.ShapeDtypeStruct((slots, width), bf16),
            jax.ShapeDtypeStruct((slots, width // 2), bf16),
        ],
        cost_estimate=estimate(
            flops=3 * slots * width * grad.shape[1],
            bytes_accessed=8 * slots * width + 4 * width * grad.shape[1],
            transcendentals=0,
        ),
        compiler_params=pltpu.CompilerParams(vmem_limit_bytes=56 << 20),
        name="gelu_back",
    )(place, grad, slope, *pieces)


def weight_grad_kernel(depth, rows, turn, firsts, place_ref, *refs):
    products = len(firsts)
    ins, out_refs = refs[: 4 * products], refs[4 * products :]
    step = pl.program_id(0)
    inner = lax.rem(step, turn)

    def product(own_ref, other_ref, mine_ref, take_ref):
        total = dot_tn(own_ref[...], mine_ref[...]) + dot_tn(other_ref[...], take_ref[...])
        total = total.reshape(depth, 2, 2, 2, rows, total.shape[-1])

        @pl.when(step < turn)
        def _():
            first = place_ref[3] == 0
            for x in range(2):
                low, high = total[:, x, :, 0], total[:, x, :, 1]
                out_refs[0][x] = jnp.where(first, high, low).astype(bf16)
                out_refs[1][x] = jnp.where(first, low, high).astype(bf16)

        @pl.when(step >= turn)
        def _():
            first = place_ref[1] == 0
            for y in range(2):
                low, high = total[:, 0, :, y], total[:, 1, :, y]
                out_refs[2][y] = jnp.where(first, high, low).astype(bf16)
                out_refs[3][y] = jnp.where(first, low, high).astype(bf16)

    if products == 1:
        product(*ins)
        return
    for n, (begin, end) in enumerate(firsts):

        @pl.when((inner >= begin) & (inner < end))
        def _(n=n):
            product(*ins[4 * n : 4 * n + 4])


def weight_grad_call(place, products, rows, chunk):
    specs, operands, firsts = [], [], []
    turn = flops = 0
    for own, other, rhs, take, groups in products:
        slots, columns = rhs.shape[0], rhs.shape[1] // groups
        per = columns // 2 // chunk
        count = groups * per // 2
        assert groups * per % 2 == 0 and columns % (2 * chunk) == 0
        flops += 6 * slots * own.shape[1] * groups * columns // 2
        firsts.append((turn, turn + count))
        specs.append((per, count, turn))
        turn += count
        operands += [own, other, rhs, take]
    in_specs = []
    for (own, *_), (per, count, begin) in zip(products, specs):
        slots = own.shape[0]

        def which(i, count=count, begin=begin):
            color = i // turn
            return color * count + jnp.clip(i - color * turn - begin, 0, count - 1)

        once = pl.Buffered(1)
        in_specs += [pl.BlockSpec(own.shape, lambda i, place: (0, 0), pipeline_mode=once)] * 2
        in_specs.append(
            pl.BlockSpec(
                (slots, chunk),
                lambda i, place, which=which, per=per: (
                    0,
                    (which(i) // per * 2 + place[2]) * per + lax.rem(which(i), per),
                ),
            )
        )
        in_specs.append(
            pl.BlockSpec((slots, chunk), lambda i, place, which=which: (0, which(i)))
        )
    width = products[0][0].shape[1]
    depth = width // rows // 8
    block = (2, depth, 2, rows, chunk)
    early = pl.BlockSpec(block, lambda i, place: (0, 0, 0, 0, jnp.minimum(i, turn - 1)))
    late = pl.BlockSpec(block, lambda i, place: (0, 0, 0, 0, jnp.maximum(i - turn, 0)))
    shape = jax.ShapeDtypeStruct((2, depth, 2, rows, turn * chunk), bf16)
    return pl.pallas_call(
        functools.partial(weight_grad_kernel, depth, rows, turn, tuple(firsts)),
        grid_spec=pltpu.PrefetchScalarGridSpec(
            num_scalar_prefetch=1,
            grid=(2 * turn,),
            in_specs=in_specs,
            out_specs=[early, early, late, late],
        ),
        out_shape=[shape] * 4,
        cost_estimate=estimate(
            flops=flops,
            bytes_accessed=sum(2 * v.size for v in operands) + 4 * width * turn * chunk,
            transcendentals=0,
        ),
        compiler_params=pltpu.CompilerParams(vmem_limit_bytes=60 << 20),
        name="weight_grad",
    )(place, *operands)


def estimate(flops, bytes_accessed, transcendentals):
    return pl.CostEstimate(
        flops=flops // 64, bytes_accessed=bytes_accessed // 64, transcendentals=transcendentals // 64
    )


class Line:
    def __init__(self):
        self.last = jnp.zeros((8, 128), f32)

    def __call__(self, *values):
        self.last, values = lax.optimization_barrier((self.last, values))
        return values[0] if len(values) == 1 else values

    def arrive(self, movers, *values):
        gots, values = self([mover.got for mover in movers], values)
        for mover, got in zip(movers, gots):
            mover.got = got
        return values[0] if len(values) == 1 else values


class Scatter:
    def __init__(self, grid, line, rows):
        self.grid, self.line, self.flips = grid, line, grid.bits()
        self.rows = rows.reshape([2] * len(self.flips) + list(rows.shape[1:]))

    def start(self):
        dim = len(self.flips) - 1
        axis, bit = self.flips.pop(0)
        self.own = lax.index_in_dim(self.rows, 0, dim, keepdims=False)
        away = self.line(lax.index_in_dim(self.rows, 1, dim, keepdims=False))
        self.got = self.grid.flip(away, axis, bit)

    def add(self):
        self.rows = self.own + self.got


class Gather:
    orders = ("yx", "xy")

    def __init__(self, grid, line, shards):
        self.grid, self.line = grid, line
        lows = [shard[:, : shard.shape[1] // 2] for shard in shards]
        highs = [shard[:, shard.shape[1] // 2 :] for shard in shards]
        self.shard = jnp.concatenate(lows + highs, axis=1)

    def first(self):
        self.shard = self.line(self.shard)
        self.got = self.grid.flip(self.shard, "z", 2)

    def second(self):
        self.pair = self.line(jnp.stack([self.shard, self.got]))
        self.got = self.grid.flip(self.pair, "z", 1)

    def third(self):
        half = self.shard.shape[1] // 2
        pairs = (self.pair, self.got)
        rows = [
            jnp.concatenate([p[:, :, i * half : (i + 1) * half] for p in pairs], axis=0)
            for i in range(2)
        ]
        self.rows = self.line(*rows)
        self.got = [self.grid.flip(v, o[0], 1) for v, o in zip(self.rows, self.orders)]

    def fourth(self):
        plane = [
            jnp.concatenate([own[None], new[None]], axis=0) for own, new in zip(self.rows, self.got)
        ]
        self.plane = self.line(*plane)
        self.got = [self.grid.flip(v, o[1], 1) for v, o in zip(self.plane, self.orders)]

    def pieces(self):
        mine = list(self.plane) + list(self.got)
        return mine + [self.grid.flip(v, "c", 1) for v in mine]


FLIPS = (0, 2, 1, 3)


def add_split_kernel(joined, place_ref, *refs):
    sums = len(refs) // (5 if joined else 6)
    outs = refs[4 * sums :]
    for n in range(sums):
        for side in range(2):
            one, two = refs[4 * n + 2 * side], refs[4 * n + 2 * side + 1]
            out = outs[side] if joined else outs[2 * n + side]
            total = one[...].astype(f32) + two[...].astype(f32)
            if joined:
                width = total.shape[-1]
                out[..., n * width : (n + 1) * width] = total.astype(out.dtype)
            else:
                out[...] = total.reshape(out.shape).astype(out.dtype)


def add_split(place, name, steps, specs, *pairs, joined=False, kind=bf16):
    in_specs, operands, out_specs, shapes = [], [], [], []
    for n, pair in enumerate(pairs):
        lead = pair[0].ndim - 3
        if pair[0].ndim == 3:
            lead = 1
        tail = pair[0].shape[lead:]
        for side in range(2):
            for array in pair:
                in_specs.append(
                    pl.BlockSpec(
                        (1,) * lead + tail,
                        lambda i, place, n=n, side=side, zeros=(0,) * len(tail): (
                            specs(i, place)[n][side] + zeros
                        ),
                    )
                )
                operands.append(array)
            if joined and n:
                continue
            wide = tail[:-1] + (tail[-1] * (len(pairs) if joined else 1),)
            out_specs.append(
                pl.BlockSpec(
                    (1,) + wide, lambda i, place, zeros=(0,) * len(wide): (i,) + zeros
                )
            )
            shapes.append(jax.ShapeDtypeStruct((steps,) + wide, kind))
    return pl.pallas_call(
        functools.partial(add_split_kernel, joined),
        grid_spec=pltpu.PrefetchScalarGridSpec(
            num_scalar_prefetch=1, grid=(steps,), in_specs=in_specs, out_specs=out_specs
        ),
        out_shape=shapes,
        cost_estimate=estimate(
            flops=sum(array.size for array in operands),
            bytes_accessed=4 * sum(array.size for array in operands),
            transcendentals=0,
        ),
        compiler_params=pltpu.CompilerParams(vmem_limit_bytes=24 << 20),
        name=name,
    )(place, *operands)


class GradSum:
    def __init__(self, grid, line, here, place, products, rows, chunk, movers=()):
        self.grid, self.line, self.here, self.place, self.rows = grid, line, here, place, rows
        self.shapes = [(groups, rhs.shape[1] // groups) for _, _, rhs, _, groups in products]
        away_one, self.one, away_two, self.two = line.arrive(
            movers, *weight_grad_call(place, products, rows, chunk)
        )
        self.got = [grid.flip(away_one, "y", 1), grid.flip(away_two, "x", 1)]

    def second(self):
        away_one, self.one, away_two, self.two = self.line(
            *add_split(self.place, "add_second", 4, self.second_specs, *self.parts())
        )
        self.got = [self.grid.flip(away_one, "x", 1), self.grid.flip(away_two, "y", 1)]

    def parts(self):
        return [(self.one, self.got[0]), (self.two, self.got[1])]

    def second_specs(self, i, place):
        x, y = place[1], place[3]
        return [((1 - x, i), (x, i)), ((1 - y, i), (y, i))]

    def third(self):
        def specs(i, place):
            low = lax.rem(place[0], 2)
            pair = ((2 * i + 1 - low,), (2 * i + low,))
            return [pair, pair]

        away, self.both = self.line(
            *add_split(self.place, "add_third", 2, specs, *self.parts(), joined=True)
        )
        self.got = self.grid.flip(away, "z", 1)

    def fourth(self):
        def specs(i, place):
            high = place[0] // 2
            return [((1 - high,), (high,))]

        away, self.both = self.line(
            *add_split(self.place, "add_fourth", 1, specs, (self.both, self.got))
        )
        away, self.both = away[0], self.both[0]
        self.got = self.grid.flip(away, "z", 2)

    def fifth(self):
        def specs(i, place):
            return [((1 - place[2],), (place[2],))]

        give, self.keep = self.line(
            *add_split(self.place, "add_fifth", 1, specs, (self.both, self.got), kind=f32)
        )
        give, self.keep = give[0], self.keep[0]
        self.take = self.grid.flip(give, "c", 1)

    def result(self):
        first = self.here["c"] == 0
        low = jnp.where(first, self.keep, self.take)
        high = jnp.where(first, self.take, self.keep)
        sums, left, middle = [], 0, low.shape[1] // 2
        for groups, columns in self.shapes:
            part = groups * columns // 4
            half = columns // 2
            sides = []
            for side in (low, high):
                colors = [side[:, left : left + part], side[:, middle + left : middle + left + part]]
                sides.append(jnp.concatenate(colors, axis=1))
            spans = [side[:, g * half : (g + 1) * half] for g in range(groups) for side in sides]
            sums.append(jnp.concatenate(spans, axis=1))
            left += part
        return sums


class Grid:
    def __init__(self, fsdp, grp):
        outer = fsdp // 2
        self.size = {"c": 2, "x": 2 if outer % 2 == 0 else 1, "y": grp}
        self.size["z"] = outer // self.size["x"]
        self.count = fsdp * grp
        self.fsdp = fsdp

    def here(self):
        place = lax.axis_index("fsdp")
        wide = self.size["x"]
        return {
            "c": place % 2,
            "x": (place // 2) % wide,
            "z": place // (2 * wide),
            "y": lax.axis_index("grp"),
        }

    def shift(self, array, axis, step):
        size = self.size[axis]
        if axis == "y":
            return lax.ppermute(array, "grp", [(i, (i + step) % size) for i in range(size)])
        stride = {"c": 1, "x": 2, "z": 2 * self.size["x"]}[axis]
        pairs = []
        for i in range(self.fsdp):
            at = (i // stride) % size
            pairs.append((i, i + ((at + step) % size - at) * stride))
        return lax.ppermute(array, "fsdp", pairs)

    def fits(self, rows):
        size = self.size
        return size["x"] == 2 and size["y"] == 2 and size["z"] == 4 and rows % 32 == 0

    def bits(self):
        flips = []
        for axis in "cxyz":
            size = self.size[axis]
            assert size & (size - 1) == 0
            bit = size // 2
            while bit:
                flips.append((axis, bit))
                bit //= 2
        return flips

    def gather_all(self, row, flips):
        for axis, bit in flips:
            row = jnp.concatenate([row[None], self.flip(row, axis, bit)[None]], axis=0)
        return row

    def sources(self, here):
        flips = self.bits()
        turn = {axis: np.zeros(self.count, np.int32) for axis in "cxyz"}
        for n in range(self.count):
            for k, (axis, bit) in enumerate(flips):
                if n >> k & 1:
                    turn[axis][n] ^= bit
        z, x, c, y = [here[axis] ^ turn[axis] for axis in "zxcy"]
        return ((z * self.size["x"] + x) * 2 + c) * self.size["y"] + y

    def flip(self, array, axis, bit):
        size = self.size[axis]
        if axis == "y":
            return lax.ppermute(array, "grp", [(i, i ^ bit) for i in range(size)])
        stride = {"c": 1, "x": 2, "z": 2 * self.size["x"]}[axis]
        pairs = [
            (i, i + (((i // stride) % size ^ bit) - (i // stride) % size) * stride)
            for i in range(self.fsdp)
        ]
        return lax.ppermute(array, "fsdp", pairs)

    def scatter_sum(self, array, axis, dim, here, kind=bf16):
        size = self.size[axis]
        total = lax.dynamic_index_in_dim(array, here[axis], dim, keepdims=False)
        for step in range(1, size):
            piece = lax.dynamic_index_in_dim(array, (here[axis] + step) % size, dim, keepdims=False)
            total = total + self.shift(piece.astype(kind), axis, step).astype(f32)
        return total


def per_device(
    grid,
    block_in,
    cotangent,
    stop_scale,
    class_label,
    w_qkv,
    w_proj,
    w_fc1,
    w_fc2,
    w_ada,
    w_table,
    m_qkv,
    m_proj,
    m_fc1,
    m_fc2,
    m_ada,
    m_table,
    v_qkv,
    v_proj,
    v_fc1,
    v_fc2,
    v_ada,
    v_table,
):
    items, slots, width = block_in.shape
    assert items == 1
    here = grid.here()
    bounds, scale_ids = scale_layout(slots)
    picked = jnp.arange(SCALES) == stop_scale[0] - 1
    length = jnp.sum(jnp.where(picked, jnp.asarray(bounds), 0))
    position = jnp.arange(slots)
    valid = (position < length).astype(f32)[:, None]
    scale_table = jnp.asarray(scale_ids)
    allowed = (scale_table[None, :] <= scale_table[:, None]) & (position[None, :] < length)
    bias = jnp.where(allowed, f32(0), f32(-1e30))
    bias_t = bias.T
    place = jnp.stack([here[axis] for axis in "zxcy"] + [length]).astype(jnp.int32)
    fits = grid.fits(w_qkv.shape[0])
    cast_qkv, cast_proj, cast_fc1, cast_fc2 = [
        w.astype(bf16) for w in (w_qkv, w_proj, w_fc1, w_fc2)
    ]
    half_qkv, half_proj, half_fc1 = [w.shape[1] // 2 for w in (w_qkv, w_proj, w_fc1)]
    line = Line()
    if fits:
        place = line(place)
        all_qkv = Gather(grid, line, [cast_qkv])
        all_qkv.first()
    labels = lax.all_to_all(
        jnp.broadcast_to(class_label, (grid.count,)), AXES, 0, 0, tiled=True
    )
    labels = jnp.take(labels, grid.sources(here))
    cast_ada = w_ada.astype(bf16)
    cast_table = w_table.astype(bf16)
    onehot = (labels[:, None] == jnp.arange(cast_table.shape[0])[None, :]).astype(bf16)
    cond = jnp.dot(onehot, cast_table, preferred_element_type=f32)
    silu_out, silu_back = jax.vjp(jax.nn.silu, cond)
    lifted_low = silu_out.astype(bf16)

    ada = jnp.dot(lifted_low, cast_ada, preferred_element_type=f32)
    flips = grid.bits()
    along = len(flips) - 2
    ada = Scatter(grid, line, ada.reshape(grid.count, -1, 128))
    if fits:
        ada.start()
        line.arrive([ada, all_qkv])
        ada.add()
        all_qkv.second()
        ada.start()
        line.arrive([ada])
        ada.add()
        line.arrive([all_qkv])
        all_qkv.third()
        all_rest = Gather(grid, line, [cast_proj, cast_fc1])
        all_rest.first()
        ada.start()
        line.arrive([ada])
        ada.add()
        line.arrive([all_qkv])
        all_qkv.fourth()
        ada.start()
        line.arrive([ada, all_rest])
        ada.add()
        ada.start()
        all_rest.second()
        line.arrive([ada])
        ada.add()
    else:
        while ada.flips:
            ada.start()
            ada.add()
    ada = ada.rows.reshape(1, 6 * width)
    gamma_one, scale_one, shift_one, gamma_two, scale_two, shift_two = [
        ada[:, i * width : (i + 1) * width] for i in range(6)
    ]

    def half_columns(rhs, core, groups=1):
        half = rhs.shape[1] // groups // 2
        parts = [
            lax.dynamic_slice_in_dim(rhs, (2 * i + core) * half, half, 1) for i in range(groups)
        ]
        return jnp.concatenate(parts, axis=1)

    def weight_grad(lhs, other_lhs, rhs, take, groups):
        half = take.shape[1]
        size = grid.size
        rows = lhs.shape[1] // grid.count
        mine = half_columns(rhs, here["c"], groups)
        both = jnp.concatenate([mine, take], axis=0)
        grad = contract_rows(jnp.concatenate([lhs, other_lhs], axis=0), both)
        grad = grad.reshape(size["z"], size["x"], 2, size["y"], rows, half)
        middle = half // 2
        one = grid.scatter_sum(grad[..., :middle], "y", 3, here)
        two = grid.scatter_sum(grad[..., middle:], "x", 1, here)
        one = grid.scatter_sum(one, "x", 1, here)
        two = grid.scatter_sum(two, "y", 2, here)
        both = grid.scatter_sum(jnp.concatenate([one, two], axis=-1), "z", 0, here)
        keep = lax.dynamic_index_in_dim(both, here["c"], 0, keepdims=False)
        give = lax.dynamic_index_in_dim(both, 1 - here["c"], 0, keepdims=False)
        take = grid.shift(give, "c", 1)
        low = jnp.where(here["c"] == 0, keep, take).reshape(rows, groups, 1, half // groups)
        high = jnp.where(here["c"] == 0, take, keep).reshape(rows, groups, 1, half // groups)
        return jnp.concatenate([low, high], axis=2).reshape(rows, 2 * half)

    tokens = block_in[0].astype(f32)
    hidden, modulate_one = jax.vjp(modulate, tokens, scale_one, shift_one)
    hidden_low = hidden.astype(bf16)
    hidden_other = grid.shift(hidden_low, "c", 1)
    if fits:
        hidden_low = line.arrive([all_qkv, all_rest], hidden_low)
        pieces_qkv = all_qkv.pieces()
        all_rest.third()
        hidden_low, pieces_qkv[4:] = line(hidden_low, pieces_qkv[4:])
        wide_qkv, packed = gather_dot(
            place, hidden_low, pieces_qkv, 0, half_qkv, [bf16], True, "gather_qkv"
        )
        packed, hidden_other = line.arrive([all_rest], packed, hidden_other)
        all_rest.fourth()
        all_fc2 = Gather(grid, line, [cast_fc2])
        all_fc2.first()
        packed = line(packed)
    else:
        wide_qkv = lax.all_gather(cast_qkv, AXES, axis=0, tiled=True)
        packed = jnp.dot(hidden_low, wide_qkv, preferred_element_type=f32).astype(bf16)
    pairs = width // 128
    heads = attend_forward(packed, bias, 0, pairs // 2)
    if fits:
        heads = line.arrive([all_fc2], *heads)
        all_fc2.second()
    packed = line(packed)
    heads = attend_forward(packed, bias, pairs // 2, pairs, heads)
    if fits:
        heads = line.arrive([all_rest, all_fc2], *heads)
        pieces_rest = all_rest.pieces()
        all_fc2.third()
    context, lse = heads
    if fits:
        context, pieces_rest[4:] = line(context, pieces_rest[4:])
        context_other = grid.shift(context, "c", 1)
        wide_proj, attended = gather_dot(
            place, context, pieces_rest, 0, half_proj, [f32], True, "gather_proj"
        )
    else:
        context_other = grid.shift(context, "c", 1)
        wide_proj = lax.all_gather(cast_proj, AXES, axis=0, tiled=True)
        attended = jnp.dot(context, wide_proj, preferred_element_type=f32)
    if fits:
        attended, gradient = line(attended, cotangent[0])
        upstream = gradient.astype(f32) * valid
        d_branch = (upstream * gamma_two).astype(bf16)
        give = half_columns(d_branch, 1 - here["c"])
        attended, context_other, d_branch, give = line.arrive(
            [all_fc2], attended, context_other, d_branch, give
        )
        all_fc2.fourth()
        attended = line(attended)
    middle = tokens + gamma_one * attended
    second, modulate_two = jax.vjp(modulate, middle, scale_two, shift_two)
    if not fits:
        upstream = cotangent[0].astype(f32) * valid
        d_branch = (upstream * gamma_two).astype(bf16)
        give = half_columns(d_branch, 1 - here["c"])
    second_low = line(second.astype(bf16))
    second_other = grid.shift(second_low, "c", 1)
    take = grid.shift(give, "c", 1)
    if fits:
        wide_fc1, slope, activated_low = gather_dot(
            place, second_low, pieces_rest, half_proj, half_fc1, [bf16, bf16], True, "gather_fc1"
        )
        slope, activated_low, second_other, take = line.arrive(
            [all_fc2], slope, activated_low, second_other, take
        )
        pieces_fc2 = all_fc2.pieces()
        pieces_fc2[4:] = line(pieces_fc2[4:])
    else:
        wide_fc1 = lax.all_gather(cast_fc1, AXES, axis=0, tiled=True)
        inner = jnp.dot(second_low, wide_fc1, preferred_element_type=f32)
        slope, activated = gelu_and_slope(inner)
        activated_low = activated.astype(bf16)
    activated_low = line(activated_low)
    activated_other = grid.shift(activated_low, "c", 1)
    if fits:
        rows_in, rows_out = w_qkv.shape[0], w_fc2.shape[0]
        d_branch = line(d_branch)
        d_inner_low, give, activated_other = line(
            *gelu_back_dot(place, d_branch, slope, pieces_fc2), activated_other
        )
        pair_fc2 = (activated_low, activated_other, d_branch, take, 1)
        sum_two = GradSum(grid, line, here, place, [pair_fc2], rows_out, 256)
    else:
        wide_fc2 = lax.all_gather(cast_fc2, AXES, axis=0, tiled=True)
        sum_fc2 = weight_grad(activated_low, activated_other, d_branch, take, 1)
        d_inner_low = (contract_cols(d_branch, wide_fc2) * slope).astype(bf16)
        give = half_columns(d_inner_low, 1 - here["c"])
    take_inner = grid.shift(give, "c", 1)
    d_inner_low = line(d_inner_low)
    if fits:
        rows = [1.0 + scale_two, gamma_one, jnp.zeros((6, width), f32)]
        d_middle, d_attended, give, d_context, sums = line(
            *modulate_back(
                place,
                d_inner_low,
                wide_fc1,
                jnp.concatenate(rows, axis=0),
                middle,
                cotangent[0],
                attended,
                wide_proj,
            )
        )
        d_scale_two, d_shift_two, d_gamma_one = sums[0:1], sums[1:2], sums[2:3]
    else:
        d_second = contract_cols(d_inner_low, wide_fc1)
        d_middle_part, d_scale_two, d_shift_two = modulate_two(d_second)
        d_middle = upstream + d_middle_part
        d_gamma_one = jnp.sum(d_middle * attended, axis=0, keepdims=True)
        d_attended = (d_middle * gamma_one).astype(bf16)
        give = half_columns(d_attended, 1 - here["c"])
        d_context = contract_cols(d_attended, wide_proj).astype(bf16)
    take = grid.shift(give, "c", 1)
    if fits:
        take, take_inner = line.arrive([sum_two], take, take_inner)
        sum_two.second()
    pair_fc1 = (second_low, second_other, d_inner_low, take_inner, 1)
    pair_proj = (context, context_other, d_attended, take, 1)
    if fits:
        sum_mid = GradSum(
            grid, line, here, place, [pair_fc1, pair_proj], rows_in, 256, [sum_two]
        )
        sum_two.third()
    else:
        sum_fc1, sum_proj = weight_grad(*pair_fc1), weight_grad(*pair_proj)
    d_context = line(d_context)
    d_packed, give = attend_backward(place, packed, d_context, lse, bias_t)
    if fits:
        d_packed, give = line.arrive([sum_two, sum_mid], d_packed, give)
    take = grid.shift(give, "c", 1)
    if fits:
        sum_mid.second()
        sum_two.fourth()
        take = line(take)
        pair_qkv = (hidden_low, hidden_other, d_packed, take, 3)
        sum_last = GradSum(
            grid, line, here, place, [pair_qkv], rows_in, 256, [sum_two, sum_mid]
        )
        sum_mid.third()
        sum_two.fifth()
    else:
        sum_qkv = weight_grad(hidden_low, hidden_other, d_packed, take, 3)
    d_packed = line(d_packed)
    if fits:
        rows = [1.0 + scale_one, jnp.zeros((7, width), f32)]
        grad_in, sums = line(
            *modulate_back(
                place, d_packed, wide_qkv, jnp.concatenate(rows, axis=0), block_in[0], d_middle
            )
        )
        d_scale_one, d_shift_one = sums[0:1], sums[1:2]
    else:
        d_hidden = contract_cols(d_packed, wide_qkv)
        d_tokens, d_scale_one, d_shift_one = modulate_one(d_hidden)
        grad_in = d_middle + d_tokens
    if fits:
        line.arrive([sum_last, sum_mid])
        sum_last.second()
        sum_mid.fourth()
        activated_low = line(activated_low)
        (branch,) = gather_dot(
            place, activated_low, pieces_fc2, 0, width // 2, [f32], False, "gather_fc2"
        )
        branch = line.arrive([sum_last, sum_mid], branch)
        sum_last.third()
        sum_mid.fifth()
        branch = line(branch)
    else:
        branch = jnp.dot(activated_low, wide_fc2, preferred_element_type=f32)
    block_out = ((middle + gamma_two * branch) * valid).astype(bf16)
    d_gamma_two = jnp.sum(upstream * branch, axis=0, keepdims=True)
    d_ada = jnp.concatenate(
        [d_gamma_one, d_scale_one, d_shift_one, d_gamma_two, d_scale_two, d_shift_two], axis=0
    ).astype(bf16)
    every_ada = grid.gather_all(line(d_ada.reshape(-1, 128)), flips[:1])
    if fits:
        every_ada = line.arrive([sum_last], every_ada)
        sum_last.fourth()
        for done in (sum_two, sum_mid):
            done.take, done.keep = line(done.take, done.keep)
    every_ada = grid.gather_all(every_ada, flips[1:2])
    if fits:
        every_ada = line.arrive([sum_last], every_ada)
        sum_last.fifth()
    every_ada = grid.gather_all(every_ada, flips[2:])
    every_ada = every_ada.reshape(grid.count, 6 * width)
    sum_ada = contract_rows(lifted_low, every_ada)
    (d_cond,) = silu_back(contract_cols(every_ada, cast_ada))
    sum_table = lax.dot_general(
        onehot.astype(f32), d_cond, (((0,), (0,)), ((), ())), precision=highest
    )
    if fits:
        (sum_fc2,) = sum_two.result()
        sum_fc1, sum_proj = sum_mid.result()
        (sum_qkv,) = sum_last.result()
        sum_qkv = sum_qkv + line.last[0, 0]
    counter = f32(STEP)
    bias_one = 1.0 - jnp.power(f32(0.5), counter)
    bias_two = 1.0 - jnp.power(f32(0.5), counter)
    rates = learn_rates()
    updates = [
        adamw(w, g, m, v, bias_one, bias_two, rate)
        for w, g, m, v, rate in zip(
            (w_qkv, w_proj, w_fc1, w_fc2, w_ada, w_table),
            (sum_qkv, sum_proj, sum_fc1, sum_fc2, sum_ada, sum_table),
            (m_qkv, m_proj, m_fc1, m_fc2, m_ada, m_table),
            (v_qkv, v_proj, v_fc1, v_fc2, v_ada, v_table),
            rates,
        )
    ]
    return (block_out[None], grad_in[None]) + tuple(
        update[kind] for kind in range(4) for update in updates
    )


def solution(mesh):
    grid = Grid(mesh.shape["fsdp"], mesh.shape["grp"])
    items = P(AXES, None, None)
    vector = P(AXES)
    rows = P(AXES, None)
    columns = P(None, AXES)
    weights = (rows, rows, rows, rows, rows, columns)

    def run(*arrays):
        return per_device(grid, *arrays)

    return jax.shard_map(
        run,
        mesh=mesh,
        in_specs=(items, items, vector, vector) + weights * 3,
        out_specs=(items, items) + weights * 4,
        check_vma=False,
    )
```

```python
import functools

import jax
import jax.numpy as jnp
import numpy as np
from jax import lax
from jax.experimental import pallas as pl
from jax.experimental.pallas import tpu as pltpu
from jax.sharding import PartitionSpec as P

D = 1024
HEADS = 16
HEAD = 64
FF = 4096
SCALES = 10
STEP = 3
AXES = ("fsdp", "grp")

patch_sides = (1, 2, 3, 4, 5, 6, 8, 10, 13, 16)
norm_eps = 1e-06
adam_eps = 1e-08
decay = 0.05
highest = lax.Precision.HIGHEST
bf16 = jnp.bfloat16
f32 = jnp.float32


def scale_layout(slots):
    squares = np.array(patch_sides[:SCALES], dtype=np.int64) ** 2
    bounds = np.cumsum(squares)
    scale_ids = np.searchsorted(bounds, np.arange(slots), side="right")
    return (bounds.astype(np.int32), scale_ids.astype(np.int32))


def norm_rows(values):
    centre = values - jnp.mean(values, axis=-1, keepdims=True)
    spread = jnp.mean(centre * centre, axis=-1, keepdims=True)
    return centre * lax.rsqrt(spread + norm_eps)


def modulate(values, scale_row, shift_row):
    return norm_rows(values) * (1.0 + scale_row) + shift_row


def gelu_tanh(values):
    return jax.nn.gelu(values, approximate=True)


def gelu_and_slope(v):
    root = np.float32(np.sqrt(2 / np.pi))
    cube = np.float32(0.044715) * root
    square = v * v
    t = jnp.tanh(v * (root + cube * square))
    half = 0.5 + 0.5 * t
    act = v * half
    return [half + act * ((1.0 - t) * (root + (3 * cube) * square)), act]


def learn_rates():
    return (D ** (-0.5), (D // 16) ** (-0.5), D ** (-0.5), FF ** (-0.5), D ** (-0.5), 1.0)


def adamw(weight, gradient, first, second, bias_one, bias_two, rate):
    first_new = 0.5 * first + 0.5 * gradient
    second_new = 0.5 * second + 0.5 * gradient * gradient
    update = first_new / bias_one / (jnp.sqrt(second_new / bias_two) + adam_eps) + decay * weight
    weight_new = weight - rate * update
    return (weight_new, weight_new.astype(bf16), first_new, second_new)


def contract_rows(former, latter):
    return lax.dot_general(former, latter, (((0,), (0,)), ((), ())), preferred_element_type=f32)


def contract_cols(former, latter):
    return lax.dot_general(former, latter, (((1,), (1,)), ((), ())), preferred_element_type=f32)


def dot_nt(former, latter):
    return lax.dot_general(former, latter, (((1,), (1,)), ((), ())), preferred_element_type=f32)


def dot_nn(former, latter):
    return lax.dot_general(former, latter, (((1,), (0,)), ((), ())), preferred_element_type=f32)


def dot_tn(former, latter):
    return lax.dot_general(former, latter, (((0,), (0,)), ((), ())), preferred_element_type=f32)


FORWARD_TILES = ((0, 240, 256), (240, 416, 432), (416, 680, 680))
BACKWARD_TILES = ((0, 128, 160), (128, 384, 432), (384, 680, 680))


def attend_kernel(q_ref, k_ref, v_ref, bias_ref, context_ref, lse_ref):
    for begin, end, keys in FORWARD_TILES:
        q = q_ref[begin:end, :] * bf16(0.125)
        lane = lax.broadcasted_iota(jnp.int32, q.shape, 1)
        contexts, totals = [], []
        for head in range(2):
            own = jnp.where((lane < HEAD) == (head == 0), q, bf16(0))
            scores = dot_nt(own, k_ref[:keys, :]) + bias_ref[begin:end, :keys]
            largest = jnp.max(scores, axis=1, keepdims=True)
            expo = jnp.exp(scores - largest)
            total = jnp.sum(expo, axis=1, keepdims=True)
            probs = (expo * (1.0 / total)).astype(bf16)
            totals.append(largest + jnp.log(total))
            contexts.append(dot_nn(probs, v_ref[:keys, :]))
        left = lax.broadcasted_iota(jnp.int32, contexts[0].shape, 1) < HEAD
        context_ref[begin:end, :] = jnp.where(left, contexts[0], contexts[1]).astype(bf16)
        lse = jnp.where(left, totals[0], totals[1]).T
        lse_ref[0, 0:1, begin:end] = lse[0:1]
        lse_ref[0, 1:2, begin:end] = lse[HEAD : HEAD + 1]


def attend_forward(packed, bias, begin, end, so_far=None):
    slots, width = packed.shape[0], packed.shape[1] // 3
    pairs = width // 128
    assert slots == FORWARD_TILES[-1][1]

    def block(offset):
        return pl.BlockSpec((slots, 128), lambda i: (0, offset + begin + i))

    more = list(so_far) if so_far else []

    def kernel(q_ref, k_ref, v_ref, bias_ref, *refs):
        attend_kernel(q_ref, k_ref, v_ref, bias_ref, *refs[len(more) :])

    return pl.pallas_call(
        kernel,
        grid=(end - begin,),
        in_specs=[
            block(0),
            block(pairs),
            block(2 * pairs),
            pl.BlockSpec((slots, slots), lambda i: (0, 0), pipeline_mode=pl.Buffered(1)),
        ]
        + [pl.BlockSpec(memory_space=pl.ANY)] * len(more),
        out_specs=[block(0), pl.BlockSpec((1, 2, slots), lambda i: (begin + i, 0, 0))],
        out_shape=[
            jax.ShapeDtypeStruct((slots, width), bf16),
            jax.ShapeDtypeStruct((pairs, 2, slots), f32),
        ],
        input_output_aliases={4 + i: i for i in range(len(more))},
        cost_estimate=estimate(
            flops=5 * slots * slots * width,
            bytes_accessed=6 * slots * width,
            transcendentals=slots * slots * HEADS // 2,
        ),
        compiler_params=pltpu.CompilerParams(vmem_limit_bytes=20 << 20),
        name="attend",
    )(packed, packed, packed, bias, *more)


def attend_back_kernel(
    half, place_ref, q_ref, k_ref, v_ref, grad_ref, lse_ref, bias_ref, out_ref, give_ref, *refs
):
    keys_ref, values_ref, y_ref, out_sems, give_sems = refs
    step = pl.program_id(0)
    slot = lax.rem(step, 2)
    width = 2 * half * 128

    def copies(step, slot, run):
        pair = lax.rem(step + (1 - place_ref[2]) * half, 2 * half)
        for i in range(3):
            at = pl.multiple_of(i * width + pair * 128, 128)
            run(
                pltpu.make_async_copy(
                    y_ref.at[slot, i], out_ref.at[:, pl.ds(at, 128)], out_sems.at[slot, i]
                )
            )

        @pl.when(step < half)
        def _():
            for i in range(3):
                at = pl.multiple_of((i * half + step) * 128, 128)
                run(
                    pltpu.make_async_copy(
                        y_ref.at[slot, i], give_ref.at[:, pl.ds(at, 128)], give_sems.at[slot, i]
                    )
                )

    @pl.when(step >= 2)
    def _():
        copies(step - 2, slot, lambda copy: copy.wait())

    for count, (begin, end, keys) in enumerate(reversed(BACKWARD_TILES)):
        q = q_ref[begin:end, :] * bf16(0.125)
        grad = grad_ref[begin:end, :]
        k = k_ref[:keys, :]
        v = v_ref[:keys, :]
        left = lax.broadcasted_iota(jnp.int32, q.shape, 1) < HEAD
        d_q, d_k, d_v = [], [], []
        for head in range(2):
            own = left == (head == 0)
            scores = dot_nt(k, jnp.where(own, q, bf16(0))) + bias_ref[:keys, begin:end]
            probs = jnp.exp(scores - lse_ref[0, head : head + 1, begin:end])
            d_probs = dot_nt(v, jnp.where(own, grad, bf16(0)))
            inner = jnp.sum(probs * d_probs, axis=0, keepdims=True)
            d_scores = (probs * (d_probs - inner)).astype(bf16)
            d_v.append(dot_nn(probs.astype(bf16), grad))
            d_k.append(dot_nn(d_scores, q))
            d_q.append(dot_tn(d_scores, k))
        first = lax.broadcasted_iota(jnp.int32, d_k[0].shape, 1) < HEAD
        d_k = jnp.where(first, d_k[0], d_k[1])
        d_v = jnp.where(first, d_v[0], d_v[1])
        if count == 0:
            keys_ref[:keys, :] = d_k
            values_ref[:keys, :] = d_v
        else:
            keys_ref[:keys, :] += d_k
            values_ref[:keys, :] += d_v
        y_ref[slot, 0, begin:end, :] = (jnp.where(left, d_q[0], d_q[1]) * 0.125).astype(bf16)
    y_ref[slot, 1] = keys_ref[...].astype(bf16)
    y_ref[slot, 2] = values_ref[...].astype(bf16)
    copies(step, slot, lambda copy: copy.start())

    @pl.when(step == 2 * half - 1)
    def _():
        copies(step - 1, 1 - slot, lambda copy: copy.wait())
        copies(step, slot, lambda copy: copy.wait())


def attend_backward(place, packed, d_context, lse, bias_t):
    slots, width = packed.shape[0], packed.shape[1] // 3
    pairs = width // 128
    half = pairs // 2
    assert slots == BACKWARD_TILES[-1][1] and pairs >= 2

    def at(i, place):
        return lax.rem(i + (1 - place[2]) * half, pairs)

    def block(offset):
        return pl.BlockSpec((slots, 128), lambda i, place: (0, offset + at(i, place)))

    return pl.pallas_call(
        functools.partial(attend_back_kernel, half),
        grid_spec=pltpu.PrefetchScalarGridSpec(
            num_scalar_prefetch=1,
            grid=(pairs,),
            in_specs=[
                block(0),
                block(pairs),
                block(2 * pairs),
                block(0),
                pl.BlockSpec((1, 2, slots), lambda i, place: (at(i, place), 0, 0)),
                pl.BlockSpec((slots, slots), lambda i, place: (0, 0), pipeline_mode=pl.Buffered(1)),
            ],
            out_specs=[pl.BlockSpec(memory_space=pl.ANY)] * 2,
            scratch_shapes=[
                pltpu.VMEM((slots, 128), f32),
                pltpu.VMEM((slots, 128), f32),
                pltpu.VMEM((2, 3, slots, 128), bf16),
                pltpu.SemaphoreType.DMA((2, 3)),
                pltpu.SemaphoreType.DMA((2, 3)),
            ],
        ),
        out_shape=[
            jax.ShapeDtypeStruct((slots, 3 * width), bf16),
            jax.ShapeDtypeStruct((slots, 3 * width // 2), bf16),
        ],
        cost_estimate=estimate(
            flops=20 * slots * slots * width,
            bytes_accessed=16 * slots * width,
            transcendentals=slots * slots * HEADS,
        ),
        compiler_params=pltpu.CompilerParams(vmem_limit_bytes=28 << 20),
        name="attend_back",
    )(place, packed, packed, packed, d_context, lse, bias_t)


def start_pieces(place_ref, pieces, w_ref, sems, rows, left, half, color):
    z, x, c, y = [place_ref[i] for i in range(4)]
    for far in range(2):
        for core in range(2):
            piece = pieces[core * 4 + far * 2 + color]
            for near in range(2):
                step_x, step_y = (far, near) if color == 0 else (near, far)
                for step in range(4):
                    at = (z ^ FLIPS[step]) * 2 + (x ^ step_x)
                    at = (at * 2 + (c ^ core)) * 2 + (y ^ step_y)
                    at = pl.multiple_of(at * rows, rows)
                    pltpu.make_async_copy(
                        piece.at[near, step, :, pl.ds(left, half)],
                        w_ref.at[color, pl.ds(at, rows), :],
                        sems.at[color],
                    ).start()


def gather_kernel(layout, place_ref, x_ref, *refs):
    rows, left, half, chunk, gelu, keep = layout
    outs = 2 if gelu else 1
    pieces, refs = refs[:8], refs[8:]
    whole_ref, refs = (refs[0], refs[1:]) if keep else (None, refs)
    out_refs, w_ref, y_refs = refs[:outs], refs[outs], refs[outs + 1 : 2 * outs + 1]
    in_sems, whole_sems, out_sems = refs[2 * outs + 1 :]
    start = functools.partial(start_pieces, place_ref, pieces, w_ref, in_sems, rows, left, half)
    start(0)
    waits = []
    for color in range(2):
        own = w_ref.at[color]
        pltpu.make_async_copy(own, own, in_sems.at[color]).wait()
        if color == 0:
            start(1)
        if keep:
            copy = pltpu.make_async_copy(
                own, whole_ref.at[:, pl.ds(color * half, half)], whole_sems.at[color]
            )
            copy.start()
            waits.append(copy)
        def outs_of(at, run):
            for i in range(outs):
                run(
                    pltpu.make_async_copy(
                        y_refs[i].at[:, pl.ds(at, chunk)],
                        out_refs[i].at[:, pl.ds(at, chunk)],
                        out_sems.at[i, at // chunk],
                    )
                )

        def step(n, carry, color=color):
            begin = pl.multiple_of(n * chunk, chunk)
            at = pl.multiple_of(color * half + n * chunk, chunk)
            result = dot_nn(x_ref[...], w_ref[color, :, pl.ds(begin, chunk)])
            values = gelu_and_slope(result) if gelu else [result]
            for i, value in enumerate(values):
                y_refs[i][:, pl.ds(at, chunk)] = value.astype(y_refs[i].dtype)
            outs_of(at, lambda copy: copy.start())
            return carry

        lax.fori_loop(0, half // chunk, step, 0)
        for n in range(half // chunk):
            outs_of(color * half + n * chunk, lambda copy: waits.append(copy))
    for copy in waits:
        copy.wait()


def gather_dot(place, x, pieces, left, half, kinds, keep, name):
    rows = pieces[0].shape[2]
    whole, width = rows * 32, 2 * half
    slots = x.shape[0]
    chunk = min(512, half)
    anywhere = pl.BlockSpec(memory_space=pl.ANY)
    shapes = [jax.ShapeDtypeStruct((whole, width), bf16)] * keep
    shapes += [jax.ShapeDtypeStruct((slots, width), kind) for kind in kinds]
    return pl.pallas_call(
        functools.partial(gather_kernel, (rows, left, half, chunk, len(kinds) == 2, keep)),
        grid_spec=pltpu.PrefetchScalarGridSpec(
            num_scalar_prefetch=1,
            grid=(1,),
            in_specs=[pl.BlockSpec(x.shape, lambda i, place: (0, 0))] + [anywhere] * 8,
            out_specs=[anywhere] * len(shapes),
            scratch_shapes=[pltpu.VMEM((2, whole, half), bf16)]
            + [pltpu.VMEM((slots, width), kind) for kind in kinds]
            + [
                pltpu.SemaphoreType.DMA((2,)),
                pltpu.SemaphoreType.DMA((2,)),
                pltpu.SemaphoreType.DMA((len(kinds), width // chunk)),
            ],
        ),
        out_shape=shapes,
        cost_estimate=estimate(
            flops=3 * slots * whole * width,
            bytes_accessed=2 * whole * width + 4 * slots * width,
            transcendentals=0,
        ),
        compiler_params=pltpu.CompilerParams(vmem_limit_bytes=56 << 20),
        name=name,
    )(place, x, *pieces)


def modulate_back_kernel(steps, more, place_ref, x_ref, w_ref, rows_ref, *refs):
    value_hbm, add_hbm, refs = refs[0], refs[1], refs[2:]
    if more:
        attended_hbm, proj_hbm, refs = refs[0], refs[1], refs[2:]
        out_hbm, low_hbm, give_hbm, context_hbm, sums_ref, refs = *refs[:5], refs[5:]
        total_ref, value_ref, add_ref, attended_ref, proj_ref, low_ref, context_ref, sems = refs
    else:
        out_hbm, sums_ref, total_ref, value_ref, add_ref, sems = refs
    step = pl.program_id(0)
    pairs = [(value_hbm, value_ref), (add_hbm, add_ref)]
    if more:
        pairs += [(attended_hbm, attended_ref), (proj_hbm, proj_ref)]
    loads = [pltpu.make_async_copy(a, b, sems.at[i]) for i, (a, b) in enumerate(pairs)]
    part = dot_nt(x_ref[...], w_ref[...])

    @pl.when(step == 0)
    def _():
        for load in loads:
            load.start()
        total_ref[...] = part

    @pl.when(step > 0)
    def _():
        total_ref[...] += part

    @pl.when(step == steps - 1)
    def _():
        for load in loads:
            load.wait()
        slots, width = total_ref.shape
        gain = rows_ref[0:1, :]
        length = place_ref[4]

        def block(at, count, sums):
            value = value_ref[pl.ds(at, count), :].astype(f32)
            centre = value - jnp.mean(value, axis=1, keepdims=True)
            rate = lax.rsqrt(jnp.mean(centre * centre, axis=1, keepdims=True) + norm_eps)
            normal = centre * rate
            grad = total_ref[pl.ds(at, count), :]
            scaled = grad * gain
            inner = jnp.mean(scaled * normal, axis=1, keepdims=True)
            result = rate * (scaled - jnp.mean(scaled, axis=1, keepdims=True) - normal * inner)
            add = add_ref[pl.ds(at, count), :].astype(f32)
            sums = [
                sums[0] + jnp.sum(grad * normal, axis=0, keepdims=True),
                sums[1] + jnp.sum(grad, axis=0, keepdims=True),
            ] + sums[2:]
            if more:
                slot = at + lax.broadcasted_iota(jnp.int32, (count, 1), 0)
                add = add * (slot < length).astype(f32)
            result = add + result
            total_ref[pl.ds(at, count), :] = result
            if more:
                attended = attended_ref[pl.ds(at, count), :]
                sums[2] = sums[2] + jnp.sum(result * attended, axis=0, keepdims=True)
                low_ref[pl.ds(at, count), :] = (result * rows_ref[1:2, :]).astype(bf16)
            return sums

        count = 32
        whole = slots // count
        sums = [jnp.zeros((1, width), f32) for _ in range(3 if more else 2)]
        sums = lax.fori_loop(
            0, whole, lambda i, sums: block(pl.multiple_of(i * count, count), count, sums), sums
        )
        if slots % count:
            sums = block(whole * count, slots % count, sums)
        sums_ref[...] = jnp.concatenate(
            sums + [jnp.zeros((8 - len(sums), width), f32)], axis=0
        )
        stores = [pltpu.make_async_copy(total_ref, out_hbm, sems.at[4])]
        if more:
            half = width // 2
            other = pl.multiple_of((1 - place_ref[2]) * half, half)
            stores += [
                pltpu.make_async_copy(low_ref.at[:, pl.ds(other, half)], give_hbm, sems.at[5]),
                pltpu.make_async_copy(low_ref, low_hbm, sems.at[6]),
            ]
        for store in stores:
            store.start()
        if more:
            context_ref[...] = dot_nt(low_ref[...], proj_ref[...]).astype(bf16)
            stores.append(pltpu.make_async_copy(context_ref, context_hbm, sems.at[7]))
            stores[-1].start()
        for store in stores:
            store.wait()


def modulate_back(place, x, weight, rows, value, add, attended=None, proj=None):
    more = proj is not None
    slots, depth = x.shape
    width = weight.shape[0]
    chunk = 1024
    assert depth % chunk == 0
    anywhere = pl.BlockSpec(memory_space=pl.ANY)
    operands = [value, add] + ([attended, proj] if more else [])
    shapes = [jax.ShapeDtypeStruct((slots, width), f32)]
    scratch = [
        pltpu.VMEM((slots, width), f32),
        pltpu.VMEM((slots, width), value.dtype),
        pltpu.VMEM((slots, width), add.dtype),
    ]
    if more:
        shapes += [
            jax.ShapeDtypeStruct((slots, width), bf16),
            jax.ShapeDtypeStruct((slots, width // 2), bf16),
            jax.ShapeDtypeStruct((slots, width), bf16),
        ]
        scratch += [
            pltpu.VMEM((slots, width), f32),
            pltpu.VMEM(proj.shape, bf16),
            pltpu.VMEM((slots, width), bf16),
            pltpu.VMEM((slots, width), bf16),
        ]
    return pl.pallas_call(
        functools.partial(modulate_back_kernel, depth // chunk, more),
        grid_spec=pltpu.PrefetchScalarGridSpec(
            num_scalar_prefetch=1,
            grid=(depth // chunk,),
            in_specs=[
                pl.BlockSpec((slots, chunk), lambda i, place: (0, i)),
                pl.BlockSpec((width, chunk), lambda i, place: (0, i)),
                pl.BlockSpec((8, width), lambda i, place: (0, 0)),
            ]
            + [anywhere] * len(operands),
            out_specs=[anywhere] * len(shapes)
            + [pl.BlockSpec((8, width), lambda i, place: (0, 0))],
            scratch_shapes=scratch + [pltpu.SemaphoreType.DMA((8,))],
        ),
        out_shape=shapes + [jax.ShapeDtypeStruct((8, width), f32)],
        cost_estimate=estimate(
            flops=3 * slots * width * (depth + width * more),
            bytes_accessed=2 * (slots + width) * depth + 16 * slots * width,
            transcendentals=0,
        ),
        compiler_params=pltpu.CompilerParams(vmem_limit_bytes=48 << 20),
        name="modulate_back",
    )(place, x, weight, rows, *operands)


def gelu_back_kernel(rows, place_ref, grad_ref, slope_ref, *refs):
    pieces, (out_ref, give_ref), refs = refs[:8], refs[8:10], refs[10:]
    w_ref, s_ref, y_ref, in_sems, s_sems, y_sems, give_sems = refs
    z, x, c, y = [place_ref[i] for i in range(4)]
    block = 4 * rows
    chunks = [(step, far_x) for step in range(4) for far_x in range(2)]
    where = [
        pl.multiple_of(((z ^ FLIPS[step]) * 2 + (x ^ far_x)) * block, block) for step, far_x in chunks
    ]
    half = pieces[0].shape[-1]

    def start(n):
        step, far_x = chunks[n]
        for core in range(2):
            for far_y in range(2):
                at = pl.multiple_of(((c ^ core) * 2 + (y ^ far_y)) * rows, rows)
                for color in range(2):
                    far, near = (far_x, far_y) if color == 0 else (far_y, far_x)
                    pltpu.make_async_copy(
                        pieces[core * 4 + far * 2 + color].at[near, step],
                        w_ref.at[n, pl.ds(at, rows), pl.ds(color * half, half)],
                        in_sems.at[n],
                    ).start()
        pltpu.make_async_copy(
            slope_ref.at[:, pl.ds(where[n], block)], s_ref.at[n], s_sems.at[n]
        ).start()

    def give(n, run):
        @pl.when(lax.shift_right_logical(z ^ FLIPS[chunks[n][0]], 1) != c)
        def _():
            at = pl.multiple_of(where[n] - (1 - c) * (4 * block), block)
            run(
                pltpu.make_async_copy(
                    y_ref.at[n], give_ref.at[:, pl.ds(at, block)], give_sems.at[n]
                )
            )

    ahead = 2
    for n in range(ahead):
        start(n)
    waits = []
    for n in range(len(chunks)):
        pltpu.make_async_copy(w_ref.at[n], w_ref.at[n], in_sems.at[n]).wait()
        pltpu.make_async_copy(s_ref.at[n], s_ref.at[n], s_sems.at[n]).wait()
        if n + ahead < len(chunks):
            start(n + ahead)
        y_ref[n] = (dot_nt(grad_ref[...], w_ref[n]) * s_ref[n].astype(f32)).astype(bf16)
        copy = pltpu.make_async_copy(
            y_ref.at[n], out_ref.at[:, pl.ds(where[n], block)], y_sems.at[n]
        )
        copy.start()
        waits.append(copy)
        give(n, lambda copy: copy.start())
    for n in range(len(chunks)):
        give(n, lambda copy: copy.wait())
    for copy in waits:
        copy.wait()


def gelu_back_dot(place, grad, slope, pieces):
    slots, width = slope.shape
    rows = pieces[0].shape[2]
    assert width == 32 * rows and grad.shape[1] == 2 * pieces[0].shape[3]
    anywhere = pl.BlockSpec(memory_space=pl.ANY)
    block = 4 * rows
    return pl.pallas_call(
        functools.partial(gelu_back_kernel, rows),
        grid_spec=pltpu.PrefetchScalarGridSpec(
            num_scalar_prefetch=1,
            grid=(1,),
            in_specs=[pl.BlockSpec(grad.shape, lambda i, place: (0, 0))] + [anywhere] * 9,
            out_specs=[anywhere] * 2,
            scratch_shapes=[
                pltpu.VMEM((8, block, grad.shape[1]), bf16),
                pltpu.VMEM((8, slots, block), slope.dtype),
                pltpu.VMEM((8, slots, block), bf16),
            ]
            + [pltpu.SemaphoreType.DMA((8,))] * 4,
        ),
        out_shape=[
            jax.ShapeDtypeStruct((slots, width), bf16),
            jax.ShapeDtypeStruct((slots, width // 2), bf16),
        ],
        cost_estimate=estimate(
            flops=3 * slots * width * grad.shape[1],
            bytes_accessed=8 * slots * width + 4 * width * grad.shape[1],
            transcendentals=0,
        ),
        compiler_params=pltpu.CompilerParams(vmem_limit_bytes=56 << 20),
        name="gelu_back",
    )(place, grad, slope, *pieces)


def weight_grad_kernel(depth, rows, turn, firsts, place_ref, *refs):
    products = len(firsts)
    ins, out_refs = refs[: 4 * products], refs[4 * products :]
    step = pl.program_id(0)
    inner = lax.rem(step, turn)

    def product(own_ref, other_ref, mine_ref, take_ref):
        total = dot_tn(own_ref[...], mine_ref[...]) + dot_tn(other_ref[...], take_ref[...])
        total = total.reshape(depth, 2, 2, 2, rows, total.shape[-1])

        @pl.when(step < turn)
        def _():
            first = place_ref[3] == 0
            for x in range(2):
                low, high = total[:, x, :, 0], total[:, x, :, 1]
                out_refs[0][x] = jnp.where(first, high, low).astype(bf16)
                out_refs[1][x] = jnp.where(first, low, high).astype(bf16)

        @pl.when(step >= turn)
        def _():
            first = place_ref[1] == 0
            for y in range(2):
                low, high = total[:, 0, :, y], total[:, 1, :, y]
                out_refs[2][y] = jnp.where(first, high, low).astype(bf16)
                out_refs[3][y] = jnp.where(first, low, high).astype(bf16)

    if products == 1:
        product(*ins)
        return
    for n, (begin, end) in enumerate(firsts):

        @pl.when((inner >= begin) & (inner < end))
        def _(n=n):
            product(*ins[4 * n : 4 * n + 4])


def weight_grad_call(place, products, rows, chunk):
    specs, operands, firsts = [], [], []
    turn = flops = 0
    for own, other, rhs, take, groups in products:
        slots, columns = rhs.shape[0], rhs.shape[1] // groups
        per = columns // 2 // chunk
        count = groups * per // 2
        assert groups * per % 2 == 0 and columns % (2 * chunk) == 0
        flops += 6 * slots * own.shape[1] * groups * columns // 2
        firsts.append((turn, turn + count))
        specs.append((per, count, turn))
        turn += count
        operands += [own, other, rhs, take]
    in_specs = []
    for (own, *_), (per, count, begin) in zip(products, specs):
        slots = own.shape[0]

        def which(i, count=count, begin=begin):
            color = i // turn
            return color * count + jnp.clip(i - color * turn - begin, 0, count - 1)

        once = pl.Buffered(1)
        in_specs += [pl.BlockSpec(own.shape, lambda i, place: (0, 0), pipeline_mode=once)] * 2
        in_specs.append(
            pl.BlockSpec(
                (slots, chunk),
                lambda i, place, which=which, per=per: (
                    0,
                    (which(i) // per * 2 + place[2]) * per + lax.rem(which(i), per),
                ),
            )
        )
        in_specs.append(
            pl.BlockSpec((slots, chunk), lambda i, place, which=which: (0, which(i)))
        )
    width = products[0][0].shape[1]
    depth = width // rows // 8
    block = (2, depth, 2, rows, chunk)
    early = pl.BlockSpec(block, lambda i, place: (0, 0, 0, 0, jnp.minimum(i, turn - 1)))
    late = pl.BlockSpec(block, lambda i, place: (0, 0, 0, 0, jnp.maximum(i - turn, 0)))
    shape = jax.ShapeDtypeStruct((2, depth, 2, rows, turn * chunk), bf16)
    return pl.pallas_call(
        functools.partial(weight_grad_kernel, depth, rows, turn, tuple(firsts)),
        grid_spec=pltpu.PrefetchScalarGridSpec(
            num_scalar_prefetch=1,
            grid=(2 * turn,),
            in_specs=in_specs,
            out_specs=[early, early, late, late],
        ),
        out_shape=[shape] * 4,
        cost_estimate=estimate(
            flops=flops,
            bytes_accessed=sum(2 * v.size for v in operands) + 4 * width * turn * chunk,
            transcendentals=0,
        ),
        compiler_params=pltpu.CompilerParams(vmem_limit_bytes=60 << 20),
        name="weight_grad",
    )(place, *operands)


def estimate(flops, bytes_accessed, transcendentals):
    return pl.CostEstimate(
        flops=flops // 64, bytes_accessed=bytes_accessed // 64, transcendentals=transcendentals // 64
    )


def weight_grad_rows_kernel(rows, place_ref, own_ref, other_ref, mine_ref, take_ref, *out_refs):
    total = dot_tn(own_ref[...], mine_ref[...]) + dot_tn(other_ref[...], take_ref[...])
    total = total.reshape(2, 2, 2, rows, total.shape[-1])
    half = total.shape[-1] // 2
    first_y, first_x = place_ref[3] == 0, place_ref[1] == 0
    for i in range(2):
        low, high = total[i, :, 0, :, :half], total[i, :, 1, :, :half]
        out_refs[0][i, 0] = jnp.where(first_y, high, low).astype(bf16)
        out_refs[1][i, 0] = jnp.where(first_y, low, high).astype(bf16)
        low, high = total[0, :, i, :, half:], total[1, :, i, :, half:]
        out_refs[2][i, 0] = jnp.where(first_x, high, low).astype(bf16)
        out_refs[3][i, 0] = jnp.where(first_x, low, high).astype(bf16)


def weight_grad_rows(place, own, other, rhs, take, rows):
    slots, width = own.shape
    half = take.shape[1]
    depth = width // rows // 8
    out = pl.BlockSpec((2, 1, 2, rows, half // 2), lambda i, place: (0, i, 0, 0, 0))
    by_z = pl.BlockSpec((slots, 8 * rows), lambda i, place: (0, i))
    shape = jax.ShapeDtypeStruct((2, depth, 2, rows, half // 2), bf16)
    return pl.pallas_call(
        functools.partial(weight_grad_rows_kernel, rows),
        grid_spec=pltpu.PrefetchScalarGridSpec(
            num_scalar_prefetch=1,
            grid=(depth,),
            in_specs=[
                by_z,
                by_z,
                pl.BlockSpec((slots, half), lambda i, place: (0, place[2])),
                pl.BlockSpec((slots, half), lambda i, place: (0, 0)),
            ],
            out_specs=[out] * 4,
        ),
        out_shape=[shape] * 4,
        cost_estimate=estimate(
            flops=4 * slots * width * half,
            bytes_accessed=4 * slots * (width + half) + 2 * width * half,
            transcendentals=0,
        ),
        compiler_params=pltpu.CompilerParams(vmem_limit_bytes=60 << 20),
        name="weight_grad_rows",
    )(place, own, other, rhs, take)


class Line:
    def __init__(self):
        self.last = jnp.zeros((8, 128), f32)

    def __call__(self, *values):
        self.last, values = lax.optimization_barrier((self.last, values))
        return values[0] if len(values) == 1 else values

    def arrive(self, movers, *values):
        gots, values = self([mover.got for mover in movers], values)
        for mover, got in zip(movers, gots):
            mover.got = got
        return values[0] if len(values) == 1 else values


class Scatter:
    def __init__(self, grid, line, rows):
        self.grid, self.line, self.flips = grid, line, grid.bits()
        self.rows = rows.reshape([2] * len(self.flips) + list(rows.shape[1:]))

    def start(self):
        dim = len(self.flips) - 1
        axis, bit = self.flips.pop(0)
        self.own = lax.index_in_dim(self.rows, 0, dim, keepdims=False)
        away = self.line(lax.index_in_dim(self.rows, 1, dim, keepdims=False))
        self.got = self.grid.flip(away, axis, bit)

    def add(self):
        self.rows = self.own + self.got


class Gather:
    orders = ("yx", "xy")

    def __init__(self, grid, line, shards):
        self.grid, self.line = grid, line
        lows = [shard[:, : shard.shape[1] // 2] for shard in shards]
        highs = [shard[:, shard.shape[1] // 2 :] for shard in shards]
        self.shard = jnp.concatenate(lows + highs, axis=1)

    def first(self):
        self.shard = self.line(self.shard)
        self.got = self.grid.flip(self.shard, "z", 2)

    def second(self):
        self.pair = self.line(jnp.stack([self.shard, self.got]))
        self.got = self.grid.flip(self.pair, "z", 1)

    def third(self):
        half = self.shard.shape[1] // 2
        pairs = (self.pair, self.got)
        rows = [
            jnp.concatenate([p[:, :, i * half : (i + 1) * half] for p in pairs], axis=0)
            for i in range(2)
        ]
        self.rows = self.line(*rows)
        self.got = [self.grid.flip(v, o[0], 1) for v, o in zip(self.rows, self.orders)]

    def fourth(self):
        plane = [
            jnp.concatenate([own[None], new[None]], axis=0) for own, new in zip(self.rows, self.got)
        ]
        self.plane = self.line(*plane)
        self.got = [self.grid.flip(v, o[1], 1) for v, o in zip(self.plane, self.orders)]
        self.near = [self.grid.flip(v, "c", 1) for v in self.plane]

    def pieces(self):
        far = [self.grid.flip(v, "c", 1) for v in self.got]
        return list(self.plane) + list(self.got) + list(self.near) + far


FLIPS = (0, 2, 1, 3)


def add_split_kernel(joined, place_ref, *refs):
    sums = len(refs) // (5 if joined else 6)
    outs = refs[4 * sums :]
    for n in range(sums):
        for side in range(2):
            one, two = refs[4 * n + 2 * side], refs[4 * n + 2 * side + 1]
            out = outs[side] if joined else outs[2 * n + side]
            total = one[...].astype(f32) + two[...].astype(f32)
            if joined:
                width = total.shape[-1]
                out[..., n * width : (n + 1) * width] = total.astype(out.dtype)
            else:
                out[...] = total.reshape(out.shape).astype(out.dtype)


def add_split(place, name, steps, specs, *pairs, joined=False, kind=bf16):
    in_specs, operands, out_specs, shapes = [], [], [], []
    for n, pair in enumerate(pairs):
        lead = pair[0].ndim - 3
        if pair[0].ndim == 3:
            lead = 1
        tail = pair[0].shape[lead:]
        for side in range(2):
            for array in pair:
                in_specs.append(
                    pl.BlockSpec(
                        (1,) * lead + tail,
                        lambda i, place, n=n, side=side, zeros=(0,) * len(tail): (
                            specs(i, place)[n][side] + zeros
                        ),
                    )
                )
                operands.append(array)
            if joined and n:
                continue
            wide = tail[:-1] + (tail[-1] * (len(pairs) if joined else 1),)
            out_specs.append(
                pl.BlockSpec(
                    (1,) + wide, lambda i, place, zeros=(0,) * len(wide): (i,) + zeros
                )
            )
            shapes.append(jax.ShapeDtypeStruct((steps,) + wide, kind))
    return pl.pallas_call(
        functools.partial(add_split_kernel, joined),
        grid_spec=pltpu.PrefetchScalarGridSpec(
            num_scalar_prefetch=1, grid=(steps,), in_specs=in_specs, out_specs=out_specs
        ),
        out_shape=shapes,
        cost_estimate=estimate(
            flops=sum(array.size for array in operands),
            bytes_accessed=4 * sum(array.size for array in operands),
            transcendentals=0,
        ),
        compiler_params=pltpu.CompilerParams(vmem_limit_bytes=24 << 20),
        name=name,
    )(place, *operands)


class GradSum:
    def __init__(self, grid, line, here, place, products, rows, chunk, movers=()):
        self.grid, self.line, self.here, self.place, self.rows = grid, line, here, place, rows
        self.shapes = [(groups, rhs.shape[1] // groups) for _, _, rhs, _, groups in products]
        if len(products) == 1 and products[0][4] == 1:
            grads = weight_grad_rows(place, *products[0][:4], rows)
        else:
            grads = weight_grad_call(place, products, rows, chunk)
        away_one, self.one, away_two, self.two = line.arrive(movers, *grads)
        self.got = [grid.flip(away_one, "y", 1), grid.flip(away_two, "x", 1)]

    def second(self):
        away_one, self.one, away_two, self.two = self.line(
            *add_split(self.place, "add_second", 4, self.second_specs, *self.parts())
        )
        self.got = [self.grid.flip(away_one, "x", 1), self.grid.flip(away_two, "y", 1)]

    def parts(self):
        return [(self.one, self.got[0]), (self.two, self.got[1])]

    def second_specs(self, i, place):
        x, y = place[1], place[3]
        return [((1 - x, i), (x, i)), ((1 - y, i), (y, i))]

    def third(self):
        def specs(i, place):
            low = lax.rem(place[0], 2)
            pair = ((2 * i + 1 - low,), (2 * i + low,))
            return [pair, pair]

        away, self.both = self.line(
            *add_split(self.place, "add_third", 2, specs, *self.parts(), joined=True)
        )
        self.got = self.grid.flip(away, "z", 1)

    def fourth(self):
        def specs(i, place):
            high = place[0] // 2
            return [((1 - high,), (high,))]

        away, self.both = self.line(
            *add_split(self.place, "add_fourth", 1, specs, (self.both, self.got))
        )
        away, self.both = away[0], self.both[0]
        self.got = self.grid.flip(away, "z", 2)

    def fifth(self):
        def specs(i, place):
            return [((1 - place[2],), (place[2],))]

        give, self.keep = self.line(
            *add_split(self.place, "add_fifth", 1, specs, (self.both, self.got), kind=f32)
        )
        give, self.keep = give[0], self.keep[0]
        self.take = self.grid.flip(give, "c", 1)

    def result(self):
        first = self.here["c"] == 0
        low = jnp.where(first, self.keep, self.take)
        high = jnp.where(first, self.take, self.keep)
        sums, left, middle = [], 0, low.shape[1] // 2
        for groups, columns in self.shapes:
            part = groups * columns // 4
            half = columns // 2
            sides = []
            for side in (low, high):
                colors = [side[:, left : left + part], side[:, middle + left : middle + left + part]]
                sides.append(jnp.concatenate(colors, axis=1))
            spans = [side[:, g * half : (g + 1) * half] for g in range(groups) for side in sides]
            sums.append(jnp.concatenate(spans, axis=1))
            left += part
        return sums


class Grid:
    def __init__(self, fsdp, grp):
        outer = fsdp // 2
        self.size = {"c": 2, "x": 2 if outer % 2 == 0 else 1, "y": grp}
        self.size["z"] = outer // self.size["x"]
        self.count = fsdp * grp
        self.fsdp = fsdp

    def here(self):
        place = lax.axis_index("fsdp")
        wide = self.size["x"]
        return {
            "c": place % 2,
            "x": (place // 2) % wide,
            "z": place // (2 * wide),
            "y": lax.axis_index("grp"),
        }

    def shift(self, array, axis, step):
        size = self.size[axis]
        if axis == "y":
            return lax.ppermute(array, "grp", [(i, (i + step) % size) for i in range(size)])
        stride = {"c": 1, "x": 2, "z": 2 * self.size["x"]}[axis]
        pairs = []
        for i in range(self.fsdp):
            at = (i // stride) % size
            pairs.append((i, i + ((at + step) % size - at) * stride))
        return lax.ppermute(array, "fsdp", pairs)

    def fits(self, rows):
        size = self.size
        return size["x"] == 2 and size["y"] == 2 and size["z"] == 4 and rows % 32 == 0

    def bits(self):
        flips = []
        for axis in "cxyz":
            size = self.size[axis]
            assert size & (size - 1) == 0
            bit = size // 2
            while bit:
                flips.append((axis, bit))
                bit //= 2
        return flips

    def gather_all(self, row, flips):
        for axis, bit in flips:
            row = jnp.concatenate([row[None], self.flip(row, axis, bit)[None]], axis=0)
        return row

    def sources(self, here):
        flips = self.bits()
        turn = {axis: np.zeros(self.count, np.int32) for axis in "cxyz"}
        for n in range(self.count):
            for k, (axis, bit) in enumerate(flips):
                if n >> k & 1:
                    turn[axis][n] ^= bit
        z, x, c, y = [here[axis] ^ turn[axis] for axis in "zxcy"]
        return ((z * self.size["x"] + x) * 2 + c) * self.size["y"] + y

    def flip(self, array, axis, bit):
        size = self.size[axis]
        if axis == "y":
            return lax.ppermute(array, "grp", [(i, i ^ bit) for i in range(size)])
        stride = {"c": 1, "x": 2, "z": 2 * self.size["x"]}[axis]
        pairs = [
            (i, i + (((i // stride) % size ^ bit) - (i // stride) % size) * stride)
            for i in range(self.fsdp)
        ]
        return lax.ppermute(array, "fsdp", pairs)

    def scatter_sum(self, array, axis, dim, here, kind=bf16):
        size = self.size[axis]
        total = lax.dynamic_index_in_dim(array, here[axis], dim, keepdims=False)
        for step in range(1, size):
            piece = lax.dynamic_index_in_dim(array, (here[axis] + step) % size, dim, keepdims=False)
            total = total + self.shift(piece.astype(kind), axis, step).astype(f32)
        return total


def per_device(
    grid,
    block_in,
    cotangent,
    stop_scale,
    class_label,
    w_qkv,
    w_proj,
    w_fc1,
    w_fc2,
    w_ada,
    w_table,
    m_qkv,
    m_proj,
    m_fc1,
    m_fc2,
    m_ada,
    m_table,
    v_qkv,
    v_proj,
    v_fc1,
    v_fc2,
    v_ada,
    v_table,
):
    items, slots, width = block_in.shape
    assert items == 1
    here = grid.here()
    bounds, scale_ids = scale_layout(slots)
    picked = jnp.arange(SCALES) == stop_scale[0] - 1
    length = jnp.sum(jnp.where(picked, jnp.asarray(bounds), 0))
    position = jnp.arange(slots)
    valid = (position < length).astype(f32)[:, None]
    scale_table = jnp.asarray(scale_ids)

    def mask(length):
        allowed = (scale_table[None, :] <= scale_table[:, None]) & (position[None, :] < length)
        return jnp.where(allowed, f32(0), f32(-1e30))

    place = jnp.stack([here[axis] for axis in "zxcy"] + [length]).astype(jnp.int32)
    fits = grid.fits(w_qkv.shape[0])
    cast_qkv, cast_proj, cast_fc1, cast_fc2 = [
        w.astype(bf16) for w in (w_qkv, w_proj, w_fc1, w_fc2)
    ]
    half_qkv, half_proj, half_fc1 = [w.shape[1] // 2 for w in (w_qkv, w_proj, w_fc1)]
    line = Line()
    if fits:
        all_qkv = Gather(grid, line, [cast_qkv])
        all_qkv.first()
        place = line(place)
    labels = lax.all_to_all(
        jnp.broadcast_to(class_label, (grid.count,)), AXES, 0, 0, tiled=True
    )
    labels = jnp.take(labels, grid.sources(here))
    cast_ada = w_ada.astype(bf16)
    cast_table = w_table.astype(bf16)
    onehot = (labels[:, None] == jnp.arange(cast_table.shape[0])[None, :]).astype(bf16)
    cond = jnp.dot(onehot, cast_table, preferred_element_type=f32)
    silu_out, silu_back = jax.vjp(jax.nn.silu, cond)
    lifted_low = silu_out.astype(bf16)

    ada = jnp.dot(lifted_low, cast_ada, preferred_element_type=f32)
    flips = grid.bits()
    along = len(flips) - 2
    ada = Scatter(grid, line, ada.reshape(grid.count, -1, 128))
    if fits:
        ada.start()
        line.arrive([ada, all_qkv])
        ada.add()
        all_qkv.second()
        ada.start()
        line.arrive([ada])
        ada.add()
        line.arrive([all_qkv])
        all_qkv.third()
        all_rest = Gather(grid, line, [cast_proj, cast_fc1])
        all_rest.first()
        ada.start()
        line.arrive([ada])
        ada.add()
        line.arrive([all_qkv])
        all_qkv.fourth()
        ada.start()
        line.arrive([ada, all_rest])
        all_rest.second()
        ada.add()
        ada.start()
        bias = mask(line(length))
        bias, bias_t = line.arrive([all_qkv, all_rest], bias, bias.T)
        pieces_qkv = all_qkv.pieces()
        all_rest.third()
        line.arrive([ada])
        ada.add()
    else:
        while ada.flips:
            ada.start()
            ada.add()
        bias = mask(length)
        bias_t = bias.T
    ada = ada.rows.reshape(1, 6 * width)
    gamma_one, scale_one, shift_one, gamma_two, scale_two, shift_two = [
        ada[:, i * width : (i + 1) * width] for i in range(6)
    ]

    def half_columns(rhs, core, groups=1):
        half = rhs.shape[1] // groups // 2
        parts = [
            lax.dynamic_slice_in_dim(rhs, (2 * i + core) * half, half, 1) for i in range(groups)
        ]
        return jnp.concatenate(parts, axis=1)

    def weight_grad(lhs, other_lhs, rhs, take, groups):
        half = take.shape[1]
        size = grid.size
        rows = lhs.shape[1] // grid.count
        mine = half_columns(rhs, here["c"], groups)
        both = jnp.concatenate([mine, take], axis=0)
        grad = contract_rows(jnp.concatenate([lhs, other_lhs], axis=0), both)
        grad = grad.reshape(size["z"], size["x"], 2, size["y"], rows, half)
        middle = half // 2
        one = grid.scatter_sum(grad[..., :middle], "y", 3, here)
        two = grid.scatter_sum(grad[..., middle:], "x", 1, here)
        one = grid.scatter_sum(one, "x", 1, here)
        two = grid.scatter_sum(two, "y", 2, here)
        both = grid.scatter_sum(jnp.concatenate([one, two], axis=-1), "z", 0, here)
        keep = lax.dynamic_index_in_dim(both, here["c"], 0, keepdims=False)
        give = lax.dynamic_index_in_dim(both, 1 - here["c"], 0, keepdims=False)
        take = grid.shift(give, "c", 1)
        low = jnp.where(here["c"] == 0, keep, take).reshape(rows, groups, 1, half // groups)
        high = jnp.where(here["c"] == 0, take, keep).reshape(rows, groups, 1, half // groups)
        return jnp.concatenate([low, high], axis=2).reshape(rows, 2 * half)

    tokens = block_in[0].astype(f32)
    hidden, modulate_one = jax.vjp(modulate, tokens, scale_one, shift_one)
    hidden_low = hidden.astype(bf16)
    hidden_other = grid.shift(hidden_low, "c", 1)
    if fits:
        hidden_low, pieces_qkv[4:] = line(hidden_low, pieces_qkv[4:])
        wide_qkv, packed = gather_dot(
            place, hidden_low, pieces_qkv, 0, half_qkv, [bf16], True, "gather_qkv"
        )
        packed, hidden_other = line.arrive([all_rest], packed, hidden_other)
        all_rest.fourth()
        all_fc2 = Gather(grid, line, [cast_fc2])
        all_fc2.first()
        packed = line(packed)
    else:
        wide_qkv = lax.all_gather(cast_qkv, AXES, axis=0, tiled=True)
        packed = jnp.dot(hidden_low, wide_qkv, preferred_element_type=f32).astype(bf16)
    pairs = width // 128
    heads = attend_forward(packed, bias, 0, pairs // 2)
    if fits:
        heads, all_rest.near = line.arrive([all_fc2], heads, all_rest.near)
        all_fc2.second()
    packed = line(packed)
    heads = attend_forward(packed, bias, pairs // 2, pairs, heads)
    if fits:
        heads = line.arrive([all_rest, all_fc2], *heads)
        pieces_rest = all_rest.pieces()
        all_fc2.third()
    context, lse = heads
    if fits:
        context, pieces_rest[4:] = line(context, pieces_rest[4:])
        wide_proj, attended = gather_dot(
            place, context, pieces_rest, 0, half_proj, [f32], True, "gather_proj"
        )
    else:
        wide_proj = lax.all_gather(cast_proj, AXES, axis=0, tiled=True)
        attended = jnp.dot(context, wide_proj, preferred_element_type=f32)
    if fits:
        attended = line.arrive([all_fc2], attended)
        all_fc2.fourth()
        attended = line(attended)
    middle = tokens + gamma_one * attended
    second, modulate_two = jax.vjp(modulate, middle, scale_two, shift_two)
    if not fits:
        upstream = cotangent[0].astype(f32) * valid
        d_branch = (upstream * gamma_two).astype(bf16)
        give = half_columns(d_branch, 1 - here["c"])
    second_low = line(second.astype(bf16))
    second_other = grid.shift(second_low, "c", 1)
    if fits:
        wide_fc1, slope, activated_low = gather_dot(
            place, second_low, pieces_rest, half_proj, half_fc1, [bf16, bf16], True, "gather_fc1"
        )
        activated_low, gradient = line(activated_low, cotangent[0])
        upstream = gradient.astype(f32) * valid
        d_branch = (upstream * gamma_two).astype(bf16)
        give = half_columns(d_branch, 1 - here["c"])
        slope, activated_low, second_other, d_branch, give = line.arrive(
            [all_fc2], slope, activated_low, second_other, d_branch, give
        )
        pieces_fc2 = all_fc2.pieces()
        pieces_fc2[4:] = line(pieces_fc2[4:])
    else:
        wide_fc1 = lax.all_gather(cast_fc1, AXES, axis=0, tiled=True)
        inner = jnp.dot(second_low, wide_fc1, preferred_element_type=f32)
        slope, activated = gelu_and_slope(inner)
        activated_low = activated.astype(bf16)
    activated_low, context = line(activated_low, context)
    activated_other = grid.shift(activated_low, "c", 1)
    context_other = grid.shift(context, "c", 1)
    take = grid.shift(give, "c", 1)
    if fits:
        rows_in, rows_out = w_qkv.shape[0], w_fc2.shape[0]
        d_branch = line(d_branch)
        d_inner_low, give, activated_other, take, context_other = line(
            *gelu_back_dot(place, d_branch, slope, pieces_fc2), activated_other, take, context_other
        )
        pair_fc2 = (activated_low, activated_other, d_branch, take, 1)
        sum_two = GradSum(grid, line, here, place, [pair_fc2], rows_out, 256)
    else:
        wide_fc2 = lax.all_gather(cast_fc2, AXES, axis=0, tiled=True)
        sum_fc2 = weight_grad(activated_low, activated_other, d_branch, take, 1)
        d_inner_low = (contract_cols(d_branch, wide_fc2) * slope).astype(bf16)
        give = half_columns(d_inner_low, 1 - here["c"])
    take_inner = grid.shift(give, "c", 1)
    d_inner_low = line(d_inner_low)
    if fits:
        rows = [1.0 + scale_two, gamma_one, jnp.zeros((6, width), f32)]
        d_middle, d_attended, give, d_context, sums = line(
            *modulate_back(
                place,
                d_inner_low,
                wide_fc1,
                jnp.concatenate(rows, axis=0),
                middle,
                cotangent[0],
                attended,
                wide_proj,
            )
        )
        d_scale_two, d_shift_two, d_gamma_one = sums[0:1], sums[1:2], sums[2:3]
    else:
        d_second = contract_cols(d_inner_low, wide_fc1)
        d_middle_part, d_scale_two, d_shift_two = modulate_two(d_second)
        d_middle = upstream + d_middle_part
        d_gamma_one = jnp.sum(d_middle * attended, axis=0, keepdims=True)
        d_attended = (d_middle * gamma_one).astype(bf16)
        give = half_columns(d_attended, 1 - here["c"])
        d_context = contract_cols(d_attended, wide_proj).astype(bf16)
    take = grid.shift(give, "c", 1)
    if fits:
        take, take_inner = line.arrive([sum_two], take, take_inner)
        sum_two.second()
    pair_fc1 = (second_low, second_other, d_inner_low, take_inner, 1)
    pair_proj = (context, context_other, d_attended, take, 1)
    if fits:
        sum_mid = GradSum(
            grid, line, here, place, [pair_fc1, pair_proj], rows_in, 256, [sum_two]
        )
        sum_two.third()
    else:
        sum_fc1, sum_proj = weight_grad(*pair_fc1), weight_grad(*pair_proj)
    d_context = line(d_context)
    d_packed, give = attend_backward(place, packed, d_context, lse, bias_t)
    if fits:
        d_packed, give = line.arrive([sum_two, sum_mid], d_packed, give)
    take = grid.shift(give, "c", 1)
    if fits:
        sum_mid.second()
        sum_two.fourth()
        take = line(take)
        pair_qkv = (hidden_low, hidden_other, d_packed, take, 3)
        sum_last = GradSum(
            grid, line, here, place, [pair_qkv], rows_in, 256, [sum_two, sum_mid]
        )
        sum_mid.third()
        sum_two.fifth()
    else:
        sum_qkv = weight_grad(hidden_low, hidden_other, d_packed, take, 3)
    d_packed = line(d_packed)
    if fits:
        rows = [1.0 + scale_one, jnp.zeros((7, width), f32)]
        grad_in, sums = line(
            *modulate_back(
                place, d_packed, wide_qkv, jnp.concatenate(rows, axis=0), block_in[0], d_middle
            )
        )
        d_scale_one, d_shift_one = sums[0:1], sums[1:2]
    else:
        d_hidden = contract_cols(d_packed, wide_qkv)
        d_tokens, d_scale_one, d_shift_one = modulate_one(d_hidden)
        grad_in = d_middle + d_tokens
    if fits:
        line.arrive([sum_last, sum_mid])
        sum_last.second()
        sum_mid.fourth()
        activated_low = line(activated_low)
        (branch,) = gather_dot(
            place, activated_low, pieces_fc2, 0, width // 2, [f32], False, "gather_fc2"
        )
        branch = line.arrive([sum_last, sum_mid], branch)
        sum_last.third()
        sum_mid.fifth()
        branch = line(branch)
    else:
        branch = jnp.dot(activated_low, wide_fc2, preferred_element_type=f32)
    block_out = ((middle + gamma_two * branch) * valid).astype(bf16)
    d_gamma_two = jnp.sum(upstream * branch, axis=0, keepdims=True)
    d_ada = jnp.concatenate(
        [d_gamma_one, d_scale_one, d_shift_one, d_gamma_two, d_scale_two, d_shift_two], axis=0
    ).astype(bf16)
    every_ada = grid.gather_all(line(d_ada.reshape(-1, 128)), flips[:1])
    if fits:
        every_ada = line.arrive([sum_last], every_ada)
        sum_last.fourth()
        for done in (sum_two, sum_mid):
            done.take, done.keep = line(done.take, done.keep)
    every_ada = grid.gather_all(every_ada, flips[1:2])
    if fits:
        every_ada = line.arrive([sum_last], every_ada)
        sum_last.fifth()
    every_ada = grid.gather_all(every_ada, flips[2:])
    every_ada = every_ada.reshape(grid.count, 6 * width)
    sum_ada = contract_rows(lifted_low, every_ada)
    (d_cond,) = silu_back(contract_cols(every_ada, cast_ada))
    sum_table = lax.dot_general(
        onehot.astype(f32), d_cond, (((0,), (0,)), ((), ())), precision=highest
    )
    if fits:
        (sum_fc2,) = sum_two.result()
        sum_fc1, sum_proj = sum_mid.result()
        (sum_qkv,) = sum_last.result()
        sum_qkv = sum_qkv + line.last[0, 0]
    counter = f32(STEP)
    bias_one = 1.0 - jnp.power(f32(0.5), counter)
    bias_two = 1.0 - jnp.power(f32(0.5), counter)
    rates = learn_rates()
    updates = [
        adamw(w, g, m, v, bias_one, bias_two, rate)
        for w, g, m, v, rate in zip(
            (w_qkv, w_proj, w_fc1, w_fc2, w_ada, w_table),
            (sum_qkv, sum_proj, sum_fc1, sum_fc2, sum_ada, sum_table),
            (m_qkv, m_proj, m_fc1, m_fc2, m_ada, m_table),
            (v_qkv, v_proj, v_fc1, v_fc2, v_ada, v_table),
            rates,
        )
    ]
    return (block_out[None], grad_in[None]) + tuple(
        update[kind] for kind in range(4) for update in updates
    )


def solution(mesh):
    grid = Grid(mesh.shape["fsdp"], mesh.shape["grp"])
    items = P(AXES, None, None)
    vector = P(AXES)
    rows = P(AXES, None)
    columns = P(None, AXES)
    weights = (rows, rows, rows, rows, rows, columns)

    def run(*arrays):
        return per_device(grid, *arrays)

    return jax.shard_map(
        run,
        mesh=mesh,
        in_specs=(items, items, vector, vector) + weights * 3,
        out_specs=(items, items) + weights * 4,
        check_vma=False,
    )
```

```python
import functools

import jax
import jax.numpy as jnp
import numpy as np
from jax import lax
from jax.experimental import pallas as pl
from jax.experimental.pallas import tpu as pltpu
from jax.sharding import PartitionSpec as P

D = 1024
HEADS = 16
HEAD = 64
FF = 4096
SCALES = 10
STEP = 3
AXES = ("fsdp", "grp")

patch_sides = (1, 2, 3, 4, 5, 6, 8, 10, 13, 16)
norm_eps = 1e-06
adam_eps = 1e-08
decay = 0.05
highest = lax.Precision.HIGHEST
bf16 = jnp.bfloat16
f32 = jnp.float32


def scale_layout(slots):
    squares = np.array(patch_sides[:SCALES], dtype=np.int64) ** 2
    bounds = np.cumsum(squares)
    scale_ids = np.searchsorted(bounds, np.arange(slots), side="right")
    return (bounds.astype(np.int32), scale_ids.astype(np.int32))


def norm_rows(values):
    centre = values - jnp.mean(values, axis=-1, keepdims=True)
    spread = jnp.mean(centre * centre, axis=-1, keepdims=True)
    return centre * lax.rsqrt(spread + norm_eps)


def modulate(values, scale_row, shift_row):
    return norm_rows(values) * (1.0 + scale_row) + shift_row


def gelu_tanh(values):
    return jax.nn.gelu(values, approximate=True)


def gelu_and_slope(v):
    root = np.float32(np.sqrt(2 / np.pi))
    cube = np.float32(0.044715) * root
    square = v * v
    t = jnp.tanh(v * (root + cube * square))
    half = 0.5 + 0.5 * t
    act = v * half
    return [half + act * ((1.0 - t) * (root + (3 * cube) * square)), act]


def learn_rates():
    return (D ** (-0.5), (D // 16) ** (-0.5), D ** (-0.5), FF ** (-0.5), D ** (-0.5), 1.0)


def adamw(weight, gradient, first, second, bias_one, bias_two, rate):
    first_new = 0.5 * first + 0.5 * gradient
    second_new = 0.5 * second + 0.5 * gradient * gradient
    update = first_new / bias_one / (jnp.sqrt(second_new / bias_two) + adam_eps) + decay * weight
    weight_new = weight - rate * update
    return (weight_new, weight_new.astype(bf16), first_new, second_new)


def contract_rows(former, latter):
    return lax.dot_general(former, latter, (((0,), (0,)), ((), ())), preferred_element_type=f32)


def contract_cols(former, latter):
    return lax.dot_general(former, latter, (((1,), (1,)), ((), ())), preferred_element_type=f32)


def dot_nt(former, latter):
    return lax.dot_general(former, latter, (((1,), (1,)), ((), ())), preferred_element_type=f32)


def dot_nn(former, latter):
    return lax.dot_general(former, latter, (((1,), (0,)), ((), ())), preferred_element_type=f32)


def dot_tn(former, latter):
    return lax.dot_general(former, latter, (((0,), (0,)), ((), ())), preferred_element_type=f32)


FORWARD_TILES = ((0, 240, 256), (240, 416, 432), (416, 680, 680))
BACKWARD_TILES = ((0, 128, 160), (128, 384, 432), (384, 680, 680))


def attend_kernel(q_ref, k_ref, v_ref, bias_ref, context_ref, lse_ref):
    for begin, end, keys in FORWARD_TILES:
        q = q_ref[begin:end, :] * bf16(0.125)
        lane = lax.broadcasted_iota(jnp.int32, q.shape, 1)
        contexts, totals = [], []
        for head in range(2):
            own = jnp.where((lane < HEAD) == (head == 0), q, bf16(0))
            scores = dot_nt(own, k_ref[:keys, :]) + bias_ref[begin:end, :keys]
            largest = jnp.max(scores, axis=1, keepdims=True)
            expo = jnp.exp(scores - largest)
            total = jnp.sum(expo, axis=1, keepdims=True)
            probs = (expo * (1.0 / total)).astype(bf16)
            totals.append(largest + jnp.log(total))
            contexts.append(dot_nn(probs, v_ref[:keys, :]))
        left = lax.broadcasted_iota(jnp.int32, contexts[0].shape, 1) < HEAD
        context_ref[begin:end, :] = jnp.where(left, contexts[0], contexts[1]).astype(bf16)
        lse = jnp.where(left, totals[0], totals[1]).T
        lse_ref[0, 0:1, begin:end] = lse[0:1]
        lse_ref[0, 1:2, begin:end] = lse[HEAD : HEAD + 1]


def attend_forward(packed, bias, begin, end, so_far=None):
    slots, width = packed.shape[0], packed.shape[1] // 3
    pairs = width // 128
    assert slots == FORWARD_TILES[-1][1]

    def block(offset):
        return pl.BlockSpec((slots, 128), lambda i: (0, offset + begin + i))

    more = list(so_far) if so_far else []

    def kernel(q_ref, k_ref, v_ref, bias_ref, *refs):
        attend_kernel(q_ref, k_ref, v_ref, bias_ref, *refs[len(more) :])

    return pl.pallas_call(
        kernel,
        grid=(end - begin,),
        in_specs=[
            block(0),
            block(pairs),
            block(2 * pairs),
            pl.BlockSpec((slots, slots), lambda i: (0, 0), pipeline_mode=pl.Buffered(1)),
        ]
        + [pl.BlockSpec(memory_space=pl.ANY)] * len(more),
        out_specs=[block(0), pl.BlockSpec((1, 2, slots), lambda i: (begin + i, 0, 0))],
        out_shape=[
            jax.ShapeDtypeStruct((slots, width), bf16),
            jax.ShapeDtypeStruct((pairs, 2, slots), f32),
        ],
        input_output_aliases={4 + i: i for i in range(len(more))},
        cost_estimate=estimate(
            flops=5 * slots * slots * width,
            bytes_accessed=6 * slots * width,
            transcendentals=slots * slots * HEADS // 2,
        ),
        compiler_params=pltpu.CompilerParams(vmem_limit_bytes=20 << 20),
        name="attend",
    )(packed, packed, packed, bias, *more)


def attend_back_kernel(
    half, place_ref, q_ref, k_ref, v_ref, grad_ref, lse_ref, bias_ref, out_ref, give_ref, *refs
):
    keys_ref, values_ref, y_ref, out_sems, give_sems = refs
    step = pl.program_id(0)
    slot = lax.rem(step, 2)
    width = 2 * half * 128

    def copies(step, slot, run):
        pair = lax.rem(step + (1 - place_ref[2]) * half, 2 * half)
        for i in range(3):
            at = pl.multiple_of(i * width + pair * 128, 128)
            run(
                pltpu.make_async_copy(
                    y_ref.at[slot, i], out_ref.at[:, pl.ds(at, 128)], out_sems.at[slot, i]
                )
            )

        @pl.when(step < half)
        def _():
            for i in range(3):
                at = pl.multiple_of((i * half + step) * 128, 128)
                run(
                    pltpu.make_async_copy(
                        y_ref.at[slot, i], give_ref.at[:, pl.ds(at, 128)], give_sems.at[slot, i]
                    )
                )

    @pl.when(step >= 2)
    def _():
        copies(step - 2, slot, lambda copy: copy.wait())

    for count, (begin, end, keys) in enumerate(reversed(BACKWARD_TILES)):
        q = q_ref[begin:end, :] * bf16(0.125)
        grad = grad_ref[begin:end, :]
        k = k_ref[:keys, :]
        v = v_ref[:keys, :]
        left = lax.broadcasted_iota(jnp.int32, q.shape, 1) < HEAD
        d_q, d_k, d_v = [], [], []
        for head in range(2):
            own = left == (head == 0)
            scores = dot_nt(k, jnp.where(own, q, bf16(0))) + bias_ref[:keys, begin:end]
            probs = jnp.exp(scores - lse_ref[0, head : head + 1, begin:end])
            d_probs = dot_nt(v, jnp.where(own, grad, bf16(0)))
            inner = jnp.sum(probs * d_probs, axis=0, keepdims=True)
            d_scores = (probs * (d_probs - inner)).astype(bf16)
            d_v.append(dot_nn(probs.astype(bf16), grad))
            d_k.append(dot_nn(d_scores, q))
            d_q.append(dot_tn(d_scores, k))
        first = lax.broadcasted_iota(jnp.int32, d_k[0].shape, 1) < HEAD
        d_k = jnp.where(first, d_k[0], d_k[1])
        d_v = jnp.where(first, d_v[0], d_v[1])
        if count == 0:
            keys_ref[:keys, :] = d_k
            values_ref[:keys, :] = d_v
        else:
            keys_ref[:keys, :] += d_k
            values_ref[:keys, :] += d_v
        y_ref[slot, 0, begin:end, :] = (jnp.where(left, d_q[0], d_q[1]) * 0.125).astype(bf16)
    y_ref[slot, 1] = keys_ref[...].astype(bf16)
    y_ref[slot, 2] = values_ref[...].astype(bf16)
    copies(step, slot, lambda copy: copy.start())

    @pl.when(step == 2 * half - 1)
    def _():
        copies(step - 1, 1 - slot, lambda copy: copy.wait())
        copies(step, slot, lambda copy: copy.wait())


def attend_backward(place, packed, d_context, lse, bias_t):
    slots, width = packed.shape[0], packed.shape[1] // 3
    pairs = width // 128
    half = pairs // 2
    assert slots == BACKWARD_TILES[-1][1] and pairs >= 2

    def at(i, place):
        return lax.rem(i + (1 - place[2]) * half, pairs)

    def block(offset):
        return pl.BlockSpec((slots, 128), lambda i, place: (0, offset + at(i, place)))

    return pl.pallas_call(
        functools.partial(attend_back_kernel, half),
        grid_spec=pltpu.PrefetchScalarGridSpec(
            num_scalar_prefetch=1,
            grid=(pairs,),
            in_specs=[
                block(0),
                block(pairs),
                block(2 * pairs),
                block(0),
                pl.BlockSpec((1, 2, slots), lambda i, place: (at(i, place), 0, 0)),
                pl.BlockSpec((slots, slots), lambda i, place: (0, 0), pipeline_mode=pl.Buffered(1)),
            ],
            out_specs=[pl.BlockSpec(memory_space=pl.ANY)] * 2,
            scratch_shapes=[
                pltpu.VMEM((slots, 128), f32),
                pltpu.VMEM((slots, 128), f32),
                pltpu.VMEM((2, 3, slots, 128), bf16),
                pltpu.SemaphoreType.DMA((2, 3)),
                pltpu.SemaphoreType.DMA((2, 3)),
            ],
        ),
        out_shape=[
            jax.ShapeDtypeStruct((slots, 3 * width), bf16),
            jax.ShapeDtypeStruct((slots, 3 * width // 2), bf16),
        ],
        cost_estimate=estimate(
            flops=20 * slots * slots * width,
            bytes_accessed=16 * slots * width,
            transcendentals=slots * slots * HEADS,
        ),
        compiler_params=pltpu.CompilerParams(vmem_limit_bytes=28 << 20),
        name="attend_back",
    )(place, packed, packed, packed, d_context, lse, bias_t)


def start_pieces(place_ref, pieces, w_ref, sems, rows, left, half, color):
    z, x, c, y = [place_ref[i] for i in range(4)]
    for far in range(2):
        for core in range(2):
            piece = pieces[core * 4 + far * 2 + color]
            for near in range(2):
                step_x, step_y = (far, near) if color == 0 else (near, far)
                for step in range(4):
                    at = (z ^ FLIPS[step]) * 2 + (x ^ step_x)
                    at = (at * 2 + (c ^ core)) * 2 + (y ^ step_y)
                    at = pl.multiple_of(at * rows, rows)
                    pltpu.make_async_copy(
                        piece.at[near, step, :, pl.ds(left, half)],
                        w_ref.at[color, pl.ds(at, rows), :],
                        sems.at[color],
                    ).start()


def gather_kernel(layout, place_ref, x_ref, *refs):
    rows, left, half, chunk, gelu, keep = layout
    outs = 2 if gelu else 1
    pieces, refs = refs[:8], refs[8:]
    whole_ref, refs = (refs[0], refs[1:]) if keep else (None, refs)
    out_refs, w_ref, y_refs = refs[:outs], refs[outs], refs[outs + 1 : 2 * outs + 1]
    in_sems, whole_sems, out_sems = refs[2 * outs + 1 :]
    start = functools.partial(start_pieces, place_ref, pieces, w_ref, in_sems, rows, left, half)
    start(0)
    waits = []
    for color in range(2):
        own = w_ref.at[color]
        pltpu.make_async_copy(own, own, in_sems.at[color]).wait()
        if color == 0:
            start(1)
        if keep:
            copy = pltpu.make_async_copy(
                own, whole_ref.at[:, pl.ds(color * half, half)], whole_sems.at[color]
            )
            copy.start()
            waits.append(copy)
        def outs_of(at, run):
            for i in range(outs):
                run(
                    pltpu.make_async_copy(
                        y_refs[i].at[:, pl.ds(at, chunk)],
                        out_refs[i].at[:, pl.ds(at, chunk)],
                        out_sems.at[i, at // chunk],
                    )
                )

        def step(n, carry, color=color):
            begin = pl.multiple_of(n * chunk, chunk)
            at = pl.multiple_of(color * half + n * chunk, chunk)
            result = dot_nn(x_ref[...], w_ref[color, :, pl.ds(begin, chunk)])
            values = gelu_and_slope(result) if gelu else [result]
            for i, value in enumerate(values):
                y_refs[i][:, pl.ds(at, chunk)] = value.astype(y_refs[i].dtype)
            outs_of(at, lambda copy: copy.start())
            return carry

        lax.fori_loop(0, half // chunk, step, 0)
        for n in range(half // chunk):
            outs_of(color * half + n * chunk, lambda copy: waits.append(copy))
    for copy in waits:
        copy.wait()


def gather_dot(place, x, pieces, left, half, kinds, keep, name):
    rows = pieces[0].shape[2]
    whole, width = rows * 32, 2 * half
    slots = x.shape[0]
    chunk = min(512, half)
    anywhere = pl.BlockSpec(memory_space=pl.ANY)
    shapes = [jax.ShapeDtypeStruct((whole, width), bf16)] * keep
    shapes += [jax.ShapeDtypeStruct((slots, width), kind) for kind in kinds]
    return pl.pallas_call(
        functools.partial(gather_kernel, (rows, left, half, chunk, len(kinds) == 2, keep)),
        grid_spec=pltpu.PrefetchScalarGridSpec(
            num_scalar_prefetch=1,
            grid=(1,),
            in_specs=[pl.BlockSpec(x.shape, lambda i, place: (0, 0))] + [anywhere] * 8,
            out_specs=[anywhere] * len(shapes),
            scratch_shapes=[pltpu.VMEM((2, whole, half), bf16)]
            + [pltpu.VMEM((slots, width), kind) for kind in kinds]
            + [
                pltpu.SemaphoreType.DMA((2,)),
                pltpu.SemaphoreType.DMA((2,)),
                pltpu.SemaphoreType.DMA((len(kinds), width // chunk)),
            ],
        ),
        out_shape=shapes,
        cost_estimate=estimate(
            flops=3 * slots * whole * width,
            bytes_accessed=2 * whole * width + 4 * slots * width,
            transcendentals=0,
        ),
        compiler_params=pltpu.CompilerParams(vmem_limit_bytes=56 << 20),
        name=name,
    )(place, x, *pieces)


def modulate_back_kernel(steps, more, place_ref, x_ref, w_ref, rows_ref, *refs):
    value_hbm, add_hbm, refs = refs[0], refs[1], refs[2:]
    if more:
        attended_hbm, proj_hbm, refs = refs[0], refs[1], refs[2:]
        out_hbm, low_hbm, give_hbm, context_hbm, sums_ref, refs = *refs[:5], refs[5:]
        total_ref, value_ref, add_ref, attended_ref, proj_ref, low_ref, context_ref, sems = refs
    else:
        out_hbm, sums_ref, total_ref, value_ref, add_ref, sems = refs
    step = pl.program_id(0)
    pairs = [(value_hbm, value_ref), (add_hbm, add_ref)]
    if more:
        pairs += [(attended_hbm, attended_ref), (proj_hbm, proj_ref)]
    loads = [pltpu.make_async_copy(a, b, sems.at[i]) for i, (a, b) in enumerate(pairs)]
    part = dot_nt(x_ref[...], w_ref[...])

    for i, load in enumerate(loads):

        @pl.when(step == min(i, steps - 2))
        def _(load=load):
            load.start()

    @pl.when(step == 0)
    def _():
        total_ref[...] = part

    @pl.when(step > 0)
    def _():
        total_ref[...] += part

    @pl.when(step == steps - 1)
    def _():
        for load in loads:
            load.wait()
        slots, width = total_ref.shape
        gain = rows_ref[0:1, :]
        length = place_ref[4]

        def block(at, count, sums):
            value = value_ref[pl.ds(at, count), :].astype(f32)
            centre = value - jnp.mean(value, axis=1, keepdims=True)
            rate = lax.rsqrt(jnp.mean(centre * centre, axis=1, keepdims=True) + norm_eps)
            normal = centre * rate
            grad = total_ref[pl.ds(at, count), :]
            scaled = grad * gain
            inner = jnp.mean(scaled * normal, axis=1, keepdims=True)
            result = rate * (scaled - jnp.mean(scaled, axis=1, keepdims=True) - normal * inner)
            add = add_ref[pl.ds(at, count), :].astype(f32)
            sums = [
                sums[0] + jnp.sum(grad * normal, axis=0, keepdims=True),
                sums[1] + jnp.sum(grad, axis=0, keepdims=True),
            ] + sums[2:]
            if more:
                slot = at + lax.broadcasted_iota(jnp.int32, (count, 1), 0)
                add = add * (slot < length).astype(f32)
            result = add + result
            total_ref[pl.ds(at, count), :] = result
            if more:
                attended = attended_ref[pl.ds(at, count), :]
                sums[2] = sums[2] + jnp.sum(result * attended, axis=0, keepdims=True)
                low_ref[pl.ds(at, count), :] = (result * rows_ref[1:2, :]).astype(bf16)
            return sums

        count = 32
        whole = slots // count
        sums = [jnp.zeros((1, width), f32) for _ in range(3 if more else 2)]
        sums = lax.fori_loop(
            0, whole, lambda i, sums: block(pl.multiple_of(i * count, count), count, sums), sums
        )
        if slots % count:
            sums = block(whole * count, slots % count, sums)
        sums_ref[...] = jnp.concatenate(
            sums + [jnp.zeros((8 - len(sums), width), f32)], axis=0
        )
        stores = [pltpu.make_async_copy(total_ref, out_hbm, sems.at[4])]
        if more:
            half = width // 2
            other = pl.multiple_of((1 - place_ref[2]) * half, half)
            stores += [
                pltpu.make_async_copy(low_ref.at[:, pl.ds(other, half)], give_hbm, sems.at[5]),
                pltpu.make_async_copy(low_ref, low_hbm, sems.at[6]),
            ]
        for store in stores:
            store.start()
        if more:
            context_ref[...] = dot_nt(low_ref[...], proj_ref[...]).astype(bf16)
            stores.append(pltpu.make_async_copy(context_ref, context_hbm, sems.at[7]))
            stores[-1].start()
        for store in stores:
            store.wait()


def modulate_back(place, x, weight, rows, value, add, attended=None, proj=None):
    more = proj is not None
    slots, depth = x.shape
    width = weight.shape[0]
    chunk = 1024
    assert depth % chunk == 0
    anywhere = pl.BlockSpec(memory_space=pl.ANY)
    operands = [value, add] + ([attended, proj] if more else [])
    shapes = [jax.ShapeDtypeStruct((slots, width), f32)]
    scratch = [
        pltpu.VMEM((slots, width), f32),
        pltpu.VMEM((slots, width), value.dtype),
        pltpu.VMEM((slots, width), add.dtype),
    ]
    if more:
        shapes += [
            jax.ShapeDtypeStruct((slots, width), bf16),
            jax.ShapeDtypeStruct((slots, width // 2), bf16),
            jax.ShapeDtypeStruct((slots, width), bf16),
        ]
        scratch += [
            pltpu.VMEM((slots, width), f32),
            pltpu.VMEM(proj.shape, bf16),
            pltpu.VMEM((slots, width), bf16),
            pltpu.VMEM((slots, width), bf16),
        ]
    return pl.pallas_call(
        functools.partial(modulate_back_kernel, depth // chunk, more),
        grid_spec=pltpu.PrefetchScalarGridSpec(
            num_scalar_prefetch=1,
            grid=(depth // chunk,),
            in_specs=[
                pl.BlockSpec((slots, chunk), lambda i, place: (0, i)),
                pl.BlockSpec((width, chunk), lambda i, place: (0, i)),
                pl.BlockSpec((8, width), lambda i, place: (0, 0)),
            ]
            + [anywhere] * len(operands),
            out_specs=[anywhere] * len(shapes)
            + [pl.BlockSpec((8, width), lambda i, place: (0, 0))],
            scratch_shapes=scratch + [pltpu.SemaphoreType.DMA((8,))],
        ),
        out_shape=shapes + [jax.ShapeDtypeStruct((8, width), f32)],
        cost_estimate=estimate(
            flops=3 * slots * width * (depth + width * more),
            bytes_accessed=2 * (slots + width) * depth + 16 * slots * width,
            transcendentals=0,
        ),
        compiler_params=pltpu.CompilerParams(vmem_limit_bytes=48 << 20),
        name="modulate_back",
    )(place, x, weight, rows, *operands)


def gelu_back_kernel(rows, place_ref, grad_ref, slope_ref, *refs):
    pieces, (out_ref, give_ref), refs = refs[:8], refs[8:10], refs[10:]
    w_ref, s_ref, y_ref, in_sems, s_sems, y_sems, give_sems = refs
    z, x, c, y = [place_ref[i] for i in range(4)]
    block = 4 * rows
    chunks = [(step, far_x) for step in range(4) for far_x in range(2)]
    where = [
        pl.multiple_of(((z ^ FLIPS[step]) * 2 + (x ^ far_x)) * block, block) for step, far_x in chunks
    ]
    half = pieces[0].shape[-1]

    def start(n):
        step, far_x = chunks[n]
        for core in range(2):
            for far_y in range(2):
                at = pl.multiple_of(((c ^ core) * 2 + (y ^ far_y)) * rows, rows)
                for color in range(2):
                    far, near = (far_x, far_y) if color == 0 else (far_y, far_x)
                    pltpu.make_async_copy(
                        pieces[core * 4 + far * 2 + color].at[near, step],
                        w_ref.at[n, pl.ds(at, rows), pl.ds(color * half, half)],
                        in_sems.at[n],
                    ).start()
        pltpu.make_async_copy(
            slope_ref.at[:, pl.ds(where[n], block)], s_ref.at[n], s_sems.at[n]
        ).start()

    def give(n, run):
        @pl.when(lax.shift_right_logical(z ^ FLIPS[chunks[n][0]], 1) != c)
        def _():
            at = pl.multiple_of(where[n] - (1 - c) * (4 * block), block)
            run(
                pltpu.make_async_copy(
                    y_ref.at[n], give_ref.at[:, pl.ds(at, block)], give_sems.at[n]
                )
            )

    ahead = 2
    for n in range(ahead):
        start(n)
    waits = []
    for n in range(len(chunks)):
        pltpu.make_async_copy(w_ref.at[n], w_ref.at[n], in_sems.at[n]).wait()
        pltpu.make_async_copy(s_ref.at[n], s_ref.at[n], s_sems.at[n]).wait()
        if n + ahead < len(chunks):
            start(n + ahead)
        y_ref[n] = (dot_nt(grad_ref[...], w_ref[n]) * s_ref[n].astype(f32)).astype(bf16)
        copy = pltpu.make_async_copy(
            y_ref.at[n], out_ref.at[:, pl.ds(where[n], block)], y_sems.at[n]
        )
        copy.start()
        waits.append(copy)
        give(n, lambda copy: copy.start())
    for n in range(len(chunks)):
        give(n, lambda copy: copy.wait())
    for copy in waits:
        copy.wait()


def gelu_back_dot(place, grad, slope, pieces):
    slots, width = slope.shape
    rows = pieces[0].shape[2]
    assert width == 32 * rows and grad.shape[1] == 2 * pieces[0].shape[3]
    anywhere = pl.BlockSpec(memory_space=pl.ANY)
    block = 4 * rows
    return pl.pallas_call(
        functools.partial(gelu_back_kernel, rows),
        grid_spec=pltpu.PrefetchScalarGridSpec(
            num_scalar_prefetch=1,
            grid=(1,),
            in_specs=[pl.BlockSpec(grad.shape, lambda i, place: (0, 0))] + [anywhere] * 9,
            out_specs=[anywhere] * 2,
            scratch_shapes=[
                pltpu.VMEM((8, block, grad.shape[1]), bf16),
                pltpu.VMEM((8, slots, block), slope.dtype),
                pltpu.VMEM((8, slots, block), bf16),
            ]
            + [pltpu.SemaphoreType.DMA((8,))] * 4,
        ),
        out_shape=[
            jax.ShapeDtypeStruct((slots, width), bf16),
            jax.ShapeDtypeStruct((slots, width // 2), bf16),
        ],
        cost_estimate=estimate(
            flops=3 * slots * width * grad.shape[1],
            bytes_accessed=8 * slots * width + 4 * width * grad.shape[1],
            transcendentals=0,
        ),
        compiler_params=pltpu.CompilerParams(vmem_limit_bytes=56 << 20),
        name="gelu_back",
    )(place, grad, slope, *pieces)


def weight_grad_kernel(depth, rows, turn, firsts, place_ref, *refs):
    products = len(firsts)
    ins, out_refs = refs[: 4 * products], refs[4 * products :]
    step = pl.program_id(0)
    inner = lax.rem(step, turn)

    def product(own_ref, other_ref, mine_ref, take_ref):
        total = dot_tn(own_ref[...], mine_ref[...]) + dot_tn(other_ref[...], take_ref[...])
        total = total.reshape(depth, 2, 2, 2, rows, total.shape[-1])

        @pl.when(step < turn)
        def _():
            first = place_ref[3] == 0
            for x in range(2):
                low, high = total[:, x, :, 0], total[:, x, :, 1]
                out_refs[0][x] = jnp.where(first, high, low).astype(bf16)
                out_refs[1][x] = jnp.where(first, low, high).astype(bf16)

        @pl.when(step >= turn)
        def _():
            first = place_ref[1] == 0
            for y in range(2):
                low, high = total[:, 0, :, y], total[:, 1, :, y]
                out_refs[2][y] = jnp.where(first, high, low).astype(bf16)
                out_refs[3][y] = jnp.where(first, low, high).astype(bf16)

    if products == 1:
        product(*ins)
        return
    for n, (begin, end) in enumerate(firsts):

        @pl.when((inner >= begin) & (inner < end))
        def _(n=n):
            product(*ins[4 * n : 4 * n + 4])


def weight_grad_call(place, products, rows, chunk):
    specs, operands, firsts = [], [], []
    turn = flops = 0
    for own, other, rhs, take, groups in products:
        slots, columns = rhs.shape[0], rhs.shape[1] // groups
        per = columns // 2 // chunk
        count = groups * per // 2
        assert groups * per % 2 == 0 and columns % (2 * chunk) == 0
        flops += 6 * slots * own.shape[1] * groups * columns // 2
        firsts.append((turn, turn + count))
        specs.append((per, count, turn))
        turn += count
        operands += [own, other, rhs, take]
    in_specs = []
    for (own, *_), (per, count, begin) in zip(products, specs):
        slots = own.shape[0]

        def which(i, count=count, begin=begin):
            color = i // turn
            return color * count + jnp.clip(i - color * turn - begin, 0, count - 1)

        once = pl.Buffered(1)
        in_specs += [pl.BlockSpec(own.shape, lambda i, place: (0, 0), pipeline_mode=once)] * 2
        in_specs.append(
            pl.BlockSpec(
                (slots, chunk),
                lambda i, place, which=which, per=per: (
                    0,
                    (which(i) // per * 2 + place[2]) * per + lax.rem(which(i), per),
                ),
            )
        )
        in_specs.append(
            pl.BlockSpec((slots, chunk), lambda i, place, which=which: (0, which(i)))
        )
    width = products[0][0].shape[1]
    depth = width // rows // 8
    block = (2, depth, 2, rows, chunk)
    early = pl.BlockSpec(block, lambda i, place: (0, 0, 0, 0, jnp.minimum(i, turn - 1)))
    late = pl.BlockSpec(block, lambda i, place: (0, 0, 0, 0, jnp.maximum(i - turn, 0)))
    shape = jax.ShapeDtypeStruct((2, depth, 2, rows, turn * chunk), bf16)
    return pl.pallas_call(
        functools.partial(weight_grad_kernel, depth, rows, turn, tuple(firsts)),
        grid_spec=pltpu.PrefetchScalarGridSpec(
            num_scalar_prefetch=1,
            grid=(2 * turn,),
            in_specs=in_specs,
            out_specs=[early, early, late, late],
        ),
        out_shape=[shape] * 4,
        cost_estimate=estimate(
            flops=flops,
            bytes_accessed=sum(2 * v.size for v in operands) + 4 * width * turn * chunk,
            transcendentals=0,
        ),
        compiler_params=pltpu.CompilerParams(vmem_limit_bytes=60 << 20),
        name="weight_grad",
    )(place, *operands)


def estimate(flops, bytes_accessed, transcendentals):
    return pl.CostEstimate(
        flops=flops // 64, bytes_accessed=bytes_accessed // 64, transcendentals=transcendentals // 64
    )


def weight_grad_rows_kernel(rows, place_ref, own_ref, other_ref, mine_ref, take_ref, *out_refs):
    total = dot_tn(own_ref[...], mine_ref[...]) + dot_tn(other_ref[...], take_ref[...])
    total = total.reshape(2, 2, 2, rows, total.shape[-1])
    half = total.shape[-1] // 2
    first_y, first_x = place_ref[3] == 0, place_ref[1] == 0
    for i in range(2):
        low, high = total[i, :, 0, :, :half], total[i, :, 1, :, :half]
        out_refs[0][i, 0] = jnp.where(first_y, high, low).astype(bf16)
        out_refs[1][i, 0] = jnp.where(first_y, low, high).astype(bf16)
        low, high = total[0, :, i, :, half:], total[1, :, i, :, half:]
        out_refs[2][i, 0] = jnp.where(first_x, high, low).astype(bf16)
        out_refs[3][i, 0] = jnp.where(first_x, low, high).astype(bf16)


def weight_grad_rows(place, own, other, rhs, take, rows):
    slots, width = own.shape
    half = take.shape[1]
    depth = width // rows // 8
    out = pl.BlockSpec((2, 1, 2, rows, half // 2), lambda i, place: (0, i, 0, 0, 0))
    by_z = pl.BlockSpec((slots, 8 * rows), lambda i, place: (0, i))
    shape = jax.ShapeDtypeStruct((2, depth, 2, rows, half // 2), bf16)
    return pl.pallas_call(
        functools.partial(weight_grad_rows_kernel, rows),
        grid_spec=pltpu.PrefetchScalarGridSpec(
            num_scalar_prefetch=1,
            grid=(depth,),
            in_specs=[
                by_z,
                by_z,
                pl.BlockSpec((slots, half), lambda i, place: (0, place[2])),
                pl.BlockSpec((slots, half), lambda i, place: (0, 0)),
            ],
            out_specs=[out] * 4,
        ),
        out_shape=[shape] * 4,
        cost_estimate=estimate(
            flops=4 * slots * width * half,
            bytes_accessed=4 * slots * (width + half) + 2 * width * half,
            transcendentals=0,
        ),
        compiler_params=pltpu.CompilerParams(vmem_limit_bytes=60 << 20),
        name="weight_grad_rows",
    )(place, own, other, rhs, take)


class Line:
    def __init__(self):
        self.last = jnp.zeros((8, 128), f32)

    def __call__(self, *values):
        self.last, values = lax.optimization_barrier((self.last, values))
        return values[0] if len(values) == 1 else values

    def arrive(self, movers, *values):
        gots, values = self([mover.got for mover in movers], values)
        for mover, got in zip(movers, gots):
            mover.got = got
        return values[0] if len(values) == 1 else values


class Scatter:
    def __init__(self, grid, line, rows):
        self.grid, self.line, self.flips = grid, line, grid.bits()
        self.rows = rows.reshape([2] * len(self.flips) + list(rows.shape[1:]))

    def start(self):
        dim = len(self.flips) - 1
        axis, bit = self.flips.pop(0)
        self.own = lax.index_in_dim(self.rows, 0, dim, keepdims=False)
        away = self.line(lax.index_in_dim(self.rows, 1, dim, keepdims=False))
        self.got = self.grid.flip(away, axis, bit)

    def add(self):
        self.rows = self.own + self.got


class Gather:
    orders = ("yx", "xy")

    def __init__(self, grid, line, shards):
        self.grid, self.line = grid, line
        lows = [shard[:, : shard.shape[1] // 2] for shard in shards]
        highs = [shard[:, shard.shape[1] // 2 :] for shard in shards]
        self.shard = jnp.concatenate(lows + highs, axis=1)

    def first(self):
        self.shard = self.line(self.shard)
        self.got = self.grid.flip(self.shard, "z", 2)

    def second(self):
        self.pair = self.line(jnp.stack([self.shard, self.got]))
        self.got = self.grid.flip(self.pair, "z", 1)

    def third(self):
        half = self.shard.shape[1] // 2
        pairs = (self.pair, self.got)
        rows = [
            jnp.concatenate([p[:, :, i * half : (i + 1) * half] for p in pairs], axis=0)
            for i in range(2)
        ]
        self.rows = self.line(*rows)
        self.got = [self.grid.flip(v, o[0], 1) for v, o in zip(self.rows, self.orders)]

    def fourth(self):
        plane = [
            jnp.concatenate([own[None], new[None]], axis=0) for own, new in zip(self.rows, self.got)
        ]
        self.plane = self.line(*plane)
        self.got = [self.grid.flip(v, o[1], 1) for v, o in zip(self.plane, self.orders)]
        self.near = [self.grid.flip(v, "c", 1) for v in self.plane]

    def pieces(self):
        far = [self.grid.flip(v, "c", 1) for v in self.got]
        return list(self.plane) + list(self.got) + list(self.near) + far


FLIPS = (0, 2, 1, 3)


def add_split_kernel(joined, place_ref, *refs):
    sums = len(refs) // (5 if joined else 6)
    outs = refs[4 * sums :]
    for n in range(sums):
        for side in range(2):
            one, two = refs[4 * n + 2 * side], refs[4 * n + 2 * side + 1]
            out = outs[side] if joined else outs[2 * n + side]
            total = one[...].astype(f32) + two[...].astype(f32)
            if joined:
                width = total.shape[-1]
                out[..., n * width : (n + 1) * width] = total.astype(out.dtype)
            else:
                out[...] = total.reshape(out.shape).astype(out.dtype)


def add_split(place, name, steps, specs, *pairs, joined=False, kind=bf16):
    in_specs, operands, out_specs, shapes = [], [], [], []
    for n, pair in enumerate(pairs):
        lead = pair[0].ndim - 3
        if pair[0].ndim == 3:
            lead = 1
        tail = pair[0].shape[lead:]
        for side in range(2):
            for array in pair:
                in_specs.append(
                    pl.BlockSpec(
                        (1,) * lead + tail,
                        lambda i, place, n=n, side=side, zeros=(0,) * len(tail): (
                            specs(i, place)[n][side] + zeros
                        ),
                    )
                )
                operands.append(array)
            if joined and n:
                continue
            wide = tail[:-1] + (tail[-1] * (len(pairs) if joined else 1),)
            out_specs.append(
                pl.BlockSpec(
                    (1,) + wide, lambda i, place, zeros=(0,) * len(wide): (i,) + zeros
                )
            )
            shapes.append(jax.ShapeDtypeStruct((steps,) + wide, kind))
    return pl.pallas_call(
        functools.partial(add_split_kernel, joined),
        grid_spec=pltpu.PrefetchScalarGridSpec(
            num_scalar_prefetch=1, grid=(steps,), in_specs=in_specs, out_specs=out_specs
        ),
        out_shape=shapes,
        cost_estimate=estimate(
            flops=sum(array.size for array in operands),
            bytes_accessed=4 * sum(array.size for array in operands),
            transcendentals=0,
        ),
        compiler_params=pltpu.CompilerParams(vmem_limit_bytes=24 << 20),
        name=name,
    )(place, *operands)


class GradSum:
    def __init__(self, grid, line, here, place, products, rows, chunk, movers=()):
        self.grid, self.line, self.here, self.place, self.rows = grid, line, here, place, rows
        self.shapes = [(groups, rhs.shape[1] // groups) for _, _, rhs, _, groups in products]
        if len(products) == 1 and products[0][4] == 1:
            grads = weight_grad_rows(place, *products[0][:4], rows)
        else:
            grads = weight_grad_call(place, products, rows, chunk)
        away_one, self.one, away_two, self.two = line.arrive(movers, *grads)
        self.got = [grid.flip(away_one, "y", 1), grid.flip(away_two, "x", 1)]

    def second(self):
        away_one, self.one, away_two, self.two = self.line(
            *add_split(self.place, "add_second", 4, self.second_specs, *self.parts())
        )
        self.got = [self.grid.flip(away_one, "x", 1), self.grid.flip(away_two, "y", 1)]

    def parts(self):
        return [(self.one, self.got[0]), (self.two, self.got[1])]

    def second_specs(self, i, place):
        x, y = place[1], place[3]
        return [((1 - x, i), (x, i)), ((1 - y, i), (y, i))]

    def third(self):
        def specs(i, place):
            low = lax.rem(place[0], 2)
            pair = ((2 * i + 1 - low,), (2 * i + low,))
            return [pair, pair]

        away, self.both = self.line(
            *add_split(self.place, "add_third", 2, specs, *self.parts(), joined=True)
        )
        self.got = self.grid.flip(away, "z", 1)

    def fourth(self):
        def specs(i, place):
            high = place[0] // 2
            return [((1 - high,), (high,))]

        away, self.both = self.line(
            *add_split(self.place, "add_fourth", 1, specs, (self.both, self.got))
        )
        away, self.both = away[0], self.both[0]
        self.got = self.grid.flip(away, "z", 2)

    def fifth(self):
        def specs(i, place):
            return [((1 - place[2],), (place[2],))]

        give, self.keep = self.line(
            *add_split(self.place, "add_fifth", 1, specs, (self.both, self.got), kind=f32)
        )
        give, self.keep = give[0], self.keep[0]
        self.take = self.grid.flip(give, "c", 1)

    def result(self):
        first = self.here["c"] == 0
        low = jnp.where(first, self.keep, self.take)
        high = jnp.where(first, self.take, self.keep)
        sums, left, middle = [], 0, low.shape[1] // 2
        for groups, columns in self.shapes:
            part = groups * columns // 4
            half = columns // 2
            sides = []
            for side in (low, high):
                colors = [side[:, left : left + part], side[:, middle + left : middle + left + part]]
                sides.append(jnp.concatenate(colors, axis=1))
            spans = [side[:, g * half : (g + 1) * half] for g in range(groups) for side in sides]
            sums.append(jnp.concatenate(spans, axis=1))
            left += part
        return sums


class Grid:
    def __init__(self, fsdp, grp):
        outer = fsdp // 2
        self.size = {"c": 2, "x": 2 if outer % 2 == 0 else 1, "y": grp}
        self.size["z"] = outer // self.size["x"]
        self.count = fsdp * grp
        self.fsdp = fsdp

    def here(self):
        place = lax.axis_index("fsdp")
        wide = self.size["x"]
        return {
            "c": place % 2,
            "x": (place // 2) % wide,
            "z": place // (2 * wide),
            "y": lax.axis_index("grp"),
        }

    def shift(self, array, axis, step):
        size = self.size[axis]
        if axis == "y":
            return lax.ppermute(array, "grp", [(i, (i + step) % size) for i in range(size)])
        stride = {"c": 1, "x": 2, "z": 2 * self.size["x"]}[axis]
        pairs = []
        for i in range(self.fsdp):
            at = (i // stride) % size
            pairs.append((i, i + ((at + step) % size - at) * stride))
        return lax.ppermute(array, "fsdp", pairs)

    def fits(self, rows):
        size = self.size
        return size["x"] == 2 and size["y"] == 2 and size["z"] == 4 and rows % 32 == 0

    def bits(self):
        flips = []
        for axis in "cxyz":
            size = self.size[axis]
            assert size & (size - 1) == 0
            bit = size // 2
            while bit:
                flips.append((axis, bit))
                bit //= 2
        return flips

    def gather_all(self, row, flips):
        for axis, bit in flips:
            row = jnp.concatenate([row[None], self.flip(row, axis, bit)[None]], axis=0)
        return row

    def sources(self, here):
        flips = self.bits()
        turn = {axis: np.zeros(self.count, np.int32) for axis in "cxyz"}
        for n in range(self.count):
            for k, (axis, bit) in enumerate(flips):
                if n >> k & 1:
                    turn[axis][n] ^= bit
        z, x, c, y = [here[axis] ^ turn[axis] for axis in "zxcy"]
        return ((z * self.size["x"] + x) * 2 + c) * self.size["y"] + y

    def flip(self, array, axis, bit):
        size = self.size[axis]
        if axis == "y":
            return lax.ppermute(array, "grp", [(i, i ^ bit) for i in range(size)])
        stride = {"c": 1, "x": 2, "z": 2 * self.size["x"]}[axis]
        pairs = [
            (i, i + (((i // stride) % size ^ bit) - (i // stride) % size) * stride)
            for i in range(self.fsdp)
        ]
        return lax.ppermute(array, "fsdp", pairs)

    def scatter_sum(self, array, axis, dim, here, kind=bf16):
        size = self.size[axis]
        total = lax.dynamic_index_in_dim(array, here[axis], dim, keepdims=False)
        for step in range(1, size):
            piece = lax.dynamic_index_in_dim(array, (here[axis] + step) % size, dim, keepdims=False)
            total = total + self.shift(piece.astype(kind), axis, step).astype(f32)
        return total


def per_device(
    grid,
    block_in,
    cotangent,
    stop_scale,
    class_label,
    w_qkv,
    w_proj,
    w_fc1,
    w_fc2,
    w_ada,
    w_table,
    m_qkv,
    m_proj,
    m_fc1,
    m_fc2,
    m_ada,
    m_table,
    v_qkv,
    v_proj,
    v_fc1,
    v_fc2,
    v_ada,
    v_table,
):
    items, slots, width = block_in.shape
    assert items == 1
    here = grid.here()
    bounds, scale_ids = scale_layout(slots)
    picked = jnp.arange(SCALES) == stop_scale[0] - 1
    length = jnp.sum(jnp.where(picked, jnp.asarray(bounds), 0))
    position = jnp.arange(slots)
    valid = (position < length).astype(f32)[:, None]
    scale_table = jnp.asarray(scale_ids)

    def mask(length):
        allowed = (scale_table[None, :] <= scale_table[:, None]) & (position[None, :] < length)
        return jnp.where(allowed, f32(0), f32(-1e30))

    place = jnp.stack([here[axis] for axis in "zxcy"] + [length]).astype(jnp.int32)
    fits = grid.fits(w_qkv.shape[0])
    cast_qkv, cast_proj, cast_fc1, cast_fc2 = [
        w.astype(bf16) for w in (w_qkv, w_proj, w_fc1, w_fc2)
    ]
    half_qkv, half_proj, half_fc1 = [w.shape[1] // 2 for w in (w_qkv, w_proj, w_fc1)]
    line = Line()
    if fits:
        all_qkv = Gather(grid, line, [cast_qkv])
        all_qkv.first()
        place = line(place)
    labels = lax.all_to_all(
        jnp.broadcast_to(class_label, (grid.count,)), AXES, 0, 0, tiled=True
    )
    labels = jnp.take(labels, grid.sources(here))
    cast_ada = w_ada.astype(bf16)
    cast_table = w_table.astype(bf16)
    onehot = (labels[:, None] == jnp.arange(cast_table.shape[0])[None, :]).astype(bf16)
    cond = jnp.dot(onehot, cast_table, preferred_element_type=f32)
    silu_out, silu_back = jax.vjp(jax.nn.silu, cond)
    lifted_low = silu_out.astype(bf16)

    ada = jnp.dot(lifted_low, cast_ada, preferred_element_type=f32)
    flips = grid.bits()
    along = len(flips) - 2
    ada = Scatter(grid, line, ada.reshape(grid.count, -1, 128))
    if fits:
        ada.start()
        line.arrive([ada, all_qkv])
        ada.add()
        all_qkv.second()
        ada.start()
        line.arrive([ada])
        ada.add()
        line.arrive([all_qkv])
        all_qkv.third()
        all_rest = Gather(grid, line, [cast_proj, cast_fc1])
        all_rest.first()
        ada.start()
        line.arrive([ada])
        ada.add()
        line.arrive([all_qkv])
        all_qkv.fourth()
        ada.start()
        line.arrive([ada, all_rest])
        all_rest.second()
        ada.add()
        ada.start()
        bias = mask(line(length))
        bias, bias_t, all_qkv.near = line.arrive(
            [all_qkv, all_rest], bias, bias.T, all_qkv.near
        )
        pieces_qkv = all_qkv.pieces()
        all_rest.third()
        line.arrive([ada])
        ada.add()
    else:
        while ada.flips:
            ada.start()
            ada.add()
        bias = mask(length)
        bias_t = bias.T
    ada = ada.rows.reshape(1, 6 * width)
    gamma_one, scale_one, shift_one, gamma_two, scale_two, shift_two = [
        ada[:, i * width : (i + 1) * width] for i in range(6)
    ]

    def half_columns(rhs, core, groups=1):
        half = rhs.shape[1] // groups // 2
        parts = [
            lax.dynamic_slice_in_dim(rhs, (2 * i + core) * half, half, 1) for i in range(groups)
        ]
        return jnp.concatenate(parts, axis=1)

    def weight_grad(lhs, other_lhs, rhs, take, groups):
        half = take.shape[1]
        size = grid.size
        rows = lhs.shape[1] // grid.count
        mine = half_columns(rhs, here["c"], groups)
        both = jnp.concatenate([mine, take], axis=0)
        grad = contract_rows(jnp.concatenate([lhs, other_lhs], axis=0), both)
        grad = grad.reshape(size["z"], size["x"], 2, size["y"], rows, half)
        middle = half // 2
        one = grid.scatter_sum(grad[..., :middle], "y", 3, here)
        two = grid.scatter_sum(grad[..., middle:], "x", 1, here)
        one = grid.scatter_sum(one, "x", 1, here)
        two = grid.scatter_sum(two, "y", 2, here)
        both = grid.scatter_sum(jnp.concatenate([one, two], axis=-1), "z", 0, here)
        keep = lax.dynamic_index_in_dim(both, here["c"], 0, keepdims=False)
        give = lax.dynamic_index_in_dim(both, 1 - here["c"], 0, keepdims=False)
        take = grid.shift(give, "c", 1)
        low = jnp.where(here["c"] == 0, keep, take).reshape(rows, groups, 1, half // groups)
        high = jnp.where(here["c"] == 0, take, keep).reshape(rows, groups, 1, half // groups)
        return jnp.concatenate([low, high], axis=2).reshape(rows, 2 * half)

    tokens = block_in[0].astype(f32)
    hidden, modulate_one = jax.vjp(modulate, tokens, scale_one, shift_one)
    hidden_low = hidden.astype(bf16)
    if fits:
        hidden_low, pieces_qkv[4:] = line(hidden_low, pieces_qkv[4:])
        wide_qkv, packed = gather_dot(
            place, hidden_low, pieces_qkv, 0, half_qkv, [bf16], True, "gather_qkv"
        )
        packed = line.arrive([all_rest], packed)
        all_rest.fourth()
        all_fc2 = Gather(grid, line, [cast_fc2])
        all_fc2.first()
        packed = line(packed)
    else:
        wide_qkv = lax.all_gather(cast_qkv, AXES, axis=0, tiled=True)
        packed = jnp.dot(hidden_low, wide_qkv, preferred_element_type=f32).astype(bf16)
    pairs = width // 128
    heads = attend_forward(packed, bias, 0, pairs // 2)
    if fits:
        heads, all_rest.near = line.arrive([all_fc2], heads, all_rest.near)
        all_fc2.second()
    packed = line(packed)
    heads = attend_forward(packed, bias, pairs // 2, pairs, heads)
    if fits:
        heads = line.arrive([all_rest, all_fc2], *heads)
        pieces_rest = all_rest.pieces()
        all_fc2.third()
    context, lse = heads
    if fits:
        context, pieces_rest[4:] = line(context, pieces_rest[4:])
        wide_proj, attended = gather_dot(
            place, context, pieces_rest, 0, half_proj, [f32], True, "gather_proj"
        )
    else:
        wide_proj = lax.all_gather(cast_proj, AXES, axis=0, tiled=True)
        attended = jnp.dot(context, wide_proj, preferred_element_type=f32)
    if fits:
        attended = line.arrive([all_fc2], attended)
        all_fc2.fourth()
        attended = line(attended)
    middle = tokens + gamma_one * attended
    second, modulate_two = jax.vjp(modulate, middle, scale_two, shift_two)
    if not fits:
        upstream = cotangent[0].astype(f32) * valid
        d_branch = (upstream * gamma_two).astype(bf16)
        give = half_columns(d_branch, 1 - here["c"])
    second_low = line(second.astype(bf16))
    second_other = grid.shift(second_low, "c", 1)
    if fits:
        wide_fc1, slope, activated_low = gather_dot(
            place, second_low, pieces_rest, half_proj, half_fc1, [bf16, bf16], True, "gather_fc1"
        )
        activated_low, gradient = line(activated_low, cotangent[0])
        upstream = gradient.astype(f32) * valid
        d_branch = (upstream * gamma_two).astype(bf16)
        give = half_columns(d_branch, 1 - here["c"])
        slope, activated_low, second_other, d_branch, give = line.arrive(
            [all_fc2], slope, activated_low, second_other, d_branch, give
        )
        pieces_fc2 = all_fc2.pieces()
        pieces_fc2[4:] = line(pieces_fc2[4:])
    else:
        wide_fc1 = lax.all_gather(cast_fc1, AXES, axis=0, tiled=True)
        inner = jnp.dot(second_low, wide_fc1, preferred_element_type=f32)
        slope, activated = gelu_and_slope(inner)
        activated_low = activated.astype(bf16)
    activated_low, context, hidden_low = line(activated_low, context, hidden_low)
    activated_other = grid.shift(activated_low, "c", 1)
    context_other = grid.shift(context, "c", 1)
    hidden_other = grid.shift(hidden_low, "c", 1)
    take = grid.shift(give, "c", 1)
    if fits:
        rows_in, rows_out = w_qkv.shape[0], w_fc2.shape[0]
        d_branch = line(d_branch)
        d_inner_low, give, activated_other, take, context_other, hidden_other = line(
            *gelu_back_dot(place, d_branch, slope, pieces_fc2),
            activated_other,
            take,
            context_other,
            hidden_other,
        )
        pair_fc2 = (activated_low, activated_other, d_branch, take, 1)
        sum_two = GradSum(grid, line, here, place, [pair_fc2], rows_out, 256)
    else:
        wide_fc2 = lax.all_gather(cast_fc2, AXES, axis=0, tiled=True)
        sum_fc2 = weight_grad(activated_low, activated_other, d_branch, take, 1)
        d_inner_low = (contract_cols(d_branch, wide_fc2) * slope).astype(bf16)
        give = half_columns(d_inner_low, 1 - here["c"])
    take_inner = grid.shift(give, "c", 1)
    d_inner_low = line(d_inner_low)
    if fits:
        rows = [1.0 + scale_two, gamma_one, jnp.zeros((6, width), f32)]
        d_middle, d_attended, give, d_context, sums = line(
            *modulate_back(
                place,
                d_inner_low,
                wide_fc1,
                jnp.concatenate(rows, axis=0),
                middle,
                cotangent[0],
                attended,
                wide_proj,
            )
        )
        d_scale_two, d_shift_two, d_gamma_one = sums[0:1], sums[1:2], sums[2:3]
    else:
        d_second = contract_cols(d_inner_low, wide_fc1)
        d_middle_part, d_scale_two, d_shift_two = modulate_two(d_second)
        d_middle = upstream + d_middle_part
        d_gamma_one = jnp.sum(d_middle * attended, axis=0, keepdims=True)
        d_attended = (d_middle * gamma_one).astype(bf16)
        give = half_columns(d_attended, 1 - here["c"])
        d_context = contract_cols(d_attended, wide_proj).astype(bf16)
    take = grid.shift(give, "c", 1)
    if fits:
        take_inner = line.arrive([sum_two], take_inner)
        sum_two.second()
        take = line(take)
    pair_fc1 = (second_low, second_other, d_inner_low, take_inner, 1)
    pair_proj = (context, context_other, d_attended, take, 1)
    if fits:
        sum_mid = GradSum(
            grid, line, here, place, [pair_fc1, pair_proj], rows_in, 256, [sum_two]
        )
        sum_two.third()
    else:
        sum_fc1, sum_proj = weight_grad(*pair_fc1), weight_grad(*pair_proj)
    d_context = line(d_context)
    d_packed, give = attend_backward(place, packed, d_context, lse, bias_t)
    if fits:
        d_packed, give = line.arrive([sum_two, sum_mid], d_packed, give)
    take = grid.shift(give, "c", 1)
    if fits:
        sum_mid.second()
        sum_two.fourth()
        take = line(take)
        pair_qkv = (hidden_low, hidden_other, d_packed, take, 3)
        sum_last = GradSum(
            grid, line, here, place, [pair_qkv], rows_in, 256, [sum_two, sum_mid]
        )
        sum_mid.third()
        sum_two.fifth()
    else:
        sum_qkv = weight_grad(hidden_low, hidden_other, d_packed, take, 3)
    d_packed = line(d_packed)
    if fits:
        rows = [1.0 + scale_one, jnp.zeros((7, width), f32)]
        grad_in, sums = line(
            *modulate_back(
                place, d_packed, wide_qkv, jnp.concatenate(rows, axis=0), block_in[0], d_middle
            )
        )
        d_scale_one, d_shift_one = sums[0:1], sums[1:2]
    else:
        d_hidden = contract_cols(d_packed, wide_qkv)
        d_tokens, d_scale_one, d_shift_one = modulate_one(d_hidden)
        grad_in = d_middle + d_tokens
    if fits:
        line.arrive([sum_last, sum_mid])
        sum_last.second()
        sum_mid.fourth()
        activated_low = line(activated_low)
        (branch,) = gather_dot(
            place, activated_low, pieces_fc2, 0, width // 2, [f32], False, "gather_fc2"
        )
        branch = line.arrive([sum_last, sum_mid], branch)
        sum_last.third()
        sum_mid.fifth()
        branch = line(branch)
    else:
        branch = jnp.dot(activated_low, wide_fc2, preferred_element_type=f32)
    block_out = ((middle + gamma_two * branch) * valid).astype(bf16)
    d_gamma_two = jnp.sum(upstream * branch, axis=0, keepdims=True)
    d_ada = jnp.concatenate(
        [d_gamma_one, d_scale_one, d_shift_one, d_gamma_two, d_scale_two, d_shift_two], axis=0
    ).astype(bf16)
    every_ada = grid.gather_all(line(d_ada.reshape(-1, 128)), flips[:1])
    if fits:
        every_ada = line.arrive([sum_last], every_ada)
        sum_last.fourth()
        for done in (sum_two, sum_mid):
            done.take, done.keep = line(done.take, done.keep)
    every_ada = grid.gather_all(every_ada, flips[1:2])
    if fits:
        every_ada = line.arrive([sum_last], every_ada)
        sum_last.fifth()
    every_ada = grid.gather_all(every_ada, flips[2:])
    every_ada = every_ada.reshape(grid.count, 6 * width)
    sum_ada = contract_rows(lifted_low, every_ada)
    (d_cond,) = silu_back(contract_cols(every_ada, cast_ada))
    sum_table = lax.dot_general(
        onehot.astype(f32), d_cond, (((0,), (0,)), ((), ())), precision=highest
    )
    if fits:
        (sum_fc2,) = sum_two.result()
        sum_fc1, sum_proj = sum_mid.result()
        (sum_qkv,) = sum_last.result()
        sum_qkv = sum_qkv + line.last[0, 0]
    counter = f32(STEP)
    bias_one = 1.0 - jnp.power(f32(0.5), counter)
    bias_two = 1.0 - jnp.power(f32(0.5), counter)
    rates = learn_rates()
    updates = [
        adamw(w, g, m, v, bias_one, bias_two, rate)
        for w, g, m, v, rate in zip(
            (w_qkv, w_proj, w_fc1, w_fc2, w_ada, w_table),
            (sum_qkv, sum_proj, sum_fc1, sum_fc2, sum_ada, sum_table),
            (m_qkv, m_proj, m_fc1, m_fc2, m_ada, m_table),
            (v_qkv, v_proj, v_fc1, v_fc2, v_ada, v_table),
            rates,
        )
    ]
    return (block_out[None], grad_in[None]) + tuple(
        update[kind] for kind in range(4) for update in updates
    )


def solution(mesh):
    grid = Grid(mesh.shape["fsdp"], mesh.shape["grp"])
    items = P(AXES, None, None)
    vector = P(AXES)
    rows = P(AXES, None)
    columns = P(None, AXES)
    weights = (rows, rows, rows, rows, rows, columns)

    def run(*arrays):
        return per_device(grid, *arrays)

    return jax.shard_map(
        run,
        mesh=mesh,
        in_specs=(items, items, vector, vector) + weights * 3,
        out_specs=(items, items) + weights * 4,
        check_vma=False,
    )
```

```python
import functools

import jax
import jax.numpy as jnp
import numpy as np
from jax import lax
from jax.experimental import pallas as pl
from jax.experimental.pallas import tpu as pltpu
from jax.sharding import PartitionSpec as P

D = 1024
HEADS = 16
HEAD = 64
FF = 4096
SCALES = 10
STEP = 3
AXES = ("fsdp", "grp")

patch_sides = (1, 2, 3, 4, 5, 6, 8, 10, 13, 16)
norm_eps = 1e-06
adam_eps = 1e-08
decay = 0.05
highest = lax.Precision.HIGHEST
bf16 = jnp.bfloat16
f32 = jnp.float32


def scale_layout(slots):
    squares = np.array(patch_sides[:SCALES], dtype=np.int64) ** 2
    bounds = np.cumsum(squares)
    scale_ids = np.searchsorted(bounds, np.arange(slots), side="right")
    return (bounds.astype(np.int32), scale_ids.astype(np.int32))


def norm_rows(values):
    centre = values - jnp.mean(values, axis=-1, keepdims=True)
    spread = jnp.mean(centre * centre, axis=-1, keepdims=True)
    return centre * lax.rsqrt(spread + norm_eps)


def modulate(values, scale_row, shift_row):
    return norm_rows(values) * (1.0 + scale_row) + shift_row


def gelu_tanh(values):
    return jax.nn.gelu(values, approximate=True)


def gelu_and_slope(v):
    root = np.float32(np.sqrt(2 / np.pi))
    cube = np.float32(0.044715) * root
    square = v * v
    t = jnp.tanh(v * (root + cube * square))
    half = 0.5 + 0.5 * t
    act = v * half
    return [half + act * ((1.0 - t) * (root + (3 * cube) * square)), act]


def learn_rates():
    return (D ** (-0.5), (D // 16) ** (-0.5), D ** (-0.5), FF ** (-0.5), D ** (-0.5), 1.0)


def adamw(weight, gradient, first, second, bias_one, bias_two, rate):
    first_new = 0.5 * first + 0.5 * gradient
    second_new = 0.5 * second + 0.5 * gradient * gradient
    update = first_new / bias_one / (jnp.sqrt(second_new / bias_two) + adam_eps) + decay * weight
    weight_new = weight - rate * update
    return (weight_new, weight_new.astype(bf16), first_new, second_new)


def contract_rows(former, latter):
    return lax.dot_general(former, latter, (((0,), (0,)), ((), ())), preferred_element_type=f32)


def contract_cols(former, latter):
    return lax.dot_general(former, latter, (((1,), (1,)), ((), ())), preferred_element_type=f32)


def dot_nt(former, latter):
    return lax.dot_general(former, latter, (((1,), (1,)), ((), ())), preferred_element_type=f32)


def dot_nn(former, latter):
    return lax.dot_general(former, latter, (((1,), (0,)), ((), ())), preferred_element_type=f32)


def dot_tn(former, latter):
    return lax.dot_general(former, latter, (((0,), (0,)), ((), ())), preferred_element_type=f32)


FORWARD_TILES = ((0, 240, 256), (240, 416, 432), (416, 680, 680))
BACKWARD_TILES = ((0, 128, 160), (128, 384, 432), (384, 680, 680))


def attend_kernel(q_ref, k_ref, v_ref, bias_ref, context_ref, lse_ref):
    for begin, end, keys in FORWARD_TILES:
        q = q_ref[begin:end, :] * bf16(0.125)
        lane = lax.broadcasted_iota(jnp.int32, q.shape, 1)
        contexts, totals = [], []
        for head in range(2):
            own = jnp.where((lane < HEAD) == (head == 0), q, bf16(0))
            scores = dot_nt(own, k_ref[:keys, :]) + bias_ref[begin:end, :keys]
            largest = jnp.max(scores, axis=1, keepdims=True)
            expo = jnp.exp(scores - largest)
            total = jnp.sum(expo, axis=1, keepdims=True)
            probs = (expo * (1.0 / total)).astype(bf16)
            totals.append(largest + jnp.log(total))
            contexts.append(dot_nn(probs, v_ref[:keys, :]))
        left = lax.broadcasted_iota(jnp.int32, contexts[0].shape, 1) < HEAD
        context_ref[begin:end, :] = jnp.where(left, contexts[0], contexts[1]).astype(bf16)
        lse = jnp.where(left, totals[0], totals[1]).T
        lse_ref[0, 0:1, begin:end] = lse[0:1]
        lse_ref[0, 1:2, begin:end] = lse[HEAD : HEAD + 1]


def attend_forward(packed, bias, begin, end, so_far=None):
    slots, width = packed.shape[0], packed.shape[1] // 3
    pairs = width // 128
    assert slots == FORWARD_TILES[-1][1]

    def block(offset):
        return pl.BlockSpec((slots, 128), lambda i: (0, offset + begin + i))

    more = list(so_far) if so_far else []

    def kernel(q_ref, k_ref, v_ref, bias_ref, *refs):
        attend_kernel(q_ref, k_ref, v_ref, bias_ref, *refs[len(more) :])

    return pl.pallas_call(
        kernel,
        grid=(end - begin,),
        in_specs=[
            block(0),
            block(pairs),
            block(2 * pairs),
            pl.BlockSpec((slots, slots), lambda i: (0, 0), pipeline_mode=pl.Buffered(1)),
        ]
        + [pl.BlockSpec(memory_space=pl.ANY)] * len(more),
        out_specs=[block(0), pl.BlockSpec((1, 2, slots), lambda i: (begin + i, 0, 0))],
        out_shape=[
            jax.ShapeDtypeStruct((slots, width), bf16),
            jax.ShapeDtypeStruct((pairs, 2, slots), f32),
        ],
        input_output_aliases={4 + i: i for i in range(len(more))},
        cost_estimate=estimate(
            flops=5 * slots * slots * width,
            bytes_accessed=6 * slots * width,
            transcendentals=slots * slots * HEADS // 2,
        ),
        compiler_params=pltpu.CompilerParams(vmem_limit_bytes=20 << 20),
        name="attend",
    )(packed, packed, packed, bias, *more)


def attend_back_kernel(
    half, place_ref, q_ref, k_ref, v_ref, grad_ref, lse_ref, bias_ref, out_ref, give_ref, *refs
):
    keys_ref, values_ref, y_ref, out_sems, give_sems = refs
    step = pl.program_id(0)
    slot = lax.rem(step, 2)
    width = 2 * half * 128

    def copies(step, slot, run):
        pair = lax.rem(step + (1 - place_ref[2]) * half, 2 * half)
        for i in range(3):
            at = pl.multiple_of(i * width + pair * 128, 128)
            run(
                pltpu.make_async_copy(
                    y_ref.at[slot, i], out_ref.at[:, pl.ds(at, 128)], out_sems.at[slot, i]
                )
            )

        @pl.when(step < half)
        def _():
            for i in range(3):
                at = pl.multiple_of((i * half + step) * 128, 128)
                run(
                    pltpu.make_async_copy(
                        y_ref.at[slot, i], give_ref.at[:, pl.ds(at, 128)], give_sems.at[slot, i]
                    )
                )

    @pl.when(step >= 2)
    def _():
        copies(step - 2, slot, lambda copy: copy.wait())

    for count, (begin, end, keys) in enumerate(reversed(BACKWARD_TILES)):
        q = q_ref[begin:end, :] * bf16(0.125)
        grad = grad_ref[begin:end, :]
        k = k_ref[:keys, :]
        v = v_ref[:keys, :]
        left = lax.broadcasted_iota(jnp.int32, q.shape, 1) < HEAD
        d_q, d_k, d_v = [], [], []
        for head in range(2):
            own = left == (head == 0)
            scores = dot_nt(k, jnp.where(own, q, bf16(0))) + bias_ref[:keys, begin:end]
            probs = jnp.exp(scores - lse_ref[0, head : head + 1, begin:end])
            d_probs = dot_nt(v, jnp.where(own, grad, bf16(0)))
            inner = jnp.sum(probs * d_probs, axis=0, keepdims=True)
            d_scores = (probs * (d_probs - inner)).astype(bf16)
            d_v.append(dot_nn(probs.astype(bf16), grad))
            d_k.append(dot_nn(d_scores, q))
            d_q.append(dot_tn(d_scores, k))
        first = lax.broadcasted_iota(jnp.int32, d_k[0].shape, 1) < HEAD
        d_k = jnp.where(first, d_k[0], d_k[1])
        d_v = jnp.where(first, d_v[0], d_v[1])
        if count == 0:
            keys_ref[:keys, :] = d_k
            values_ref[:keys, :] = d_v
        else:
            keys_ref[:keys, :] += d_k
            values_ref[:keys, :] += d_v
        y_ref[slot, 0, begin:end, :] = (jnp.where(left, d_q[0], d_q[1]) * 0.125).astype(bf16)
    y_ref[slot, 1] = keys_ref[...].astype(bf16)
    y_ref[slot, 2] = values_ref[...].astype(bf16)
    copies(step, slot, lambda copy: copy.start())

    @pl.when(step == 2 * half - 1)
    def _():
        copies(step - 1, 1 - slot, lambda copy: copy.wait())
        copies(step, slot, lambda copy: copy.wait())


def attend_backward(place, packed, d_context, lse, bias_t):
    slots, width = packed.shape[0], packed.shape[1] // 3
    pairs = width // 128
    half = pairs // 2
    assert slots == BACKWARD_TILES[-1][1] and pairs >= 2

    def at(i, place):
        return lax.rem(i + (1 - place[2]) * half, pairs)

    def block(offset):
        return pl.BlockSpec((slots, 128), lambda i, place: (0, offset + at(i, place)))

    return pl.pallas_call(
        functools.partial(attend_back_kernel, half),
        grid_spec=pltpu.PrefetchScalarGridSpec(
            num_scalar_prefetch=1,
            grid=(pairs,),
            in_specs=[
                block(0),
                block(pairs),
                block(2 * pairs),
                block(0),
                pl.BlockSpec((1, 2, slots), lambda i, place: (at(i, place), 0, 0)),
                pl.BlockSpec((slots, slots), lambda i, place: (0, 0), pipeline_mode=pl.Buffered(1)),
            ],
            out_specs=[pl.BlockSpec(memory_space=pl.ANY)] * 2,
            scratch_shapes=[
                pltpu.VMEM((slots, 128), f32),
                pltpu.VMEM((slots, 128), f32),
                pltpu.VMEM((2, 3, slots, 128), bf16),
                pltpu.SemaphoreType.DMA((2, 3)),
                pltpu.SemaphoreType.DMA((2, 3)),
            ],
        ),
        out_shape=[
            jax.ShapeDtypeStruct((slots, 3 * width), bf16),
            jax.ShapeDtypeStruct((slots, 3 * width // 2), bf16),
        ],
        cost_estimate=estimate(
            flops=20 * slots * slots * width,
            bytes_accessed=16 * slots * width,
            transcendentals=slots * slots * HEADS,
        ),
        compiler_params=pltpu.CompilerParams(vmem_limit_bytes=28 << 20),
        name="attend_back",
    )(place, packed, packed, packed, d_context, lse, bias_t)


def start_pieces(place_ref, pieces, w_ref, sems, rows, left, half, color):
    z, x, c, y = [place_ref[i] for i in range(4)]
    for far in range(2):
        for core in range(2):
            piece = pieces[core * 4 + far * 2 + color]
            for near in range(2):
                step_x, step_y = (far, near) if color == 0 else (near, far)
                for step in range(4):
                    at = (z ^ FLIPS[step]) * 2 + (x ^ step_x)
                    at = (at * 2 + (c ^ core)) * 2 + (y ^ step_y)
                    at = pl.multiple_of(at * rows, rows)
                    pltpu.make_async_copy(
                        piece.at[near, step, :, pl.ds(left, half)],
                        w_ref.at[color, pl.ds(at, rows), :],
                        sems.at[color],
                    ).start()


def gather_kernel(layout, place_ref, x_ref, *refs):
    rows, left, half, chunk, gelu, keep = layout
    outs = 2 if gelu else 1
    pieces, refs = refs[:8], refs[8:]
    whole_ref, refs = (refs[0], refs[1:]) if keep else (None, refs)
    out_refs, w_ref, y_refs = refs[:outs], refs[outs], refs[outs + 1 : 2 * outs + 1]
    in_sems, whole_sems, out_sems = refs[2 * outs + 1 :]
    start = functools.partial(start_pieces, place_ref, pieces, w_ref, in_sems, rows, left, half)
    start(0)
    waits = []
    for color in range(2):
        own = w_ref.at[color]
        pltpu.make_async_copy(own, own, in_sems.at[color]).wait()
        if color == 0:
            start(1)
        if keep:
            copy = pltpu.make_async_copy(
                own, whole_ref.at[:, pl.ds(color * half, half)], whole_sems.at[color]
            )
            copy.start()
            waits.append(copy)
        def outs_of(at, run):
            for i in range(outs):
                run(
                    pltpu.make_async_copy(
                        y_refs[i].at[:, pl.ds(at, chunk)],
                        out_refs[i].at[:, pl.ds(at, chunk)],
                        out_sems.at[i, at // chunk],
                    )
                )

        def step(n, carry, color=color):
            begin = pl.multiple_of(n * chunk, chunk)
            at = pl.multiple_of(color * half + n * chunk, chunk)
            result = dot_nn(x_ref[...], w_ref[color, :, pl.ds(begin, chunk)])
            values = gelu_and_slope(result) if gelu else [result]
            for i, value in enumerate(values):
                y_refs[i][:, pl.ds(at, chunk)] = value.astype(y_refs[i].dtype)
            outs_of(at, lambda copy: copy.start())
            return carry

        lax.fori_loop(0, half // chunk, step, 0)
        for n in range(half // chunk):
            outs_of(color * half + n * chunk, lambda copy: waits.append(copy))
    for copy in waits:
        copy.wait()


def gather_dot(place, x, pieces, left, half, kinds, keep, name):
    rows = pieces[0].shape[2]
    whole, width = rows * 32, 2 * half
    slots = x.shape[0]
    chunk = min(512, half)
    anywhere = pl.BlockSpec(memory_space=pl.ANY)
    shapes = [jax.ShapeDtypeStruct((whole, width), bf16)] * keep
    shapes += [jax.ShapeDtypeStruct((slots, width), kind) for kind in kinds]
    return pl.pallas_call(
        functools.partial(gather_kernel, (rows, left, half, chunk, len(kinds) == 2, keep)),
        grid_spec=pltpu.PrefetchScalarGridSpec(
            num_scalar_prefetch=1,
            grid=(1,),
            in_specs=[pl.BlockSpec(x.shape, lambda i, place: (0, 0))] + [anywhere] * 8,
            out_specs=[anywhere] * len(shapes),
            scratch_shapes=[pltpu.VMEM((2, whole, half), bf16)]
            + [pltpu.VMEM((slots, width), kind) for kind in kinds]
            + [
                pltpu.SemaphoreType.DMA((2,)),
                pltpu.SemaphoreType.DMA((2,)),
                pltpu.SemaphoreType.DMA((len(kinds), width // chunk)),
            ],
        ),
        out_shape=shapes,
        cost_estimate=estimate(
            flops=3 * slots * whole * width,
            bytes_accessed=2 * whole * width + 4 * slots * width,
            transcendentals=0,
        ),
        compiler_params=pltpu.CompilerParams(vmem_limit_bytes=56 << 20),
        name=name,
    )(place, x, *pieces)


def modulate_back_kernel(steps, more, place_ref, x_ref, w_ref, rows_ref, *refs):
    value_hbm, add_hbm, refs = refs[0], refs[1], refs[2:]
    if more:
        attended_hbm, proj_hbm, refs = refs[0], refs[1], refs[2:]
        out_hbm, low_hbm, give_hbm, context_hbm, sums_ref, refs = *refs[:5], refs[5:]
        total_ref, value_ref, add_ref, attended_ref, proj_ref, low_ref, context_ref, sems = refs
    else:
        out_hbm, sums_ref, total_ref, value_ref, add_ref, sems = refs
    step = pl.program_id(0)
    pairs = [(value_hbm, value_ref), (add_hbm, add_ref)]
    if more:
        pairs += [(attended_hbm, attended_ref), (proj_hbm, proj_ref)]
    loads = [pltpu.make_async_copy(a, b, sems.at[i]) for i, (a, b) in enumerate(pairs)]
    part = dot_nt(x_ref[...], w_ref[...])

    for i, load in enumerate(loads):

        @pl.when(step == min(i, steps - 2))
        def _(load=load):
            load.start()

    @pl.when(step == 0)
    def _():
        total_ref[...] = part

    @pl.when(step > 0)
    def _():
        total_ref[...] += part

    @pl.when(step == steps - 1)
    def _():
        for load in loads:
            load.wait()
        slots, width = total_ref.shape
        gain = rows_ref[0:1, :]
        length = place_ref[4]

        def block(at, count, sums):
            value = value_ref[pl.ds(at, count), :].astype(f32)
            centre = value - jnp.mean(value, axis=1, keepdims=True)
            rate = lax.rsqrt(jnp.mean(centre * centre, axis=1, keepdims=True) + norm_eps)
            normal = centre * rate
            grad = total_ref[pl.ds(at, count), :]
            scaled = grad * gain
            inner = jnp.mean(scaled * normal, axis=1, keepdims=True)
            result = rate * (scaled - jnp.mean(scaled, axis=1, keepdims=True) - normal * inner)
            add = add_ref[pl.ds(at, count), :].astype(f32)
            sums = [
                sums[0] + jnp.sum(grad * normal, axis=0, keepdims=True),
                sums[1] + jnp.sum(grad, axis=0, keepdims=True),
            ] + sums[2:]
            if more:
                slot = at + lax.broadcasted_iota(jnp.int32, (count, 1), 0)
                add = add * (slot < length).astype(f32)
            result = add + result
            total_ref[pl.ds(at, count), :] = result
            if more:
                attended = attended_ref[pl.ds(at, count), :]
                sums[2] = sums[2] + jnp.sum(result * attended, axis=0, keepdims=True)
                low_ref[pl.ds(at, count), :] = (result * rows_ref[1:2, :]).astype(bf16)
            return sums

        count = 32
        whole = slots // count
        sums = [jnp.zeros((1, width), f32) for _ in range(3 if more else 2)]
        sums = lax.fori_loop(
            0, whole, lambda i, sums: block(pl.multiple_of(i * count, count), count, sums), sums
        )
        if slots % count:
            sums = block(whole * count, slots % count, sums)
        sums_ref[...] = jnp.concatenate(
            sums + [jnp.zeros((8 - len(sums), width), f32)], axis=0
        )
        stores = [pltpu.make_async_copy(total_ref, out_hbm, sems.at[4])]
        if more:
            half = width // 2
            other = pl.multiple_of((1 - place_ref[2]) * half, half)
            stores += [
                pltpu.make_async_copy(low_ref.at[:, pl.ds(other, half)], give_hbm, sems.at[5]),
                pltpu.make_async_copy(low_ref, low_hbm, sems.at[6]),
            ]
        for store in stores:
            store.start()
        if more:
            context_ref[...] = dot_nt(low_ref[...], proj_ref[...]).astype(bf16)
            stores.append(pltpu.make_async_copy(context_ref, context_hbm, sems.at[7]))
            stores[-1].start()
        for store in stores:
            store.wait()


def modulate_back(place, x, weight, rows, value, add, attended=None, proj=None):
    more = proj is not None
    slots, depth = x.shape
    width = weight.shape[0]
    chunk = 1024
    assert depth % chunk == 0
    anywhere = pl.BlockSpec(memory_space=pl.ANY)
    operands = [value, add] + ([attended, proj] if more else [])
    shapes = [jax.ShapeDtypeStruct((slots, width), f32)]
    scratch = [
        pltpu.VMEM((slots, width), f32),
        pltpu.VMEM((slots, width), value.dtype),
        pltpu.VMEM((slots, width), add.dtype),
    ]
    if more:
        shapes += [
            jax.ShapeDtypeStruct((slots, width), bf16),
            jax.ShapeDtypeStruct((slots, width // 2), bf16),
            jax.ShapeDtypeStruct((slots, width), bf16),
        ]
        scratch += [
            pltpu.VMEM((slots, width), f32),
            pltpu.VMEM(proj.shape, bf16),
            pltpu.VMEM((slots, width), bf16),
            pltpu.VMEM((slots, width), bf16),
        ]
    return pl.pallas_call(
        functools.partial(modulate_back_kernel, depth // chunk, more),
        grid_spec=pltpu.PrefetchScalarGridSpec(
            num_scalar_prefetch=1,
            grid=(depth // chunk,),
            in_specs=[
                pl.BlockSpec((slots, chunk), lambda i, place: (0, i)),
                pl.BlockSpec((width, chunk), lambda i, place: (0, i)),
                pl.BlockSpec((8, width), lambda i, place: (0, 0)),
            ]
            + [anywhere] * len(operands),
            out_specs=[anywhere] * len(shapes)
            + [pl.BlockSpec((8, width), lambda i, place: (0, 0))],
            scratch_shapes=scratch + [pltpu.SemaphoreType.DMA((8,))],
        ),
        out_shape=shapes + [jax.ShapeDtypeStruct((8, width), f32)],
        cost_estimate=estimate(
            flops=3 * slots * width * (depth + width * more),
            bytes_accessed=2 * (slots + width) * depth + 16 * slots * width,
            transcendentals=0,
        ),
        compiler_params=pltpu.CompilerParams(vmem_limit_bytes=48 << 20),
        name="modulate_back",
    )(place, x, weight, rows, *operands)


def gelu_back_kernel(rows, place_ref, grad_ref, slope_ref, *refs):
    pieces, (out_ref, give_ref), refs = refs[:8], refs[8:10], refs[10:]
    w_ref, s_ref, y_ref, in_sems, s_sems, y_sems, give_sems = refs
    z, x, c, y = [place_ref[i] for i in range(4)]
    block = 4 * rows
    chunks = [(step, far_x) for step in range(4) for far_x in range(2)]
    where = [
        pl.multiple_of(((z ^ FLIPS[step]) * 2 + (x ^ far_x)) * block, block) for step, far_x in chunks
    ]
    half = pieces[0].shape[-1]

    def start(n):
        step, far_x = chunks[n]
        for core in range(2):
            for far_y in range(2):
                at = pl.multiple_of(((c ^ core) * 2 + (y ^ far_y)) * rows, rows)
                for color in range(2):
                    far, near = (far_x, far_y) if color == 0 else (far_y, far_x)
                    pltpu.make_async_copy(
                        pieces[core * 4 + far * 2 + color].at[near, step],
                        w_ref.at[n, pl.ds(at, rows), pl.ds(color * half, half)],
                        in_sems.at[n],
                    ).start()
        pltpu.make_async_copy(
            slope_ref.at[:, pl.ds(where[n], block)], s_ref.at[n], s_sems.at[n]
        ).start()

    def give(n, run):
        @pl.when(lax.shift_right_logical(z ^ FLIPS[chunks[n][0]], 1) != c)
        def _():
            at = pl.multiple_of(where[n] - (1 - c) * (4 * block), block)
            run(
                pltpu.make_async_copy(
                    y_ref.at[n], give_ref.at[:, pl.ds(at, block)], give_sems.at[n]
                )
            )

    ahead = 2
    for n in range(ahead):
        start(n)
    waits = []
    for n in range(len(chunks)):
        pltpu.make_async_copy(w_ref.at[n], w_ref.at[n], in_sems.at[n]).wait()
        pltpu.make_async_copy(s_ref.at[n], s_ref.at[n], s_sems.at[n]).wait()
        if n + ahead < len(chunks):
            start(n + ahead)
        y_ref[n] = (dot_nt(grad_ref[...], w_ref[n]) * s_ref[n].astype(f32)).astype(bf16)
        copy = pltpu.make_async_copy(
            y_ref.at[n], out_ref.at[:, pl.ds(where[n], block)], y_sems.at[n]
        )
        copy.start()
        waits.append(copy)
        give(n, lambda copy: copy.start())
    for n in range(len(chunks)):
        give(n, lambda copy: copy.wait())
    for copy in waits:
        copy.wait()


def gelu_back_dot(place, grad, slope, pieces):
    slots, width = slope.shape
    rows = pieces[0].shape[2]
    assert width == 32 * rows and grad.shape[1] == 2 * pieces[0].shape[3]
    anywhere = pl.BlockSpec(memory_space=pl.ANY)
    block = 4 * rows
    return pl.pallas_call(
        functools.partial(gelu_back_kernel, rows),
        grid_spec=pltpu.PrefetchScalarGridSpec(
            num_scalar_prefetch=1,
            grid=(1,),
            in_specs=[pl.BlockSpec(grad.shape, lambda i, place: (0, 0))] + [anywhere] * 9,
            out_specs=[anywhere] * 2,
            scratch_shapes=[
                pltpu.VMEM((8, block, grad.shape[1]), bf16),
                pltpu.VMEM((8, slots, block), slope.dtype),
                pltpu.VMEM((8, slots, block), bf16),
            ]
            + [pltpu.SemaphoreType.DMA((8,))] * 4,
        ),
        out_shape=[
            jax.ShapeDtypeStruct((slots, width), bf16),
            jax.ShapeDtypeStruct((slots, width // 2), bf16),
        ],
        cost_estimate=estimate(
            flops=3 * slots * width * grad.shape[1],
            bytes_accessed=8 * slots * width + 4 * width * grad.shape[1],
            transcendentals=0,
        ),
        compiler_params=pltpu.CompilerParams(vmem_limit_bytes=56 << 20),
        name="gelu_back",
    )(place, grad, slope, *pieces)


def weight_grad_kernel(depth, rows, turn, firsts, place_ref, *refs):
    products = len(firsts)
    ins, out_refs = refs[: 4 * products], refs[4 * products :]
    step = pl.program_id(0)
    inner = lax.rem(step, turn)

    def product(own_ref, other_ref, mine_ref, take_ref):
        total = dot_tn(own_ref[...], mine_ref[...]) + dot_tn(other_ref[...], take_ref[...])
        total = total.reshape(depth, 2, 2, 2, rows, total.shape[-1])

        @pl.when(step < turn)
        def _():
            first = place_ref[3] == 0
            for x in range(2):
                low, high = total[:, x, :, 0], total[:, x, :, 1]
                out_refs[0][x] = jnp.where(first, high, low).astype(bf16)
                out_refs[1][x] = jnp.where(first, low, high).astype(bf16)

        @pl.when(step >= turn)
        def _():
            first = place_ref[1] == 0
            for y in range(2):
                low, high = total[:, 0, :, y], total[:, 1, :, y]
                out_refs[2][y] = jnp.where(first, high, low).astype(bf16)
                out_refs[3][y] = jnp.where(first, low, high).astype(bf16)

    if products == 1:
        product(*ins)
        return
    for n, (begin, end) in enumerate(firsts):

        @pl.when((inner >= begin) & (inner < end))
        def _(n=n):
            product(*ins[4 * n : 4 * n + 4])


def weight_grad_call(place, products, rows, chunk):
    specs, operands, firsts = [], [], []
    turn = flops = 0
    for own, other, rhs, take, groups in products:
        slots, columns = rhs.shape[0], rhs.shape[1] // groups
        per = columns // 2 // chunk
        count = groups * per // 2
        assert groups * per % 2 == 0 and columns % (2 * chunk) == 0
        flops += 6 * slots * own.shape[1] * groups * columns // 2
        firsts.append((turn, turn + count))
        specs.append((per, count, turn))
        turn += count
        operands += [own, other, rhs, take]
    in_specs = []
    for (own, *_), (per, count, begin) in zip(products, specs):
        slots = own.shape[0]

        def which(i, count=count, begin=begin):
            color = i // turn
            return color * count + jnp.clip(i - color * turn - begin, 0, count - 1)

        once = pl.Buffered(1)
        in_specs += [pl.BlockSpec(own.shape, lambda i, place: (0, 0), pipeline_mode=once)] * 2
        in_specs.append(
            pl.BlockSpec(
                (slots, chunk),
                lambda i, place, which=which, per=per: (
                    0,
                    (which(i) // per * 2 + place[2]) * per + lax.rem(which(i), per),
                ),
            )
        )
        in_specs.append(
            pl.BlockSpec((slots, chunk), lambda i, place, which=which: (0, which(i)))
        )
    width = products[0][0].shape[1]
    depth = width // rows // 8
    block = (2, depth, 2, rows, chunk)
    early = pl.BlockSpec(block, lambda i, place: (0, 0, 0, 0, jnp.minimum(i, turn - 1)))
    late = pl.BlockSpec(block, lambda i, place: (0, 0, 0, 0, jnp.maximum(i - turn, 0)))
    shape = jax.ShapeDtypeStruct((2, depth, 2, rows, turn * chunk), bf16)
    return pl.pallas_call(
        functools.partial(weight_grad_kernel, depth, rows, turn, tuple(firsts)),
        grid_spec=pltpu.PrefetchScalarGridSpec(
            num_scalar_prefetch=1,
            grid=(2 * turn,),
            in_specs=in_specs,
            out_specs=[early, early, late, late],
        ),
        out_shape=[shape] * 4,
        cost_estimate=estimate(
            flops=flops,
            bytes_accessed=sum(2 * v.size for v in operands) + 4 * width * turn * chunk,
            transcendentals=0,
        ),
        compiler_params=pltpu.CompilerParams(vmem_limit_bytes=60 << 20),
        name="weight_grad",
    )(place, *operands)


def estimate(flops, bytes_accessed, transcendentals):
    return pl.CostEstimate(
        flops=flops // 64, bytes_accessed=bytes_accessed // 64, transcendentals=transcendentals // 64
    )


def weight_grad_rows_kernel(rows, place_ref, own_ref, other_ref, mine_ref, take_ref, *out_refs):
    total = dot_tn(own_ref[...], mine_ref[...]) + dot_tn(other_ref[...], take_ref[...])
    total = total.reshape(2, 2, 2, rows, total.shape[-1])
    half = total.shape[-1] // 2
    first_y, first_x = place_ref[3] == 0, place_ref[1] == 0
    for i in range(2):
        low, high = total[i, :, 0, :, :half], total[i, :, 1, :, :half]
        out_refs[0][i, 0] = jnp.where(first_y, high, low).astype(bf16)
        out_refs[1][i, 0] = jnp.where(first_y, low, high).astype(bf16)
        low, high = total[0, :, i, :, half:], total[1, :, i, :, half:]
        out_refs[2][i, 0] = jnp.where(first_x, high, low).astype(bf16)
        out_refs[3][i, 0] = jnp.where(first_x, low, high).astype(bf16)


def weight_grad_rows(place, own, other, rhs, take, rows):
    slots, width = own.shape
    half = take.shape[1]
    depth = width // rows // 8
    out = pl.BlockSpec((2, 1, 2, rows, half // 2), lambda i, place: (0, i, 0, 0, 0))
    by_z = pl.BlockSpec((slots, 8 * rows), lambda i, place: (0, i))
    shape = jax.ShapeDtypeStruct((2, depth, 2, rows, half // 2), bf16)
    return pl.pallas_call(
        functools.partial(weight_grad_rows_kernel, rows),
        grid_spec=pltpu.PrefetchScalarGridSpec(
            num_scalar_prefetch=1,
            grid=(depth,),
            in_specs=[
                by_z,
                by_z,
                pl.BlockSpec((slots, half), lambda i, place: (0, place[2])),
                pl.BlockSpec((slots, half), lambda i, place: (0, 0)),
            ],
            out_specs=[out] * 4,
        ),
        out_shape=[shape] * 4,
        cost_estimate=estimate(
            flops=4 * slots * width * half,
            bytes_accessed=4 * slots * (width + half) + 2 * width * half,
            transcendentals=0,
        ),
        compiler_params=pltpu.CompilerParams(vmem_limit_bytes=60 << 20),
        name="weight_grad_rows",
    )(place, own, other, rhs, take)


class Line:
    def __init__(self):
        self.last = jnp.zeros((8, 128), f32)

    def __call__(self, *values):
        self.last, values = lax.optimization_barrier((self.last, values))
        return values[0] if len(values) == 1 else values

    def arrive(self, movers, *values):
        gots, values = self([mover.got for mover in movers], values)
        for mover, got in zip(movers, gots):
            mover.got = got
        return values[0] if len(values) == 1 else values


class Scatter:
    def __init__(self, grid, line, rows):
        self.grid, self.line, self.flips = grid, line, grid.bits()
        self.rows = rows.reshape([2] * len(self.flips) + list(rows.shape[1:]))

    def start(self):
        dim = len(self.flips) - 1
        axis, bit = self.flips.pop(0)
        self.own = lax.index_in_dim(self.rows, 0, dim, keepdims=False)
        away = self.line(lax.index_in_dim(self.rows, 1, dim, keepdims=False))
        self.got = self.grid.flip(away, axis, bit)

    def add(self):
        self.rows = self.own + self.got


class Gather:
    orders = ("yx", "xy")

    def __init__(self, grid, line, shards):
        self.grid, self.line = grid, line
        lows = [shard[:, : shard.shape[1] // 2] for shard in shards]
        highs = [shard[:, shard.shape[1] // 2 :] for shard in shards]
        self.shard = jnp.concatenate(lows + highs, axis=1)

    def first(self):
        self.shard = self.line(self.shard)
        self.got = self.grid.flip(self.shard, "z", 2)

    def second(self):
        self.pair = self.line(jnp.stack([self.shard, self.got]))
        self.got = self.grid.flip(self.pair, "z", 1)

    def third(self):
        half = self.shard.shape[1] // 2
        pairs = (self.pair, self.got)
        rows = [
            jnp.concatenate([p[:, :, i * half : (i + 1) * half] for p in pairs], axis=0)
            for i in range(2)
        ]
        self.rows = self.line(*rows)
        self.got = [self.grid.flip(v, o[0], 1) for v, o in zip(self.rows, self.orders)]

    def fourth(self):
        plane = [
            jnp.concatenate([own[None], new[None]], axis=0) for own, new in zip(self.rows, self.got)
        ]
        self.plane = self.line(*plane)
        self.got = [self.grid.flip(v, o[1], 1) for v, o in zip(self.plane, self.orders)]
        self.near = [self.grid.flip(v, "c", 1) for v in self.plane]

    def pieces(self):
        far = [self.grid.flip(v, "c", 1) for v in self.got]
        return list(self.plane) + list(self.got) + list(self.near) + far


FLIPS = (0, 2, 1, 3)


def add_split_kernel(joined, place_ref, *refs):
    sums = len(refs) // (5 if joined else 6)
    outs = refs[4 * sums :]
    for n in range(sums):
        for side in range(2):
            one, two = refs[4 * n + 2 * side], refs[4 * n + 2 * side + 1]
            out = outs[side] if joined else outs[2 * n + side]
            total = one[...].astype(f32) + two[...].astype(f32)
            if joined:
                width = total.shape[-1]
                out[..., n * width : (n + 1) * width] = total.astype(out.dtype)
            else:
                out[...] = total.reshape(out.shape).astype(out.dtype)


def add_split(place, name, steps, specs, *pairs, joined=False, kind=bf16):
    in_specs, operands, out_specs, shapes = [], [], [], []
    for n, pair in enumerate(pairs):
        lead = pair[0].ndim - 3
        if pair[0].ndim == 3:
            lead = 1
        tail = pair[0].shape[lead:]
        for side in range(2):
            for array in pair:
                in_specs.append(
                    pl.BlockSpec(
                        (1,) * lead + tail,
                        lambda i, place, n=n, side=side, zeros=(0,) * len(tail): (
                            specs(i, place)[n][side] + zeros
                        ),
                    )
                )
                operands.append(array)
            if joined and n:
                continue
            wide = tail[:-1] + (tail[-1] * (len(pairs) if joined else 1),)
            out_specs.append(
                pl.BlockSpec(
                    (1,) + wide, lambda i, place, zeros=(0,) * len(wide): (i,) + zeros
                )
            )
            shapes.append(jax.ShapeDtypeStruct((steps,) + wide, kind))
    return pl.pallas_call(
        functools.partial(add_split_kernel, joined),
        grid_spec=pltpu.PrefetchScalarGridSpec(
            num_scalar_prefetch=1, grid=(steps,), in_specs=in_specs, out_specs=out_specs
        ),
        out_shape=shapes,
        cost_estimate=estimate(
            flops=sum(array.size for array in operands),
            bytes_accessed=4 * sum(array.size for array in operands),
            transcendentals=0,
        ),
        compiler_params=pltpu.CompilerParams(vmem_limit_bytes=24 << 20),
        name=name,
    )(place, *operands)


class GradSum:
    def __init__(self, grid, line, here, place, products, rows, chunk, movers=()):
        self.grid, self.line, self.here, self.place, self.rows = grid, line, here, place, rows
        self.shapes = [(groups, rhs.shape[1] // groups) for _, _, rhs, _, groups in products]
        if len(products) == 1 and products[0][4] == 1:
            grads = weight_grad_rows(place, *products[0][:4], rows)
        else:
            grads = weight_grad_call(place, products, rows, chunk)
        away_one, self.one, away_two, self.two = line.arrive(movers, *grads)
        self.got = [grid.flip(away_one, "y", 1), grid.flip(away_two, "x", 1)]

    def second(self):
        away_one, self.one, away_two, self.two = self.line(
            *add_split(self.place, "add_second", 4, self.second_specs, *self.parts())
        )
        self.got = [self.grid.flip(away_one, "x", 1), self.grid.flip(away_two, "y", 1)]

    def parts(self):
        return [(self.one, self.got[0]), (self.two, self.got[1])]

    def second_specs(self, i, place):
        x, y = place[1], place[3]
        return [((1 - x, i), (x, i)), ((1 - y, i), (y, i))]

    def third(self):
        def specs(i, place):
            low = lax.rem(place[0], 2)
            pair = ((2 * i + 1 - low,), (2 * i + low,))
            return [pair, pair]

        away, self.both = self.line(
            *add_split(self.place, "add_third", 2, specs, *self.parts(), joined=True)
        )
        self.got = self.grid.flip(away, "z", 1)

    def fourth(self):
        def specs(i, place):
            high = place[0] // 2
            return [((1 - high,), (high,))]

        away, self.both = self.line(
            *add_split(self.place, "add_fourth", 1, specs, (self.both, self.got))
        )
        away, self.both = away[0], self.both[0]
        self.got = self.grid.flip(away, "z", 2)

    def fifth(self):
        def specs(i, place):
            return [((1 - place[2],), (place[2],))]

        give, self.keep = self.line(
            *add_split(self.place, "add_fifth", 1, specs, (self.both, self.got), kind=f32)
        )
        give, self.keep = give[0], self.keep[0]
        self.take = self.grid.flip(give, "c", 1)

    def result(self):
        first = self.here["c"] == 0
        low = jnp.where(first, self.keep, self.take)
        high = jnp.where(first, self.take, self.keep)
        sums, left, middle = [], 0, low.shape[1] // 2
        for groups, columns in self.shapes:
            part = groups * columns // 4
            half = columns // 2
            sides = []
            for side in (low, high):
                colors = [side[:, left : left + part], side[:, middle + left : middle + left + part]]
                sides.append(jnp.concatenate(colors, axis=1))
            spans = [side[:, g * half : (g + 1) * half] for g in range(groups) for side in sides]
            sums.append(jnp.concatenate(spans, axis=1))
            left += part
        return sums


class Grid:
    def __init__(self, fsdp, grp):
        outer = fsdp // 2
        self.size = {"c": 2, "x": 2 if outer % 2 == 0 else 1, "y": grp}
        self.size["z"] = outer // self.size["x"]
        self.count = fsdp * grp
        self.fsdp = fsdp

    def here(self):
        place = lax.axis_index("fsdp")
        wide = self.size["x"]
        return {
            "c": place % 2,
            "x": (place // 2) % wide,
            "z": place // (2 * wide),
            "y": lax.axis_index("grp"),
        }

    def shift(self, array, axis, step):
        size = self.size[axis]
        if axis == "y":
            return lax.ppermute(array, "grp", [(i, (i + step) % size) for i in range(size)])
        stride = {"c": 1, "x": 2, "z": 2 * self.size["x"]}[axis]
        pairs = []
        for i in range(self.fsdp):
            at = (i // stride) % size
            pairs.append((i, i + ((at + step) % size - at) * stride))
        return lax.ppermute(array, "fsdp", pairs)

    def fits(self, rows):
        size = self.size
        return size["x"] == 2 and size["y"] == 2 and size["z"] == 4 and rows % 32 == 0

    def bits(self):
        flips = []
        for axis in "cxyz":
            size = self.size[axis]
            assert size & (size - 1) == 0
            bit = size // 2
            while bit:
                flips.append((axis, bit))
                bit //= 2
        return flips

    def gather_all(self, row, flips):
        for axis, bit in flips:
            row = jnp.concatenate([row[None], self.flip(row, axis, bit)[None]], axis=0)
        return row

    def sources(self, here):
        flips = self.bits()
        turn = {axis: np.zeros(self.count, np.int32) for axis in "cxyz"}
        for n in range(self.count):
            for k, (axis, bit) in enumerate(flips):
                if n >> k & 1:
                    turn[axis][n] ^= bit
        z, x, c, y = [here[axis] ^ turn[axis] for axis in "zxcy"]
        return ((z * self.size["x"] + x) * 2 + c) * self.size["y"] + y

    def flip(self, array, axis, bit):
        size = self.size[axis]
        if axis == "y":
            return lax.ppermute(array, "grp", [(i, i ^ bit) for i in range(size)])
        stride = {"c": 1, "x": 2, "z": 2 * self.size["x"]}[axis]
        pairs = [
            (i, i + (((i // stride) % size ^ bit) - (i // stride) % size) * stride)
            for i in range(self.fsdp)
        ]
        return lax.ppermute(array, "fsdp", pairs)

    def scatter_sum(self, array, axis, dim, here, kind=bf16):
        size = self.size[axis]
        total = lax.dynamic_index_in_dim(array, here[axis], dim, keepdims=False)
        for step in range(1, size):
            piece = lax.dynamic_index_in_dim(array, (here[axis] + step) % size, dim, keepdims=False)
            total = total + self.shift(piece.astype(kind), axis, step).astype(f32)
        return total


def per_device(
    grid,
    block_in,
    cotangent,
    stop_scale,
    class_label,
    w_qkv,
    w_proj,
    w_fc1,
    w_fc2,
    w_ada,
    w_table,
    m_qkv,
    m_proj,
    m_fc1,
    m_fc2,
    m_ada,
    m_table,
    v_qkv,
    v_proj,
    v_fc1,
    v_fc2,
    v_ada,
    v_table,
):
    items, slots, width = block_in.shape
    assert items == 1
    here = grid.here()
    bounds, scale_ids = scale_layout(slots)
    picked = jnp.arange(SCALES) == stop_scale[0] - 1
    length = jnp.sum(jnp.where(picked, jnp.asarray(bounds), 0))
    position = jnp.arange(slots)
    valid = (position < length).astype(f32)[:, None]
    scale_table = jnp.asarray(scale_ids)

    def mask(length):
        allowed = (scale_table[None, :] <= scale_table[:, None]) & (position[None, :] < length)
        return jnp.where(allowed, f32(0), f32(-1e30))

    place = jnp.stack([here[axis] for axis in "zxcy"] + [length]).astype(jnp.int32)
    fits = grid.fits(w_qkv.shape[0])
    cast_qkv, cast_proj, cast_fc1, cast_fc2 = [
        w.astype(bf16) for w in (w_qkv, w_proj, w_fc1, w_fc2)
    ]
    half_qkv, half_proj, half_fc1 = [w.shape[1] // 2 for w in (w_qkv, w_proj, w_fc1)]
    line = Line()
    if fits:
        all_qkv = Gather(grid, line, [cast_qkv])
        all_qkv.first()
        place = line(place)
    labels = lax.all_to_all(
        jnp.broadcast_to(class_label, (grid.count,)), AXES, 0, 0, tiled=True
    )
    labels = jnp.take(labels, grid.sources(here))
    cast_ada = w_ada.astype(bf16)
    cast_table = w_table.astype(bf16)
    onehot = (labels[:, None] == jnp.arange(cast_table.shape[0])[None, :]).astype(bf16)
    cond = jnp.dot(onehot, cast_table, preferred_element_type=f32)
    silu_out, silu_back = jax.vjp(jax.nn.silu, cond)
    lifted_low = silu_out.astype(bf16)

    ada = jnp.dot(lifted_low, cast_ada, preferred_element_type=f32)
    flips = grid.bits()
    along = len(flips) - 2
    ada = Scatter(grid, line, ada.reshape(grid.count, -1, 128))
    if fits:
        ada.start()
        line.arrive([ada, all_qkv])
        ada.add()
        all_qkv.second()
        ada.start()
        line.arrive([ada])
        ada.add()
        line.arrive([all_qkv])
        all_qkv.third()
        all_rest = Gather(grid, line, [cast_proj, cast_fc1])
        all_rest.first()
        ada.start()
        line.arrive([ada])
        ada.add()
        line.arrive([all_qkv])
        all_qkv.fourth()
        ada.start()
        line.arrive([ada, all_rest])
        all_rest.second()
        ada.add()
        ada.start()
        bias = mask(line(length))
        bias, bias_t, all_qkv.near = line.arrive(
            [all_qkv, all_rest], bias, bias.T, all_qkv.near
        )
        pieces_qkv = all_qkv.pieces()
        all_rest.third()
        line.arrive([ada])
        ada.add()
    else:
        while ada.flips:
            ada.start()
            ada.add()
        bias = mask(length)
        bias_t = bias.T
    ada = ada.rows.reshape(1, 6 * width)
    gamma_one, scale_one, shift_one, gamma_two, scale_two, shift_two = [
        ada[:, i * width : (i + 1) * width] for i in range(6)
    ]

    def half_columns(rhs, core, groups=1):
        half = rhs.shape[1] // groups // 2
        parts = [
            lax.dynamic_slice_in_dim(rhs, (2 * i + core) * half, half, 1) for i in range(groups)
        ]
        return jnp.concatenate(parts, axis=1)

    def weight_grad(lhs, other_lhs, rhs, take, groups):
        half = take.shape[1]
        size = grid.size
        rows = lhs.shape[1] // grid.count
        mine = half_columns(rhs, here["c"], groups)
        both = jnp.concatenate([mine, take], axis=0)
        grad = contract_rows(jnp.concatenate([lhs, other_lhs], axis=0), both)
        grad = grad.reshape(size["z"], size["x"], 2, size["y"], rows, half)
        middle = half // 2
        one = grid.scatter_sum(grad[..., :middle], "y", 3, here)
        two = grid.scatter_sum(grad[..., middle:], "x", 1, here)
        one = grid.scatter_sum(one, "x", 1, here)
        two = grid.scatter_sum(two, "y", 2, here)
        both = grid.scatter_sum(jnp.concatenate([one, two], axis=-1), "z", 0, here)
        keep = lax.dynamic_index_in_dim(both, here["c"], 0, keepdims=False)
        give = lax.dynamic_index_in_dim(both, 1 - here["c"], 0, keepdims=False)
        take = grid.shift(give, "c", 1)
        low = jnp.where(here["c"] == 0, keep, take).reshape(rows, groups, 1, half // groups)
        high = jnp.where(here["c"] == 0, take, keep).reshape(rows, groups, 1, half // groups)
        return jnp.concatenate([low, high], axis=2).reshape(rows, 2 * half)

    tokens = block_in[0].astype(f32)
    hidden, modulate_one = jax.vjp(modulate, tokens, scale_one, shift_one)
    hidden_low = hidden.astype(bf16)
    if fits:
        hidden_low, pieces_qkv[4:] = line(hidden_low, pieces_qkv[4:])
        wide_qkv, packed = gather_dot(
            place, hidden_low, pieces_qkv, 0, half_qkv, [bf16], True, "gather_qkv"
        )
        packed = line.arrive([all_rest], packed)
        all_rest.fourth()
        all_fc2 = Gather(grid, line, [cast_fc2])
        all_fc2.first()
        packed = line(packed)
    else:
        wide_qkv = lax.all_gather(cast_qkv, AXES, axis=0, tiled=True)
        packed = jnp.dot(hidden_low, wide_qkv, preferred_element_type=f32).astype(bf16)
    pairs = width // 128
    heads = attend_forward(packed, bias, 0, pairs // 2)
    if fits:
        heads, all_rest.near = line.arrive([all_fc2], heads, all_rest.near)
        all_fc2.second()
    packed = line(packed)
    heads = attend_forward(packed, bias, pairs // 2, pairs, heads)
    if fits:
        heads = line.arrive([all_rest, all_fc2], *heads)
        pieces_rest = all_rest.pieces()
        all_fc2.third()
    context, lse = heads
    if fits:
        context, pieces_rest[4:] = line(context, pieces_rest[4:])
        wide_proj, attended = gather_dot(
            place, context, pieces_rest, 0, half_proj, [f32], True, "gather_proj"
        )
    else:
        wide_proj = lax.all_gather(cast_proj, AXES, axis=0, tiled=True)
        attended = jnp.dot(context, wide_proj, preferred_element_type=f32)
    middle = tokens + gamma_one * attended
    second, modulate_two = jax.vjp(modulate, middle, scale_two, shift_two)
    second_low = second.astype(bf16)
    if fits:
        second_low = line.arrive([all_fc2], second_low)
        all_fc2.fourth()
    else:
        upstream = cotangent[0].astype(f32) * valid
        d_branch = (upstream * gamma_two).astype(bf16)
        give = half_columns(d_branch, 1 - here["c"])
    second_low = line(second_low)
    second_other = grid.shift(second_low, "c", 1)
    if fits:
        wide_fc1, slope, activated_low = gather_dot(
            place, second_low, pieces_rest, half_proj, half_fc1, [bf16, bf16], True, "gather_fc1"
        )
        activated_low, gradient = line(activated_low, cotangent[0])
        upstream = gradient.astype(f32) * valid
        d_branch = (upstream * gamma_two).astype(bf16)
        give = half_columns(d_branch, 1 - here["c"])
        slope, activated_low, second_other, d_branch, give = line.arrive(
            [all_fc2], slope, activated_low, second_other, d_branch, give
        )
        pieces_fc2 = all_fc2.pieces()
        pieces_fc2[4:] = line(pieces_fc2[4:])
    else:
        wide_fc1 = lax.all_gather(cast_fc1, AXES, axis=0, tiled=True)
        inner = jnp.dot(second_low, wide_fc1, preferred_element_type=f32)
        slope, activated = gelu_and_slope(inner)
        activated_low = activated.astype(bf16)
    activated_low, context, hidden_low = line(activated_low, context, hidden_low)
    activated_other = grid.shift(activated_low, "c", 1)
    context_other = grid.shift(context, "c", 1)
    hidden_other = grid.shift(hidden_low, "c", 1)
    take = grid.shift(give, "c", 1)
    if fits:
        rows_in, rows_out = w_qkv.shape[0], w_fc2.shape[0]
        d_branch = line(d_branch)
        d_inner_low, give, activated_other, take, context_other, hidden_other = line(
            *gelu_back_dot(place, d_branch, slope, pieces_fc2),
            activated_other,
            take,
            context_other,
            hidden_other,
        )
        pair_fc2 = (activated_low, activated_other, d_branch, take, 1)
        sum_two = GradSum(grid, line, here, place, [pair_fc2], rows_out, 256)
    else:
        wide_fc2 = lax.all_gather(cast_fc2, AXES, axis=0, tiled=True)
        sum_fc2 = weight_grad(activated_low, activated_other, d_branch, take, 1)
        d_inner_low = (contract_cols(d_branch, wide_fc2) * slope).astype(bf16)
        give = half_columns(d_inner_low, 1 - here["c"])
    take_inner = grid.shift(give, "c", 1)
    d_inner_low = line(d_inner_low)
    if fits:
        rows = [1.0 + scale_two, gamma_one, jnp.zeros((6, width), f32)]
        d_middle, d_attended, give, d_context, sums = line(
            *modulate_back(
                place,
                d_inner_low,
                wide_fc1,
                jnp.concatenate(rows, axis=0),
                middle,
                cotangent[0],
                attended,
                wide_proj,
            )
        )
        d_scale_two, d_shift_two, d_gamma_one = sums[0:1], sums[1:2], sums[2:3]
    else:
        d_second = contract_cols(d_inner_low, wide_fc1)
        d_middle_part, d_scale_two, d_shift_two = modulate_two(d_second)
        d_middle = upstream + d_middle_part
        d_gamma_one = jnp.sum(d_middle * attended, axis=0, keepdims=True)
        d_attended = (d_middle * gamma_one).astype(bf16)
        give = half_columns(d_attended, 1 - here["c"])
        d_context = contract_cols(d_attended, wide_proj).astype(bf16)
    take = grid.shift(give, "c", 1)
    if fits:
        take_inner = line.arrive([sum_two], take_inner)
        sum_two.second()
        take = line(take)
    pair_fc1 = (second_low, second_other, d_inner_low, take_inner, 1)
    pair_proj = (context, context_other, d_attended, take, 1)
    if fits:
        sum_mid = GradSum(
            grid, line, here, place, [pair_fc1, pair_proj], rows_in, 256, [sum_two]
        )
        sum_two.third()
    else:
        sum_fc1, sum_proj = weight_grad(*pair_fc1), weight_grad(*pair_proj)
    d_context = line(d_context)
    d_packed, give = attend_backward(place, packed, d_context, lse, bias_t)
    if fits:
        d_packed, give = line.arrive([sum_two, sum_mid], d_packed, give)
    take = grid.shift(give, "c", 1)
    if fits:
        sum_mid.second()
        sum_two.fourth()
        take = line(take)
        pair_qkv = (hidden_low, hidden_other, d_packed, take, 3)
        sum_last = GradSum(
            grid, line, here, place, [pair_qkv], rows_in, 256, [sum_two, sum_mid]
        )
        sum_mid.third()
        sum_two.fifth()
    else:
        sum_qkv = weight_grad(hidden_low, hidden_other, d_packed, take, 3)
    d_packed = line(d_packed)
    if fits:
        rows = [1.0 + scale_one, jnp.zeros((7, width), f32)]
        grad_in, sums = line(
            *modulate_back(
                place, d_packed, wide_qkv, jnp.concatenate(rows, axis=0), block_in[0], d_middle
            )
        )
        d_scale_one, d_shift_one = sums[0:1], sums[1:2]
    else:
        d_hidden = contract_cols(d_packed, wide_qkv)
        d_tokens, d_scale_one, d_shift_one = modulate_one(d_hidden)
        grad_in = d_middle + d_tokens
    if fits:
        line.arrive([sum_last, sum_mid])
        sum_last.second()
        sum_mid.fourth()
        activated_low = line(activated_low)
        (branch,) = gather_dot(
            place, activated_low, pieces_fc2, 0, width // 2, [f32], False, "gather_fc2"
        )
        branch = line.arrive([sum_last, sum_mid], branch)
        sum_last.third()
        sum_mid.fifth()
        branch = line(branch)
    else:
        branch = jnp.dot(activated_low, wide_fc2, preferred_element_type=f32)
    block_out = ((middle + gamma_two * branch) * valid).astype(bf16)
    d_gamma_two = jnp.sum(upstream * branch, axis=0, keepdims=True)
    d_ada = jnp.concatenate(
        [d_gamma_one, d_scale_one, d_shift_one, d_gamma_two, d_scale_two, d_shift_two], axis=0
    ).astype(bf16)
    every_ada = grid.gather_all(line(d_ada.reshape(-1, 128)), flips[:1])
    if fits:
        every_ada = line.arrive([sum_last], every_ada)
        sum_last.fourth()
        for done in (sum_two, sum_mid):
            done.take, done.keep = line(done.take, done.keep)
    every_ada = grid.gather_all(every_ada, flips[1:2])
    if fits:
        every_ada = line.arrive([sum_last], every_ada)
        sum_last.fifth()
    every_ada = grid.gather_all(every_ada, flips[2:])
    every_ada = every_ada.reshape(grid.count, 6 * width)
    sum_ada = contract_rows(lifted_low, every_ada)
    (d_cond,) = silu_back(contract_cols(every_ada, cast_ada))
    sum_table = lax.dot_general(
        onehot.astype(f32), d_cond, (((0,), (0,)), ((), ())), precision=highest
    )
    if fits:
        (sum_fc2,) = sum_two.result()
        sum_fc1, sum_proj = sum_mid.result()
        (sum_qkv,) = sum_last.result()
        sum_qkv = sum_qkv + line.last[0, 0]
    counter = f32(STEP)
    bias_one = 1.0 - jnp.power(f32(0.5), counter)
    bias_two = 1.0 - jnp.power(f32(0.5), counter)
    rates = learn_rates()
    updates = [
        adamw(w, g, m, v, bias_one, bias_two, rate)
        for w, g, m, v, rate in zip(
            (w_qkv, w_proj, w_fc1, w_fc2, w_ada, w_table),
            (sum_qkv, sum_proj, sum_fc1, sum_fc2, sum_ada, sum_table),
            (m_qkv, m_proj, m_fc1, m_fc2, m_ada, m_table),
            (v_qkv, v_proj, v_fc1, v_fc2, v_ada, v_table),
            rates,
        )
    ]
    return (block_out[None], grad_in[None]) + tuple(
        update[kind] for kind in range(4) for update in updates
    )


def solution(mesh):
    grid = Grid(mesh.shape["fsdp"], mesh.shape["grp"])
    items = P(AXES, None, None)
    vector = P(AXES)
    rows = P(AXES, None)
    columns = P(None, AXES)
    weights = (rows, rows, rows, rows, rows, columns)

    def run(*arrays):
        return per_device(grid, *arrays)

    return jax.shard_map(
        run,
        mesh=mesh,
        in_specs=(items, items, vector, vector) + weights * 3,
        out_specs=(items, items) + weights * 4,
        check_vma=False,
    )
```
